32 devices in a mesh: grp: 4 (over y, x), sub: 8 (over z, core).
Axes of the slice: x: 2, y: 2, z: 4, core: 2. Of those that a mesh axis runs over, the one named last changes fastest.
Arguments:
- residual: bfloat16 [4, 8, 1024, 2048], P('grp', 'sub'), may hold values from -6 to 6
- inverse_blocks: bfloat16 [4, 8, 1024, 1536], P('grp', 'sub'), may hold values from -0.15625 to 0.15625
- operator_tiles: bfloat16 [4, 8, 8, 8, 128, 128], P('grp', 'sub'), may hold values from -0.1875 to 0.1875
- column_blocks: int32 [4, 8, 8, 8], P('grp', 'sub'), may hold values from 0 to 11
- coarse_basis: bfloat16 [4, 8, 1024, 200], P('grp', 'sub'), may hold values from -6 to 6
- face_rows: int32 [4, 8, 4, 128], P('grp', 'sub'), may hold values from 0 to 1023
Outputs:
- local_fix: bfloat16 [4, 8, 1024, 2048], P('grp', 'sub')
- galerkin: float32 [200, 200], replicated
- coarse_rhs: float32 [200, 2048], P(None, 'sub')
The draws below stay inside these ranges and needn't reach their ends.
All inputs are finite; a program needn't handle non-finite values.
Results may differ from the reference program's by a relative error of at most 0.0029.
Values may be sent and summed in bfloat16 or wider, within the bound.
A program may use at most 128 MiB of HBM per device.

```python
import math
import jax
import jax.numpy as jnp
from jax import lax

ROWS = 1024
OV = 128
K = 2048
C = 200
TILE = 128
NNZB = 8
EXT = 1536
RB = 8
EB = 12
N_GRP = 4
N_SUB = 8


def with_ends(result, stream_key, least, largest):
    shape = result.shape
    spot = [jax.random.randint(jax.random.fold_in(stream_key, axis), (), 0, shape[axis]) for axis in range(len(shape))]
    result = result.at[tuple(spot)].set(least)
    longest = shape.index(max(shape))
    spot[longest] = (spot[longest] + 1) % shape[longest]
    return result.at[tuple(spot)].set(largest)


def strengthened(values, key, source, target, blocks, factor):
    def block_of(dim):
        return (jnp.arange(values.shape[dim]) // (values.shape[dim] // blocks)).reshape((-1,) + (1,) * (values.ndim - 1 - dim))

    first = jax.random.permutation(key, blocks)[block_of(target)]
    other_side = (block_of(target) + blocks // 2) % blocks
    return jnp.where((block_of(source) == first) | (block_of(source) == other_side), factor * values, values)


def steps_of(key, extent, cuts, smallest, high):
    factor_of = 1.0
    for dim, blocks in cuts:
        draws = jax.random.uniform(jax.random.fold_in(jax.random.fold_in(key, 6), dim), (blocks,), jnp.float32, smallest / len(cuts), high / len(cuts))
        factor_of = factor_of * jnp.repeat(jnp.exp(draws), extent[dim] // blocks).reshape((-1,) + (1,) * (len(extent) - 1 - dim))
    return factor_of


def normal_values(stream_key, shape, scale, bound, cuts=(), held_as=jnp.bfloat16):
    entries = jax.random.normal(stream_key, shape, jnp.float32) * scale
    if len(cuts) > 0:
        entries = steps_of(stream_key, shape, cuts, -0.22, 0.18) * entries
    return jnp.clip(entries, min=-bound, max=bound).astype(held_as)


def heavy_noise(rng, extent, scale, bound, cuts, heavy, kind=jnp.bfloat16):
    result = scale * jax.random.normal(rng, extent, jnp.float32)
    if cuts:
        result = result * steps_of(rng, extent, cuts, -0.22, 0.18)
    return jnp.clip(strengthened(result, jax.random.fold_in(rng, 3), *heavy), -bound, bound).astype(kind)


def setup_inputs(seed: int = 0) -> dict:
    arg_keys = jax.random.split(jax.random.key(seed), 7)
    residual = heavy_noise(arg_keys[0], (N_GRP, N_SUB, ROWS, K), 1.0, 6.0, ((0, 4), (1, 8)), (1, 3, 8, 2.0))
    inverse_blocks = normal_values(arg_keys[1], (N_GRP, N_SUB, ROWS, EXT), EXT ** -0.5, 0.15625, ((0, 4), (1, 8)))
    operator_tiles = normal_values(arg_keys[2], (N_GRP, N_SUB, RB, NNZB, TILE, TILE), (NNZB * TILE) ** -0.5, 0.1875, ((0, 4), (1, 8)))
    column_blocks = with_ends(jax.random.randint(arg_keys[3], (N_GRP, N_SUB, RB, NNZB), 0, EB), jax.random.fold_in(arg_keys[3], 1), 0, EB - 1).astype(jnp.int32)
    coarse_basis = normal_values(arg_keys[4], (N_GRP, N_SUB, ROWS, C), 1.0, 6.0, ((0, 4), (1, 8)))
    face_rows = with_ends(jax.random.randint(arg_keys[5], (N_GRP, N_SUB, 4, OV), 0, ROWS), jax.random.fold_in(arg_keys[5], 1), 0, ROWS - 1).astype(jnp.int32)
    return dict(residual=residual, inverse_blocks=inverse_blocks, operator_tiles=operator_tiles, column_blocks=column_blocks, coarse_basis=coarse_basis, face_rows=face_rows)


def incoming(stacked, face_rows, grp_at, sub_at, face_index, present):
    grp_safe = jnp.clip(grp_at, 0, N_GRP - 1)
    sub_safe = jnp.clip(sub_at, 0, N_SUB - 1)
    picked_rows = face_rows[grp_safe, sub_safe, face_index]
    rows_sent = jnp.take(stacked[grp_safe, sub_safe], picked_rows, axis=0)
    return jnp.where(present, rows_sent, jnp.zeros_like(rows_sent))

def extend(stacked, face_rows, grp_at, sub_at):
    pieces = [stacked[grp_at, sub_at], incoming(stacked, face_rows, grp_at - 1, sub_at, 0, grp_at > 0), incoming(stacked, face_rows, grp_at + 1, sub_at, 1, grp_at < N_GRP - 1), incoming(stacked, face_rows, grp_at, sub_at - 1, 2, sub_at > 0), incoming(stacked, face_rows, grp_at, sub_at + 1, 3, sub_at < N_SUB - 1)]
    return jnp.concatenate(pieces, axis=0)

def reference(residual, inverse_blocks, operator_tiles, column_blocks, coarse_basis, face_rows):

    def visit_one(totals, device_at):
        galerkin_sum, rhs_sum = totals
        grp_at = device_at // N_SUB
        sub_at = device_at % N_SUB
        resid_ext = extend(residual, face_rows, grp_at, sub_at)
        basis_ext = extend(coarse_basis, face_rows, grp_at, sub_at)
        correction = jnp.dot(inverse_blocks[grp_at, sub_at], resid_ext, preferred_element_type=jnp.float32).astype(jnp.bfloat16)
        blocks = basis_ext.reshape(EXT // TILE, TILE, C)
        picked = jnp.take(blocks, column_blocks[grp_at, sub_at], axis=0)
        applied = jnp.einsum('bjtu,bjuc->btc', operator_tiles[grp_at, sub_at].astype(jnp.float32), picked.astype(jnp.float32), precision=lax.Precision.HIGHEST)
        applied = applied.reshape(ROWS, C).astype(jnp.bfloat16)
        own_basis = coarse_basis[grp_at, sub_at]
        galerkin_sum = galerkin_sum + jnp.dot(own_basis.T, applied, preferred_element_type=jnp.float32)
        rhs_sum = rhs_sum + jnp.dot(own_basis.T, residual[grp_at, sub_at], preferred_element_type=jnp.float32)
        return ((galerkin_sum, rhs_sum), correction)
    indices = jnp.arange(N_GRP * N_SUB, dtype=jnp.int32)
    start = (jnp.zeros((C, C), jnp.float32), jnp.zeros((C, K), jnp.float32))
    (galerkin_sum, rhs_sum), corrections = lax.scan(visit_one, start, indices)
    scaling = 1.0 / math.sqrt(ROWS * N_GRP * N_SUB)
    return (corrections.reshape(N_GRP, N_SUB, ROWS, K), galerkin_sum * scaling, rhs_sum * scaling)
```

```python
import functools
import math

import jax
import jax.numpy as jnp
from jax import lax
from jax.experimental import pallas as pl
from jax.experimental.pallas import tpu as pltpu
from jax.sharding import PartitionSpec as P

MESH = pl.DeviceIdType.MESH
F32 = jnp.float32
BF16 = jnp.bfloat16


def wide_dot(a, b):
    return jnp.dot(a, b, preferred_element_type=F32)


def dot_rows(a, b):
    return lax.dot_general(a, b, (((1,), (1,)), ((), ())), preferred_element_type=F32)


def ring_free_kernel(
    n_grp, n_sub, width, scaling,
    col_ref, face_ref, basis_ref, resid_hbm, inv_hbm, tiles_hbm,
    fix_ref, gal_ref, rhs_ref,
    resid, inv, tiles, pick, ext_send, ext, face_send, face_recv, relay, total,
    keep, pair_send, pair_recv, rhs_send, rhs_recv, sum_send, sum_recv, sum_last, sum_full,
    applied, gal, gal_pair, gal_both, gal_recv, gal_sum, gal_sum_recv, gal_last, gal_full,
    in_sem, resid_sem, ext_ss, ext_rs, face_ss, face_rs, relay_ss, relay_rs,
    pair_ss, pair_rs, gpair_ss, gpair_rs, rhs_ss, rhs_rs,
    sum_ss, sum_rs, last_ss, last_rs, gal_ss, gal_rs, gsum_ss, gsum_rs, glast_ss, glast_rs,
):
    g = lax.axis_index("grp")
    s = lax.axis_index("sub")
    chip, core = s // 2, lax.rem(s, 2)
    partner = s + 1 - 2 * core
    chips = n_sub // 2
    chunks, rows, _ = resid.shape
    coarse = basis_ref.shape[0]
    row_blocks, per_row, tile = tiles.shape[:3]
    own_blocks = rows // tile
    ov = face_ref.shape[1]
    part = chunks * width // n_sub
    per_chunk = width // part
    gal_rows = gal_recv.shape[1]
    sum_rows = sum_recv.shape[1]
    relayed = n_grp == 4

    def load_resid(c):
        cols = pl.ds(pl.multiple_of(c * width, width), width)
        return pltpu.make_async_copy(resid_hbm.at[:, cols], resid.at[c], resid_sem.at[c])

    load_tiles = pltpu.make_async_copy(tiles_hbm, tiles, in_sem.at[0])
    load_inv = pltpu.make_async_copy(inv_hbm, inv, in_sem.at[1])

    @pl.loop(0, chunks)
    def _(c):
        load_resid(c).start()

    load_tiles.start()
    load_inv.start()

    barrier = pltpu.get_barrier_semaphore()

    @pl.loop(1, n_sub)
    def _(i):
        pl.semaphore_signal(barrier, inc=1, device_id=(g, lax.rem(s + i, n_sub)), device_id_type=MESH)

    @pl.loop(1, n_grp)
    def _(i):
        pl.semaphore_signal(barrier, inc=1, device_id=(lax.rem(g + i, n_grp), s), device_id_type=MESH)

    targets = ((g + 1, s), (g - 1, s), (g, s + 1), (g, s - 1))
    sends = (g < n_grp - 1, g > 0, s < n_sub - 1, s > 0)
    arrives = (g > 0, g < n_grp - 1, s > 0, s < n_sub - 1)

    def remote(src, dst, send_sem, recv_sem, device):
        return pltpu.make_async_remote_copy(
            src_ref=src, dst_ref=dst, send_sem=send_sem, recv_sem=recv_sem,
            device_id=device, device_id_type=MESH,
        )

    def ext_copy(f):
        return remote(ext_send.at[f], ext.at[own_blocks + f], ext_ss.at[f], ext_rs.at[f], targets[f])

    def face_copy(c, f, far=False):
        span = pl.ds(f * ov, ov)
        if far:
            way = (n_grp - 1) * (lax.rem(c + f, 2))
            return remote(face_send.at[c, span], relay.at[c], face_ss.at[c, f], relay_rs.at[c], (way, s))
        return remote(face_send.at[c, span], face_recv.at[c, span], face_ss.at[c, f], face_rs.at[c, f], targets[f])

    def forward(c, f):
        span = pl.ds(f * ov, ov)
        return remote(relay.at[c], face_recv.at[c, span], relay_ss.at[c], face_rs.at[c, f], (2 - f, s))

    def far_face(f):
        return (g == 1 + f) if relayed and f < 2 else None

    def face_start(c, f):
        far = far_face(f)
        if far is None:
            @pl.when(sends[f])
            def _():
                face_copy(c, f).start()
        else:
            @pl.when(far)
            def _():
                face_copy(c, f, True).start()

            @pl.when(jnp.logical_and(sends[f], jnp.logical_not(far)))
            def _():
                face_copy(c, f).start()

    def when_relaying(c, do):
        if relayed:
            turn = lax.rem(c + jnp.where(g == 3, 1, 0), 2)
            for f in range(2):
                @pl.when(jnp.logical_and(jnp.logical_or(g == 0, g == 3), turn == f))
                def _():
                    do(forward(c, f))

    lanes = lax.broadcasted_iota(jnp.int32, (ov, tile), 1)
    for f in range(4):
        wanted = jnp.broadcast_to(face_ref[f:f + 1, :].astype(F32), (ov, ov)).T.astype(jnp.int32)
        for b in range(own_blocks):
            hit = wanted == lanes + b * tile
            pick[f * ov:(f + 1) * ov, b * tile:(b + 1) * tile] = jnp.where(hit, 1.0, 0.0).astype(BF16)
    basis = basis_ref[...]
    for f in range(4):
        ext_send[f] = dot_rows(basis, pick[f * ov:(f + 1) * ov, :]).astype(BF16)
    for b in range(own_blocks):
        ext[b] = basis_ref[:, b * tile:(b + 1) * tile]

    for f in range(4):
        @pl.when(jnp.logical_not(arrives[f]))
        def _():
            ext[own_blocks + f] = jnp.zeros((coarse, tile), BF16)
            face_recv[:, f * ov:(f + 1) * ov, :] = jnp.zeros((chunks, ov, width), BF16)

    pl.semaphore_wait(barrier, n_sub - 1 + n_grp - 1)
    for f in range(4):
        @pl.when(sends[f])
        def _():
            ext_copy(f).start()

    def pair_copy(i):
        return remote(pair_send.at[i], pair_recv.at[i], pair_ss.at[i], pair_rs.at[i], (g, partner))

    @pl.loop(0, chunks)
    def _(c):
        load_resid(c).wait()
        face_send[c] = wide_dot(pick[...], resid[c]).astype(BF16)
        for f in range(4):
            face_start(c, f)
        term = wide_dot(basis_ref[...], resid[c])
        for q in range(per_chunk):
            to = c * per_chunk + q
            piece = term[:, q * part:(q + 1) * part]

            @pl.when(lax.rem(to, 2) == core)
            def _():
                keep[to // 2] = piece

            @pl.when(lax.rem(to, 2) != core)
            def _():
                pair_send[to // 2] = piece
                pair_copy(to // 2).start()

    load_tiles.wait()
    for f in range(4):
        @pl.when(arrives[f])
        def _():
            ext_copy(f).wait_recv()

    @pl.loop(0, row_blocks)
    def _(b):
        row = jnp.concatenate([tiles[b, j] for j in range(per_row)], axis=1)
        picked = jnp.concatenate([ext[col_ref[b, j]] for j in range(per_row)], axis=1)
        applied[pl.ds(pl.multiple_of(b * tile, tile), tile), :] = dot_rows(row, picked).astype(BF16)

    gal[coarse:, :] = jnp.zeros((gal.shape[0] - coarse, coarse), F32)
    gal[:coarse, :] = wide_dot(basis_ref[...], applied[...])

    gal_swap = remote(gal, gal_pair, gpair_ss.at[0], gpair_rs.at[0], (g, partner))
    gal_swap.start()
    def rhs_copy(i):
        to = lax.rem(chip + i, chips)
        return remote(rhs_send.at[to], rhs_recv.at[chip], rhs_ss.at[to], rhs_rs.at[chip], (g, to * 2 + core))

    def rhs_from(i):
        frm = lax.rem(chip + i, chips)
        return remote(rhs_send.at[frm], rhs_recv.at[frm], rhs_ss.at[frm], rhs_rs.at[frm], (g, frm * 2 + core))

    @pl.loop(1, chips)
    def _(i):
        to = lax.rem(chip + i, chips)
        pair_copy(to).wait_recv()
        rhs_send[to] = (keep[to] + pair_recv[to]).astype(BF16)
        rhs_copy(i).start()

    pair_copy(chip).wait_recv()
    sum_send[:coarse, :] = keep[chip] + pair_recv[chip]
    if sum_send.shape[0] > coarse:
        sum_send[coarse:, :] = jnp.zeros((sum_send.shape[0] - coarse, part), F32)
    load_inv.wait()

    @pl.loop(0, chunks // 2)
    def _(c):
        total[c] = wide_dot(inv[:, :rows], resid[c])

    def gal_piece(i):
        return pl.ds(pl.multiple_of(i * gal_rows, 8), gal_rows)

    def gal_copy(i):
        to = lax.rem(chip + i, chips)
        piece = gal_both.at[gal_piece(to * 2 + core)]
        return remote(piece, gal_recv.at[chip], gal_ss.at[to], gal_rs.at[chip], (g, to * 2 + core))

    def gal_from(i):
        frm = lax.rem(chip + i, chips)
        piece = gal_both.at[gal_piece(frm * 2 + core)]
        return remote(piece, gal_recv.at[frm], gal_ss.at[frm], gal_rs.at[frm], (g, frm * 2 + core))

    gal_swap.wait_recv()
    gal_both[...] = gal[...] + gal_pair[...]

    @pl.loop(1, chips)
    def _(i):
        gal_copy(i).start()

    gal_sum[...] = gal_both[gal_piece(s), :]

    @pl.loop(chunks // 2, chunks)
    def _(c):
        total[c] = wide_dot(inv[:, :rows], resid[c])

    def finish(c):
        def pass_on(copy):
            remote(relay.at[c], relay.at[c], relay_ss.at[c], relay_rs.at[c], (1, s)).wait_recv()
            copy.start()

        when_relaying(c, pass_on)
        for f in range(4):
            @pl.when(arrives[f])
            def _():
                face_copy(c, f).wait_recv()
        cols = pl.ds(pl.multiple_of(c * width, width), width)
        fix_ref[:, cols] = (total[c] + wide_dot(inv[:, rows:], face_recv[c])).astype(BF16)

    late = chunks - chunks // 4

    @pl.loop(0, late)
    def _(c):
        finish(c)

    def gsum_copy(i):
        to = lax.rem(g + i, n_grp)
        return remote(gal_sum, gal_sum_recv.at[g], gsum_ss.at[to], gsum_rs.at[g], (to, s))

    def gsum_from(i):
        frm = lax.rem(g + i, n_grp)
        return remote(gal_sum, gal_sum_recv.at[frm], gsum_ss.at[frm], gsum_rs.at[frm], (frm, s))

    def sum_piece(i):
        return pl.ds(pl.multiple_of(i * sum_rows, 8), sum_rows)

    def sum_copy(i):
        to = lax.rem(g + i, n_grp)
        return remote(sum_send.at[sum_piece(to)], sum_recv.at[g], sum_ss.at[to], sum_rs.at[g], (to, s))

    def sum_from(i):
        frm = lax.rem(g + i, n_grp)
        return remote(sum_send.at[sum_piece(frm)], sum_recv.at[frm], sum_ss.at[frm], sum_rs.at[frm], (frm, s))

    def last_copy(i):
        to = lax.rem(g + i, n_grp)
        return remote(sum_last, sum_full.at[sum_piece(g)], last_ss.at[to], last_rs.at[g], (to, s))

    def last_from(i):
        frm = lax.rem(g + i, n_grp)
        return remote(sum_last, sum_full.at[sum_piece(frm)], last_ss.at[frm], last_rs.at[frm], (frm, s))

    def glast_copy(i):
        to = lax.rem(s + i, n_sub)
        return remote(gal_last, gal_full.at[gal_piece(s)], glast_ss.at[to], glast_rs.at[s], (g, to))

    def glast_from(i):
        frm = lax.rem(s + i, n_sub)
        return remote(gal_last, gal_full.at[gal_piece(frm)], glast_ss.at[frm], glast_rs.at[frm], (g, frm))

    @pl.loop(1, chips)
    def _(i):
        gal_from(i).wait_recv()
        gal_sum[...] += gal_recv[lax.rem(chip + i, chips)]

    @pl.loop(1, n_grp)
    def _(i):
        gsum_copy(i).start()

    @pl.loop(1, chips)
    def _(i):
        rhs_from(i).wait_recv()
        sum_send[:coarse, :] += rhs_recv[lax.rem(chip + i, chips)].astype(F32)

    @pl.loop(1, n_grp)
    def _(i):
        sum_copy(i).start()

    @pl.loop(late, chunks)
    def _(c):
        finish(c)

    gal_last[...] = gal_sum[...]

    @pl.loop(1, n_grp)
    def _(i):
        gsum_from(i).wait_recv()
        gal_last[...] += gal_sum_recv[lax.rem(g + i, n_grp)]

    gal_last[...] = gal_last[...] * scaling

    @pl.loop(1, n_sub)
    def _(i):
        glast_copy(i).start()

    sum_last[...] = sum_send[sum_piece(g), :]

    @pl.loop(1, n_grp)
    def _(i):
        sum_from(i).wait_recv()
        sum_last[...] += sum_recv[lax.rem(g + i, n_grp)]

    sum_last[...] = sum_last[...] * scaling

    @pl.loop(1, n_grp)
    def _(i):
        last_copy(i).start()

    gal_full[gal_piece(s), :] = gal_last[...]
    sum_full[sum_piece(g), :] = sum_last[...]

    @pl.loop(1, n_sub)
    def _(i):
        glast_from(i).wait_recv()

    gal_ref[...] = gal_full[:coarse, :]

    @pl.loop(1, n_grp)
    def _(i):
        last_from(i).wait_recv()

    rhs_ref[...] = sum_full[:coarse, :]

    for f in range(4):
        @pl.when(sends[f])
        def _():
            ext_copy(f).wait_send()

            @pl.loop(0, chunks)
            def _(c):
                face_copy(c, f).wait_send()

    @pl.loop(0, chunks)
    def _(c):
        when_relaying(c, lambda copy: copy.wait_send())

    gal_swap.wait_send()

    @pl.loop(0, chips)
    def _(i):
        pair_copy(i).wait_send()

    @pl.loop(1, chips)
    def _(i):
        rhs_copy(i).wait_send()
        gal_copy(i).wait_send()

    @pl.loop(1, n_sub)
    def _(i):
        glast_copy(i).wait_send()

    @pl.loop(1, n_grp)
    def _(i):
        gsum_copy(i).wait_send()
        sum_copy(i).wait_send()
        last_copy(i).wait_send()


def local_any(n_grp, n_sub, residual, inverse_blocks, operator_tiles, column_blocks, coarse_basis, face_rows):
    resid = residual[0, 0]
    inv = inverse_blocks[0, 0]
    tiles = operator_tiles[0, 0]
    basis = jnp.swapaxes(coarse_basis[0, 0], 0, 1)
    faces = face_rows[0, 0]
    rows, k = resid.shape
    coarse = basis.shape[0]
    ov = faces.shape[1]
    tile = tiles.shape[-1]
    ext_blocks = inv.shape[1] // tile
    part = k // n_sub
    width = max(512, part)
    chunks = k // width
    gal_rows = -(-coarse // (8 * n_sub)) * 8
    sum_rows = -(-coarse // (8 * n_grp)) * 8
    chips = n_sub // 2
    scaling = 1.0 / math.sqrt(rows * n_grp * n_sub)
    dma = pltpu.SemaphoreType.DMA
    hbm = pl.BlockSpec(memory_space=pl.ANY)
    vmem = pl.BlockSpec(memory_space=pltpu.VMEM)
    fix, gal, rhs = pl.pallas_call(
        functools.partial(ring_free_kernel, n_grp, n_sub, width, scaling),
        out_shape=(
            pltpu.VMEM((rows, k), BF16),
            pltpu.VMEM((coarse, coarse), F32),
            pltpu.VMEM((coarse, part), F32),
        ),
        in_specs=[pl.BlockSpec(memory_space=pltpu.SMEM), vmem, vmem, hbm, hbm, hbm],
        out_specs=(vmem, vmem, vmem),
        scratch_shapes=[
            pltpu.VMEM((chunks, rows, width), BF16),
            pltpu.VMEM(inv.shape, BF16),
            pltpu.VMEM(tiles.shape, BF16),
            pltpu.VMEM((4 * ov, rows), BF16),
            pltpu.VMEM((4, coarse, tile), BF16),
            pltpu.VMEM((ext_blocks, coarse, tile), BF16),
            pltpu.VMEM((chunks, 4 * ov, width), BF16),
            pltpu.VMEM((chunks, 4 * ov, width), BF16),
            pltpu.VMEM((chunks, ov, width), BF16),
            pltpu.VMEM((chunks, rows, width), F32),
            pltpu.VMEM((chips, coarse, part), F32),
            pltpu.VMEM((chips, coarse, part), F32),
            pltpu.VMEM((chips, coarse, part), F32),
            pltpu.VMEM((chips, coarse, part), BF16),
            pltpu.VMEM((chips, coarse, part), BF16),
            pltpu.VMEM((n_grp * sum_rows, part), F32),
            pltpu.VMEM((n_grp, sum_rows, part), F32),
            pltpu.VMEM((sum_rows, part), F32),
            pltpu.VMEM((n_grp * sum_rows, part), F32),
            pltpu.VMEM((rows, coarse), BF16),
            pltpu.VMEM((n_sub * gal_rows, coarse), F32),
            pltpu.VMEM((n_sub * gal_rows, coarse), F32),
            pltpu.VMEM((n_sub * gal_rows, coarse), F32),
            pltpu.VMEM((chips, gal_rows, coarse), F32),
            pltpu.VMEM((gal_rows, coarse), F32),
            pltpu.VMEM((n_grp, gal_rows, coarse), F32),
            pltpu.VMEM((gal_rows, coarse), F32),
            pltpu.VMEM((n_sub * gal_rows, coarse), F32),
            dma((2,)),
            dma((chunks,)),
            dma((4,)),
            dma((4,)),
            dma((chunks, 4)),
            dma((chunks, 4)),
            dma((chunks,)),
            dma((chunks,)),
            dma((chips,)),
            dma((chips,)),
            dma((1,)),
            dma((1,)),
            dma((chips,)),
            dma((chips,)),
            dma((n_grp,)),
            dma((n_grp,)),
            dma((n_grp,)),
            dma((n_grp,)),
            dma((chips,)),
            dma((chips,)),
            dma((n_grp,)),
            dma((n_grp,)),
            dma((n_sub,)),
            dma((n_sub,)),
        ],
        compiler_params=pltpu.CompilerParams(
            collective_id=0, has_side_effects=True, vmem_limit_bytes=55 * 1024 * 1024
        ),
    )(column_blocks[0, 0], faces, basis, resid, inv, tiles)
    return fix[None, None], gal, rhs


def plane_kernel(
    n_sub, scaling, relayed, early,
    col_ref, face_ref, basis_ref, resid_hbm, inv_hbm, tiles_hbm,
    fix_ref, gal_ref, rhs_ref,
    resid, inv, tiles, left, ext_send, ext, face_send, face_recv, relay, total,
    keep, pair_send, pair_recv, y_keep, y_send, y_recv, z_send, z_recv, x_send, x_recv, back_send, back_recv,
    applied, gal, gal_pair, gal_both, gal_recv, gal_sum, gal_other, gal_last, gal_full, gal_half,
    in_sem, resid_sem, ext_ss, ext_rs, face_ss, face_rs, relay_ss, relay_rs,
    pair_ss, pair_rs, y_ss, y_rs, z_ss, z_rs, swap_ss, swap_rs, gal_ss, gal_rs, glast_ss, glast_rs,
):
    g = lax.axis_index("grp")
    s = lax.axis_index("sub")
    n_grp = 4
    gx, gy = lax.rem(g, 2), g // 2
    chip, core = s // 2, lax.rem(s, 2)
    beside = g + 1 - 2 * gx
    above = lax.rem(g + 2, 4)
    x_near, y_near, pair = (beside, s), (above, s), (g, s + 1 - 2 * core)
    chips = n_sub // 2
    chunks, rows, width = resid.shape
    coarse = basis_ref.shape[0]
    row_blocks, per_row, tile = tiles.shape[:3]
    own_blocks = rows // tile
    ov = face_ref.shape[1]
    faces = 4 * ov
    part = width // 2
    half = part // 2
    pieces = 2 * chips
    piece_rows = gal_sum.shape[0]
    me = chip * 2 + gy

    def load_resid(c):
        cols = pl.ds(pl.multiple_of(c * width, width), width)
        return pltpu.make_async_copy(resid_hbm.at[:, cols], resid.at[c], resid_sem.at[c])

    load_tiles = pltpu.make_async_copy(tiles_hbm, tiles, in_sem.at[0])
    load_inv = pltpu.make_async_copy(inv_hbm, inv, in_sem.at[1])

    @pl.loop(0, chunks)
    def _(c):
        load_resid(c).start()

    load_tiles.start()
    load_inv.start()

    barrier = pltpu.get_barrier_semaphore()

    def greet(device):
        pl.semaphore_signal(barrier, inc=1, device_id=device, device_id_type=MESH)

    greet(x_near)
    greet((n_grp - 1 - g, s))

    @pl.loop(1, n_sub)
    def _(i):
        greet((g, lax.rem(s + i, n_sub)))

    @pl.loop(0, chips)
    def _(i):
        greet((above, i * 2 + core))

    targets = ((g + 1, s), (g - 1, s), (g, s + 1), (g, s - 1))
    sends = (g < n_grp - 1, g > 0, s < n_sub - 1, s > 0)
    arrives = (g > 0, g < n_grp - 1, s > 0, s < n_sub - 1)

    def remote(src, dst, send_sem, recv_sem, device):
        return pltpu.make_async_remote_copy(
            src_ref=src, dst_ref=dst, send_sem=send_sem, recv_sem=recv_sem,
            device_id=device, device_id_type=MESH,
        )

    def ext_copy(f):
        return remote(ext_send.at[f], ext.at[own_blocks + f], ext_ss.at[f], ext_rs.at[f], targets[f])

    def face_copy(c, f):
        span = pl.ds(f * ov, ov)
        return remote(face_send.at[c, span], face_recv.at[c, span], face_ss.at[c, f], face_rs.at[c, f], targets[f])

    def relay_in(c, f):
        return remote(face_send.at[c, pl.ds(f * ov, ov)], relay.at[c], face_ss.at[c, f], relay_rs.at[c], y_near)

    def relay_out(c, f):
        span = pl.ds(f * ov, ov)
        return remote(relay.at[c], face_recv.at[c, span], relay_ss.at[c], face_rs.at[c, f], x_near)

    def when_relaying(do):
        for f, at in ((0, n_grp - 1), (1, 0)):
            @pl.when(g == at)
            def _():
                do(f)

    def face_start(c, f):
        if f >= 2:
            @pl.when(sends[f])
            def _():
                face_copy(c, f).start()
            return
        far = g == 1 + f

        @pl.when(jnp.logical_and(far, c < relayed))
        def _():
            relay_in(c, f).start()

        @pl.when(jnp.logical_and(far, c >= relayed))
        def _():
            face_copy(c, f).start()

        @pl.when(jnp.logical_and(jnp.logical_and(sends[f], jnp.logical_not(far)), c < early))
        def _():
            face_copy(c, f).start()

    def held_start(c, f):
        @pl.when(jnp.logical_and(sends[f], g != 1 + f))
        def _():
            face_copy(c, f).start()

    lanes = lax.broadcasted_iota(jnp.int32, (ov, tile), 1)
    for f in range(4):
        wanted = jnp.broadcast_to(face_ref[f:f + 1, :].astype(F32), (ov, ov)).T.astype(jnp.int32)
        for b in range(own_blocks):
            hit = wanted == lanes + b * tile
            left[f * ov:(f + 1) * ov, b * tile:(b + 1) * tile] = jnp.where(hit, 1.0, 0.0).astype(BF16)
    basis = basis_ref[...]
    left[faces:faces + coarse, :] = basis
    if left.shape[0] > faces + coarse:
        left[faces + coarse:, :] = jnp.zeros((left.shape[0] - faces - coarse, rows), BF16)
    for f in range(4):
        ext_send[f] = dot_rows(basis, left[f * ov:(f + 1) * ov, :]).astype(BF16)

    pl.semaphore_wait(barrier, n_sub - 1 + chips + 2)
    for f in range(4):
        @pl.when(sends[f])
        def _():
            ext_copy(f).start()

    def pair_copy(c):
        return remote(pair_send.at[c], pair_recv.at[c], pair_ss.at[c], pair_rs.at[c], pair)

    @pl.loop(0, chunks)
    def _(c):
        load_resid(c).wait()
        both = wide_dot(left[...], resid[c])
        face_send[c] = both[:faces].astype(BF16)
        for f in range(4):
            face_start(c, f)
        for q in range(2):
            @pl.when(core == q)
            def _():
                keep[c] = both[faces:faces + coarse, q * part:(q + 1) * part]
                pair_send[c] = both[faces:faces + coarse, (1 - q) * part:(2 - q) * part]

        pair_copy(c).start()

    for f in range(4):
        @pl.when(jnp.logical_not(arrives[f]))
        def _():
            ext[own_blocks + f] = jnp.zeros((coarse, tile), BF16)
            face_recv[:, f * ov:(f + 1) * ov, :] = jnp.zeros((chunks, ov, width), BF16)
    for b in range(own_blocks):
        ext[b] = basis_ref[:, b * tile:(b + 1) * tile]

    def y_copy(c):
        return remote(y_send.at[c], y_recv.at[c], y_ss.at[c], y_rs.at[c], y_near)

    def columns(i):
        return pl.ds(pl.multiple_of(i * half, half), half)

    @pl.loop(0, chunks)
    def _(c):
        pair_copy(c).wait_recv()
        y_send[c] = (keep[c, :, columns(1 - gy)] + pair_recv[c, :, columns(1 - gy)]).astype(BF16)
        y_copy(c).start()
        y_keep[c] = keep[c, :, columns(gy)] + pair_recv[c, :, columns(gy)]

    load_tiles.wait()
    for f in range(4):
        @pl.when(arrives[f])
        def _():
            ext_copy(f).wait_recv()

    @pl.loop(0, row_blocks)
    def _(b):
        row = jnp.concatenate([tiles[b, j] for j in range(per_row)], axis=1)
        picked = jnp.concatenate([ext[col_ref[b, j]] for j in range(per_row)], axis=1)
        applied[pl.ds(pl.multiple_of(b * tile, tile), tile), :] = dot_rows(row, picked).astype(BF16)

    whole = wide_dot(basis_ref[...], applied[...])
    wide = gal.shape[2]
    gal[0, :coarse, :] = whole[:, :wide]
    gal[0, coarse:, :] = jnp.zeros((gal.shape[1] - coarse, wide), F32)
    gal[1] = jnp.zeros(gal.shape[1:], F32)
    gal[1, :coarse, :coarse - wide] = whole[:, wide:]
    gal_swap = remote(gal.at[1 - core], gal_pair, swap_ss.at[0], swap_rs.at[0], pair)
    gal_swap.start()

    load_inv.wait()

    def multiply(c):
        total[c] = wide_dot(inv[:, :rows], resid[c])

    multiply(0)

    def rows_of(i):
        return pl.ds(pl.multiple_of(i * piece_rows, 8), piece_rows)

    def holder(i):
        return (lax.rem(i, 2) * 2 + gx, (i // 2) * 2 + core)

    def gal_copy(i):
        to = lax.rem(me + i, pieces)
        return remote(gal_both.at[rows_of(to)], gal_recv.at[me], gal_ss.at[to], gal_rs.at[me], holder(to))

    def gal_from(i):
        frm = lax.rem(me + i, pieces)
        return remote(gal_both.at[rows_of(frm)], gal_recv.at[frm], gal_ss.at[frm], gal_rs.at[frm], holder(frm))

    gal_swap.wait_recv()
    gal_both[...] = gal[core] + gal_pair[...]

    @pl.loop(1, pieces)
    def _(i):
        gal_copy(i).start()

    def pass_on(f):
        @pl.loop(0, relayed)
        def _(c):
            remote(relay.at[c], relay.at[c], relay_ss.at[c], relay_rs.at[c], y_near).wait_recv()
            relay_out(c, f).start()

    when_relaying(pass_on)

    def z_copy(c):
        return remote(z_send.at[c], z_recv.at[chip], z_ss.at[c], z_rs.at[chip], (g, c * 2 + core))

    def z_from(i):
        frm = lax.rem(chip + i, chips)
        return remote(z_send.at[frm], z_recv.at[frm], z_ss.at[frm], z_rs.at[frm], (g, frm * 2 + core))

    @pl.loop(0, chunks)
    def _(c):
        y_copy(c).wait_recv()
        mine = y_keep[c] + y_recv[c].astype(F32)

        @pl.when(c == chip)
        def _():
            x_send[...] = mine

        @pl.when(c != chip)
        def _():
            z_send[c] = mine.astype(BF16)
            z_copy(c).start()

    multiply(1)
    gal_sum[...] = gal_both[rows_of(me), :]

    @pl.loop(1, pieces)
    def _(i):
        gal_from(i).wait_recv()
        gal_sum[...] += gal_recv[lax.rem(me + i, pieces)]

    gal_cross = remote(gal_sum, gal_other, swap_ss.at[1], swap_rs.at[1], x_near)
    gal_cross.start()
    multiply(2)

    @pl.loop(1, chips)
    def _(i):
        z_from(i).wait_recv()
        x_send[...] += z_recv[lax.rem(chip + i, chips)].astype(F32)

    cross = remote(x_send, x_recv, swap_ss.at[2], swap_rs.at[2], x_near)
    cross.start()
    for c in range(early, chunks):
        for f in range(2):
            held_start(c, f)
    multiply(3)

    def glast_copy(i):
        to = lax.rem(me + i, pieces)
        return remote(gal_last, gal_full.at[rows_of(me)], glast_ss.at[to], glast_rs.at[me], holder(to))

    def glast_from(i):
        frm = lax.rem(me + i, pieces)
        return remote(gal_last, gal_full.at[rows_of(frm)], glast_ss.at[frm], glast_rs.at[frm], holder(frm))

    def finish(c):
        for f in range(4):
            @pl.when(arrives[f])
            def _():
                face_copy(c, f).wait_recv()
        cols = pl.ds(pl.multiple_of(c * width, width), width)
        fix_ref[:, cols] = (total[c] + wide_dot(inv[:, rows:], face_recv[c])).astype(BF16)

    gal_cross.wait_recv()
    gal_last[...] = (gal_sum[...] + gal_other[...]) * scaling

    @pl.loop(1, pieces)
    def _(i):
        glast_copy(i).start()

    gal_full[rows_of(me), :] = gal_last[...]
    finish(0)
    cross.wait_recv()
    back_send[...] = (x_send[...] + x_recv[...]) * scaling
    back = remote(back_send, back_recv, swap_ss.at[3], swap_rs.at[3], y_near)
    back.start()
    rhs_ref[:, columns(gy)] = back_send[...]
    finish(1)

    @pl.loop(1, pieces)
    def _(i):
        glast_from(i).wait_recv()

    gal_last_swap = remote(gal_full, gal_half, swap_ss.at[4], swap_rs.at[4], pair)
    gal_last_swap.start()
    finish(2)
    back.wait_recv()
    rhs_ref[:, columns(1 - gy)] = back_recv[...]
    gal_last_swap.wait_recv()
    for q in range(2):
        @pl.when(core == q)
        def _():
            low, high = (gal_full, gal_half) if q == 0 else (gal_half, gal_full)
            gal_ref[:, :wide] = low[:coarse, :]
            gal_ref[:, wide:] = high[:coarse, :coarse - wide]

    finish(3)

    for f in range(4):
        @pl.when(sends[f])
        def _():
            ext_copy(f).wait_send()

            @pl.loop(0, chunks)
            def _(c):
                face_copy(c, f).wait_send()

    def sent_on(f):
        @pl.loop(0, relayed)
        def _(c):
            relay_out(c, f).wait_send()

    when_relaying(sent_on)

    @pl.loop(0, chunks)
    def _(c):
        pair_copy(c).wait_send()
        y_copy(c).wait_send()

        @pl.when(c != chip)
        def _():
            z_copy(c).wait_send()

    @pl.loop(1, pieces)
    def _(i):
        gal_copy(i).wait_send()
        glast_copy(i).wait_send()

    for copy in (gal_swap, gal_cross, cross, back, gal_last_swap):
        copy.wait_send()


def fits_plane(mesh):
    return mesh.shape["grp"] == 4 and mesh.shape["sub"] == 8


def local_plane(n_grp, n_sub, residual, inverse_blocks, operator_tiles, column_blocks, coarse_basis, face_rows):
    resid = residual[0, 0]
    inv = inverse_blocks[0, 0]
    tiles = operator_tiles[0, 0]
    basis = jnp.swapaxes(coarse_basis[0, 0], 0, 1)
    faces = face_rows[0, 0]
    rows, k = resid.shape
    coarse = basis.shape[0]
    ov = faces.shape[1]
    tile = tiles.shape[-1]
    ext_blocks = inv.shape[1] // tile
    part = k // n_sub
    half = part // 2
    width = 2 * part
    chunks = chips = n_sub // 2
    relayed = chunks // 2
    early = chunks - 1
    pieces = 2 * chips
    piece_rows = -(-coarse // (8 * pieces)) * 8
    wide = -(-coarse // 256) * 128
    scaling = 1.0 / math.sqrt(rows * n_grp * n_sub)
    dma = pltpu.SemaphoreType.DMA
    hbm = pl.BlockSpec(memory_space=pl.ANY)
    vmem = pl.BlockSpec(memory_space=pltpu.VMEM)
    left_rows = -(-(4 * ov + coarse) // 16) * 16
    fix, gal, rhs = pl.pallas_call(
        functools.partial(plane_kernel, n_sub, scaling, relayed, early),
        out_shape=(
            pltpu.VMEM((rows, k), BF16),
            pltpu.VMEM((coarse, coarse), F32),
            pltpu.VMEM((coarse, part), F32),
        ),
        in_specs=[pl.BlockSpec(memory_space=pltpu.SMEM), vmem, vmem, hbm, hbm, hbm],
        out_specs=(vmem, vmem, vmem),
        scratch_shapes=[
            pltpu.VMEM((chunks, rows, width), BF16),
            pltpu.VMEM(inv.shape, BF16),
            pltpu.VMEM(tiles.shape, BF16),
            pltpu.VMEM((left_rows, rows), BF16),
            pltpu.VMEM((4, coarse, tile), BF16),
            pltpu.VMEM((ext_blocks, coarse, tile), BF16),
            pltpu.VMEM((chunks, 4 * ov, width), BF16),
            pltpu.VMEM((chunks, 4 * ov, width), BF16),
            pltpu.VMEM((relayed, ov, width), BF16),
            pltpu.VMEM((chunks, rows, width), F32),
            pltpu.VMEM((chips, coarse, part), F32),
            pltpu.VMEM((chips, coarse, part), F32),
            pltpu.VMEM((chips, coarse, part), F32),
            pltpu.VMEM((chips, coarse, half), F32),
            pltpu.VMEM((chips, coarse, half), BF16),
            pltpu.VMEM((chips, coarse, half), BF16),
            pltpu.VMEM((chips, coarse, half), BF16),
            pltpu.VMEM((chips, coarse, half), BF16),
            pltpu.VMEM((coarse, half), F32),
            pltpu.VMEM((coarse, half), F32),
            pltpu.VMEM((coarse, half), F32),
            pltpu.VMEM((coarse, half), F32),
            pltpu.VMEM((rows, coarse), BF16),
            pltpu.VMEM((2, pieces * piece_rows, wide), F32),
            pltpu.VMEM((pieces * piece_rows, wide), F32),
            pltpu.VMEM((pieces * piece_rows, wide), F32),
            pltpu.VMEM((pieces, piece_rows, wide), F32),
            pltpu.VMEM((piece_rows, wide), F32),
            pltpu.VMEM((piece_rows, wide), F32),
            pltpu.VMEM((piece_rows, wide), F32),
            pltpu.VMEM((pieces * piece_rows, wide), F32),
            pltpu.VMEM((pieces * piece_rows, wide), F32),
            dma((2,)),
            dma((chunks,)),
            dma((4,)),
            dma((4,)),
            dma((chunks, 4)),
            dma((chunks, 4)),
            dma((relayed,)),
            dma((relayed,)),
            dma((chips,)),
            dma((chips,)),
            dma((chips,)),
            dma((chips,)),
            dma((chips,)),
            dma((chips,)),
            dma((5,)),
            dma((5,)),
            dma((pieces,)),
            dma((pieces,)),
            dma((pieces,)),
            dma((pieces,)),
        ],
        compiler_params=pltpu.CompilerParams(
            collective_id=0, has_side_effects=True, vmem_limit_bytes=55 * 1024 * 1024
        ),
    )(column_blocks[0, 0], faces, basis, resid, inv, tiles)
    return fix[None, None], gal, rhs


def solution(mesh):
    body = local_plane if fits_plane(mesh) else local_any
    return jax.shard_map(
        functools.partial(body, mesh.shape["grp"], mesh.shape["sub"]),
        mesh=mesh,
        in_specs=(
            P("grp", "sub", None, None),
            P("grp", "sub", None, None),
            P("grp", "sub", None, None, None, None),
            P("grp", "sub", None, None),
            P("grp", "sub", None, None),
            P("grp", "sub", None, None),
        ),
        out_specs=(P("grp", "sub", None, None), P(), P(None, "sub")),
        check_vma=False,
    )
```

```python
import functools
import math

import jax
import jax.numpy as jnp
from jax import lax
from jax.experimental import pallas as pl
from jax.experimental.pallas import tpu as pltpu
from jax.sharding import PartitionSpec as P

MESH = pl.DeviceIdType.MESH
F32 = jnp.float32
BF16 = jnp.bfloat16


def wide_dot(a, b):
    return jnp.dot(a, b, preferred_element_type=F32)


def dot_rows(a, b):
    return lax.dot_general(a, b, (((1,), (1,)), ((), ())), preferred_element_type=F32)


def any_kernel(
    n_grp, n_sub, width, scaling,
    col_ref, face_ref, basis_ref, resid_hbm, inv_hbm, tiles_hbm,
    fix_ref, gal_ref, rhs_ref,
    resid, inv, tiles, pick, ext_send, ext, face_send, face_recv, relay, total,
    keep, pair_send, pair_recv, rhs_send, rhs_recv, sum_send, sum_recv, sum_last, sum_full,
    applied, gal, gal_pair, gal_both, gal_recv, gal_sum, gal_sum_recv, gal_last, gal_full,
    in_sem, resid_sem, ext_ss, ext_rs, face_ss, face_rs, relay_ss, relay_rs,
    pair_ss, pair_rs, gpair_ss, gpair_rs, rhs_ss, rhs_rs,
    sum_ss, sum_rs, last_ss, last_rs, gal_ss, gal_rs, gsum_ss, gsum_rs, glast_ss, glast_rs,
):
    g = lax.axis_index("grp")
    s = lax.axis_index("sub")
    chip, core = s // 2, lax.rem(s, 2)
    partner = s + 1 - 2 * core
    chips = n_sub // 2
    chunks, rows, _ = resid.shape
    coarse = basis_ref.shape[0]
    row_blocks, per_row, tile = tiles.shape[:3]
    own_blocks = rows // tile
    ov = face_ref.shape[1]
    part = chunks * width // n_sub
    per_chunk = width // part
    gal_rows = gal_recv.shape[1]
    sum_rows = sum_recv.shape[1]
    relayed = n_grp == 4

    def load_resid(c):
        cols = pl.ds(pl.multiple_of(c * width, width), width)
        return pltpu.make_async_copy(resid_hbm.at[:, cols], resid.at[c], resid_sem.at[c])

    load_tiles = pltpu.make_async_copy(tiles_hbm, tiles, in_sem.at[0])
    load_inv = pltpu.make_async_copy(inv_hbm, inv, in_sem.at[1])

    @pl.loop(0, chunks)
    def _(c):
        load_resid(c).start()

    load_tiles.start()
    load_inv.start()

    barrier = pltpu.get_barrier_semaphore()

    @pl.loop(1, n_sub)
    def _(i):
        pl.semaphore_signal(barrier, inc=1, device_id=(g, lax.rem(s + i, n_sub)), device_id_type=MESH)

    @pl.loop(1, n_grp)
    def _(i):
        pl.semaphore_signal(barrier, inc=1, device_id=(lax.rem(g + i, n_grp), s), device_id_type=MESH)

    targets = ((g + 1, s), (g - 1, s), (g, s + 1), (g, s - 1))
    sends = (g < n_grp - 1, g > 0, s < n_sub - 1, s > 0)
    arrives = (g > 0, g < n_grp - 1, s > 0, s < n_sub - 1)

    def remote(src, dst, send_sem, recv_sem, device):
        return pltpu.make_async_remote_copy(
            src_ref=src, dst_ref=dst, send_sem=send_sem, recv_sem=recv_sem,
            device_id=device, device_id_type=MESH,
        )

    def ext_copy(f):
        return remote(ext_send.at[f], ext.at[own_blocks + f], ext_ss.at[f], ext_rs.at[f], targets[f])

    def face_copy(c, f, far=False):
        span = pl.ds(f * ov, ov)
        if far:
            way = (n_grp - 1) * (lax.rem(c + f, 2))
            return remote(face_send.at[c, span], relay.at[c], face_ss.at[c, f], relay_rs.at[c], (way, s))
        return remote(face_send.at[c, span], face_recv.at[c, span], face_ss.at[c, f], face_rs.at[c, f], targets[f])

    def forward(c, f):
        span = pl.ds(f * ov, ov)
        return remote(relay.at[c], face_recv.at[c, span], relay_ss.at[c], face_rs.at[c, f], (2 - f, s))

    def far_face(f):
        return (g == 1 + f) if relayed and f < 2 else None

    def face_start(c, f):
        far = far_face(f)
        if far is None:
            @pl.when(sends[f])
            def _():
                face_copy(c, f).start()
        else:
            @pl.when(far)
            def _():
                face_copy(c, f, True).start()

            @pl.when(jnp.logical_and(sends[f], jnp.logical_not(far)))
            def _():
                face_copy(c, f).start()

    def when_relaying(c, do):
        if relayed:
            turn = lax.rem(c + jnp.where(g == 3, 1, 0), 2)
            for f in range(2):
                @pl.when(jnp.logical_and(jnp.logical_or(g == 0, g == 3), turn == f))
                def _():
                    do(forward(c, f))

    lanes = lax.broadcasted_iota(jnp.int32, (ov, tile), 1)
    for f in range(4):
        wanted = jnp.broadcast_to(face_ref[f:f + 1, :].astype(F32), (ov, ov)).T.astype(jnp.int32)
        for b in range(own_blocks):
            hit = wanted == lanes + b * tile
            pick[f * ov:(f + 1) * ov, b * tile:(b + 1) * tile] = jnp.where(hit, 1.0, 0.0).astype(BF16)
    basis = basis_ref[...]
    for f in range(4):
        ext_send[f] = dot_rows(basis, pick[f * ov:(f + 1) * ov, :]).astype(BF16)
    for b in range(own_blocks):
        ext[b] = basis_ref[:, b * tile:(b + 1) * tile]

    for f in range(4):
        @pl.when(jnp.logical_not(arrives[f]))
        def _():
            ext[own_blocks + f] = jnp.zeros((coarse, tile), BF16)
            face_recv[:, f * ov:(f + 1) * ov, :] = jnp.zeros((chunks, ov, width), BF16)

    pl.semaphore_wait(barrier, n_sub - 1 + n_grp - 1)
    for f in range(4):
        @pl.when(sends[f])
        def _():
            ext_copy(f).start()

    def pair_copy(i):
        return remote(pair_send.at[i], pair_recv.at[i], pair_ss.at[i], pair_rs.at[i], (g, partner))

    @pl.loop(0, chunks)
    def _(c):
        load_resid(c).wait()
        face_send[c] = wide_dot(pick[...], resid[c]).astype(BF16)
        for f in range(4):
            face_start(c, f)
        term = wide_dot(basis_ref[...], resid[c])
        for q in range(per_chunk):
            to = c * per_chunk + q
            piece = term[:, q * part:(q + 1) * part]

            @pl.when(lax.rem(to, 2) == core)
            def _():
                keep[to // 2] = piece

            @pl.when(lax.rem(to, 2) != core)
            def _():
                pair_send[to // 2] = piece
                pair_copy(to // 2).start()

    load_tiles.wait()
    for f in range(4):
        @pl.when(arrives[f])
        def _():
            ext_copy(f).wait_recv()

    @pl.loop(0, row_blocks)
    def _(b):
        row = jnp.concatenate([tiles[b, j] for j in range(per_row)], axis=1)
        picked = jnp.concatenate([ext[col_ref[b, j]] for j in range(per_row)], axis=1)
        applied[pl.ds(pl.multiple_of(b * tile, tile), tile), :] = dot_rows(row, picked).astype(BF16)

    gal[coarse:, :] = jnp.zeros((gal.shape[0] - coarse, coarse), F32)
    gal[:coarse, :] = wide_dot(basis_ref[...], applied[...])

    gal_swap = remote(gal, gal_pair, gpair_ss.at[0], gpair_rs.at[0], (g, partner))
    gal_swap.start()
    def rhs_copy(i):
        to = lax.rem(chip + i, chips)
        return remote(rhs_send.at[to], rhs_recv.at[chip], rhs_ss.at[to], rhs_rs.at[chip], (g, to * 2 + core))

    def rhs_from(i):
        frm = lax.rem(chip + i, chips)
        return remote(rhs_send.at[frm], rhs_recv.at[frm], rhs_ss.at[frm], rhs_rs.at[frm], (g, frm * 2 + core))

    @pl.loop(1, chips)
    def _(i):
        to = lax.rem(chip + i, chips)
        pair_copy(to).wait_recv()
        rhs_send[to] = (keep[to] + pair_recv[to]).astype(BF16)
        rhs_copy(i).start()

    pair_copy(chip).wait_recv()
    sum_send[:coarse, :] = keep[chip] + pair_recv[chip]
    if sum_send.shape[0] > coarse:
        sum_send[coarse:, :] = jnp.zeros((sum_send.shape[0] - coarse, part), F32)
    load_inv.wait()

    @pl.loop(0, chunks // 2)
    def _(c):
        total[c] = wide_dot(inv[:, :rows], resid[c])

    def gal_piece(i):
        return pl.ds(pl.multiple_of(i * gal_rows, 8), gal_rows)

    def gal_copy(i):
        to = lax.rem(chip + i, chips)
        piece = gal_both.at[gal_piece(to * 2 + core)]
        return remote(piece, gal_recv.at[chip], gal_ss.at[to], gal_rs.at[chip], (g, to * 2 + core))

    def gal_from(i):
        frm = lax.rem(chip + i, chips)
        piece = gal_both.at[gal_piece(frm * 2 + core)]
        return remote(piece, gal_recv.at[frm], gal_ss.at[frm], gal_rs.at[frm], (g, frm * 2 + core))

    gal_swap.wait_recv()
    gal_both[...] = gal[...] + gal_pair[...]

    @pl.loop(1, chips)
    def _(i):
        gal_copy(i).start()

    gal_sum[...] = gal_both[gal_piece(s), :]

    @pl.loop(chunks // 2, chunks)
    def _(c):
        total[c] = wide_dot(inv[:, :rows], resid[c])

    def finish(c):
        def pass_on(copy):
            remote(relay.at[c], relay.at[c], relay_ss.at[c], relay_rs.at[c], (1, s)).wait_recv()
            copy.start()

        when_relaying(c, pass_on)
        for f in range(4):
            @pl.when(arrives[f])
            def _():
                face_copy(c, f).wait_recv()
        cols = pl.ds(pl.multiple_of(c * width, width), width)
        fix_ref[:, cols] = (total[c] + wide_dot(inv[:, rows:], face_recv[c])).astype(BF16)

    late = chunks - chunks // 4

    @pl.loop(0, late)
    def _(c):
        finish(c)

    def gsum_copy(i):
        to = lax.rem(g + i, n_grp)
        return remote(gal_sum, gal_sum_recv.at[g], gsum_ss.at[to], gsum_rs.at[g], (to, s))

    def gsum_from(i):
        frm = lax.rem(g + i, n_grp)
        return remote(gal_sum, gal_sum_recv.at[frm], gsum_ss.at[frm], gsum_rs.at[frm], (frm, s))

    def sum_piece(i):
        return pl.ds(pl.multiple_of(i * sum_rows, 8), sum_rows)

    def sum_copy(i):
        to = lax.rem(g + i, n_grp)
        return remote(sum_send.at[sum_piece(to)], sum_recv.at[g], sum_ss.at[to], sum_rs.at[g], (to, s))

    def sum_from(i):
        frm = lax.rem(g + i, n_grp)
        return remote(sum_send.at[sum_piece(frm)], sum_recv.at[frm], sum_ss.at[frm], sum_rs.at[frm], (frm, s))

    def last_copy(i):
        to = lax.rem(g + i, n_grp)
        return remote(sum_last, sum_full.at[sum_piece(g)], last_ss.at[to], last_rs.at[g], (to, s))

    def last_from(i):
        frm = lax.rem(g + i, n_grp)
        return remote(sum_last, sum_full.at[sum_piece(frm)], last_ss.at[frm], last_rs.at[frm], (frm, s))

    def glast_copy(i):
        to = lax.rem(s + i, n_sub)
        return remote(gal_last, gal_full.at[gal_piece(s)], glast_ss.at[to], glast_rs.at[s], (g, to))

    def glast_from(i):
        frm = lax.rem(s + i, n_sub)
        return remote(gal_last, gal_full.at[gal_piece(frm)], glast_ss.at[frm], glast_rs.at[frm], (g, frm))

    @pl.loop(1, chips)
    def _(i):
        gal_from(i).wait_recv()
        gal_sum[...] += gal_recv[lax.rem(chip + i, chips)]

    @pl.loop(1, n_grp)
    def _(i):
        gsum_copy(i).start()

    @pl.loop(1, chips)
    def _(i):
        rhs_from(i).wait_recv()
        sum_send[:coarse, :] += rhs_recv[lax.rem(chip + i, chips)].astype(F32)

    @pl.loop(1, n_grp)
    def _(i):
        sum_copy(i).start()

    @pl.loop(late, chunks)
    def _(c):
        finish(c)

    gal_last[...] = gal_sum[...]

    @pl.loop(1, n_grp)
    def _(i):
        gsum_from(i).wait_recv()
        gal_last[...] += gal_sum_recv[lax.rem(g + i, n_grp)]

    gal_last[...] = gal_last[...] * scaling

    @pl.loop(1, n_sub)
    def _(i):
        glast_copy(i).start()

    sum_last[...] = sum_send[sum_piece(g), :]

    @pl.loop(1, n_grp)
    def _(i):
        sum_from(i).wait_recv()
        sum_last[...] += sum_recv[lax.rem(g + i, n_grp)]

    sum_last[...] = sum_last[...] * scaling

    @pl.loop(1, n_grp)
    def _(i):
        last_copy(i).start()

    gal_full[gal_piece(s), :] = gal_last[...]
    sum_full[sum_piece(g), :] = sum_last[...]

    @pl.loop(1, n_sub)
    def _(i):
        glast_from(i).wait_recv()

    gal_ref[...] = gal_full[:coarse, :]

    @pl.loop(1, n_grp)
    def _(i):
        last_from(i).wait_recv()

    rhs_ref[...] = sum_full[:coarse, :]

    for f in range(4):
        @pl.when(sends[f])
        def _():
            ext_copy(f).wait_send()

            @pl.loop(0, chunks)
            def _(c):
                face_copy(c, f).wait_send()

    @pl.loop(0, chunks)
    def _(c):
        when_relaying(c, lambda copy: copy.wait_send())

    gal_swap.wait_send()

    @pl.loop(0, chips)
    def _(i):
        pair_copy(i).wait_send()

    @pl.loop(1, chips)
    def _(i):
        rhs_copy(i).wait_send()
        gal_copy(i).wait_send()

    @pl.loop(1, n_sub)
    def _(i):
        glast_copy(i).wait_send()

    @pl.loop(1, n_grp)
    def _(i):
        gsum_copy(i).wait_send()
        sum_copy(i).wait_send()
        last_copy(i).wait_send()


def local_any(n_grp, n_sub, residual, inverse_blocks, operator_tiles, column_blocks, coarse_basis, face_rows):
    resid = residual[0, 0]
    inv = inverse_blocks[0, 0]
    tiles = operator_tiles[0, 0]
    basis = jnp.swapaxes(coarse_basis[0, 0], 0, 1)
    faces = face_rows[0, 0]
    rows, k = resid.shape
    coarse = basis.shape[0]
    ov = faces.shape[1]
    tile = tiles.shape[-1]
    ext_blocks = inv.shape[1] // tile
    part = k // n_sub
    width = max(512, part)
    chunks = k // width
    gal_rows = -(-coarse // (8 * n_sub)) * 8
    sum_rows = -(-coarse // (8 * n_grp)) * 8
    chips = n_sub // 2
    scaling = 1.0 / math.sqrt(rows * n_grp * n_sub)
    dma = pltpu.SemaphoreType.DMA
    hbm = pl.BlockSpec(memory_space=pl.ANY)
    vmem = pl.BlockSpec(memory_space=pltpu.VMEM)
    fix, gal, rhs = pl.pallas_call(
        functools.partial(any_kernel, n_grp, n_sub, width, scaling),
        out_shape=(
            pltpu.VMEM((rows, k), BF16),
            pltpu.VMEM((coarse, coarse), F32),
            pltpu.VMEM((coarse, part), F32),
        ),
        in_specs=[pl.BlockSpec(memory_space=pltpu.SMEM), vmem, vmem, hbm, hbm, hbm],
        out_specs=(vmem, vmem, vmem),
        scratch_shapes=[
            pltpu.VMEM((chunks, rows, width), BF16),
            pltpu.VMEM(inv.shape, BF16),
            pltpu.VMEM(tiles.shape, BF16),
            pltpu.VMEM((4 * ov, rows), BF16),
            pltpu.VMEM((4, coarse, tile), BF16),
            pltpu.VMEM((ext_blocks, coarse, tile), BF16),
            pltpu.VMEM((chunks, 4 * ov, width), BF16),
            pltpu.VMEM((chunks, 4 * ov, width), BF16),
            pltpu.VMEM((chunks, ov, width), BF16),
            pltpu.VMEM((chunks, rows, width), F32),
            pltpu.VMEM((chips, coarse, part), F32),
            pltpu.VMEM((chips, coarse, part), F32),
            pltpu.VMEM((chips, coarse, part), F32),
            pltpu.VMEM((chips, coarse, part), BF16),
            pltpu.VMEM((chips, coarse, part), BF16),
            pltpu.VMEM((n_grp * sum_rows, part), F32),
            pltpu.VMEM((n_grp, sum_rows, part), F32),
            pltpu.VMEM((sum_rows, part), F32),
            pltpu.VMEM((n_grp * sum_rows, part), F32),
            pltpu.VMEM((rows, coarse), BF16),
            pltpu.VMEM((n_sub * gal_rows, coarse), F32),
            pltpu.VMEM((n_sub * gal_rows, coarse), F32),
            pltpu.VMEM((n_sub * gal_rows, coarse), F32),
            pltpu.VMEM((chips, gal_rows, coarse), F32),
            pltpu.VMEM((gal_rows, coarse), F32),
            pltpu.VMEM((n_grp, gal_rows, coarse), F32),
            pltpu.VMEM((gal_rows, coarse), F32),
            pltpu.VMEM((n_sub * gal_rows, coarse), F32),
            dma((2,)),
            dma((chunks,)),
            dma((4,)),
            dma((4,)),
            dma((chunks, 4)),
            dma((chunks, 4)),
            dma((chunks,)),
            dma((chunks,)),
            dma((chips,)),
            dma((chips,)),
            dma((1,)),
            dma((1,)),
            dma((chips,)),
            dma((chips,)),
            dma((n_grp,)),
            dma((n_grp,)),
            dma((n_grp,)),
            dma((n_grp,)),
            dma((chips,)),
            dma((chips,)),
            dma((n_grp,)),
            dma((n_grp,)),
            dma((n_sub,)),
            dma((n_sub,)),
        ],
        compiler_params=pltpu.CompilerParams(
            collective_id=0, has_side_effects=True, vmem_limit_bytes=55 * 1024 * 1024
        ),
    )(column_blocks[0, 0], faces, basis, resid, inv, tiles)
    return fix[None, None], gal, rhs


def plane_kernel(
    n_sub, scaling, relayed,
    col_ref, face_ref, basis_ref, resid_hbm, inv_hbm, tiles_hbm,
    fix_ref, gal_ref, rhs_ref,
    resid, inv, tiles, left, ext_send, ext, face_send, face_recv, relay, total,
    keep, pair_send, pair_recv, y_keep, y_send, y_recv, z_send, z_recv, mine, cross_send, cross_recv,
    applied, gal, gal_pair, gal_both, gal_send, gal_recv, gal_sum, gal_other, gal_last, gal_full, gal_half,
    in_sem, resid_sem, ext_ss, ext_rs, face_ss, face_rs, relay_ss, relay_rs,
    pair_ss, pair_rs, y_ss, y_rs, z_ss, z_rs, token_sem, swap_ss, swap_rs, cross_ss, cross_rs, gal_ss, gal_rs, glast_ss, glast_rs,
):
    g = lax.axis_index("grp")
    s = lax.axis_index("sub")
    n_grp = 4
    gx, gy = lax.rem(g, 2), g // 2
    chip, core = s // 2, lax.rem(s, 2)
    beside = g + 1 - 2 * gx
    above = lax.rem(g + 2, 4)
    x_near, y_near, pair = (beside, s), (above, s), (g, s + 1 - 2 * core)
    chips = n_sub // 2
    chunks, rows, width = resid.shape
    coarse = basis_ref.shape[0]
    row_blocks, per_row, tile = tiles.shape[:3]
    own_blocks = rows // tile
    ov = face_ref.shape[1]
    faces = 4 * ov
    part = width // 2
    half = part // 2
    pieces = 2 * chips
    piece_rows = gal_sum.shape[0]
    me = chip * 2 + gy

    def load_resid(c):
        cols = pl.ds(pl.multiple_of(c * width, width), width)
        return pltpu.make_async_copy(resid_hbm.at[:, cols], resid.at[c], resid_sem.at[c])

    load_tiles = pltpu.make_async_copy(tiles_hbm, tiles, in_sem.at[0])
    load_inv = pltpu.make_async_copy(inv_hbm, inv, in_sem.at[1])

    load_resid(0).start()
    load_resid(1).start()

    barrier = pltpu.get_barrier_semaphore()

    def greet(device):
        pl.semaphore_signal(barrier, inc=1, device_id=device, device_id_type=MESH)

    across = s - 1 + 2 * core
    below, over = chip > 0, chip < chips - 1
    faces_across = jnp.logical_and(across >= 0, across < n_sub)
    middle = jnp.logical_and(g > 0, g < n_grp - 1)
    for device in (x_near, y_near, pair):
        greet(device)
    for exists, device in (
        (middle, (n_grp - 1 - g, s)), (faces_across, (g, across)), (below, (g, s - 2)), (over, (g, s + 2)),
    ):
        @pl.when(exists)
        def _():
            greet(device)

    def count(*conditions):
        return sum(jnp.where(condition, 1, 0) for condition in conditions)

    def tell(i, device):
        pl.semaphore_signal(token_sem.at[i], inc=1, device_id=device, device_id_type=MESH)

    def met():
        pl.semaphore_wait(barrier, 3 + count(middle, faces_across, below, over))
        tell(0, y_near)
        for exists, device in ((below, (g, s - 2)), (over, (g, s + 2))):
            @pl.when(exists)
            def _():
                tell(0, device)

    def met_further():
        pl.semaphore_wait(token_sem.at[0], 1 + count(below, over))
        tell(1, (g, lax.rem(s + n_sub // 2, n_sub)))

    def met_all():
        pl.semaphore_wait(token_sem.at[1], 1)

    targets = ((g + 1, s), (g - 1, s), (g, s + 1), (g, s - 1))
    sends = (g < n_grp - 1, g > 0, s < n_sub - 1, s > 0)
    arrives = (g > 0, g < n_grp - 1, s > 0, s < n_sub - 1)

    def remote(src, dst, send_sem, recv_sem, device):
        return pltpu.make_async_remote_copy(
            src_ref=src, dst_ref=dst, send_sem=send_sem, recv_sem=recv_sem,
            device_id=device, device_id_type=MESH,
        )

    def ext_copy(f):
        return remote(ext_send.at[f], ext.at[own_blocks + f], ext_ss.at[f], ext_rs.at[f], targets[f])

    def face_copy(c, f):
        span = pl.ds(f * ov, ov)
        return remote(face_send.at[c, span], face_recv.at[c, span], face_ss.at[c, f], face_rs.at[c, f], targets[f])

    first = chunks - relayed

    def relay_in(c, f):
        slot = c - first
        return remote(face_send.at[c, pl.ds(f * ov, ov)], relay.at[slot], face_ss.at[c, f], relay_rs.at[slot], y_near)

    def relay_out(c, f):
        slot, span = c - first, pl.ds(f * ov, ov)
        return remote(relay.at[slot], face_recv.at[c, span], relay_ss.at[slot], face_rs.at[c, f], x_near)

    def when_relaying(do):
        for f, at in ((0, n_grp - 1), (1, 0)):
            @pl.when(g == at)
            def _():
                do(f)

    def near(c):
        for f in range(2):
            @pl.when(jnp.logical_and(sends[f], g != 1 + f))
            def _():
                face_copy(c, f).start()

    def diagonal(c):
        for f in range(2):
            @pl.when(g == 1 + f)
            def _():
                (face_copy if c < first else relay_in)(c, f).start()

    def side(c):
        for f in range(2, 4):
            @pl.when(sends[f])
            def _():
                face_copy(c, f).start()

    lanes = lax.broadcasted_iota(jnp.int32, (ov, tile), 1)
    for f in range(4):
        wanted = jnp.broadcast_to(face_ref[f:f + 1, :].astype(F32), (ov, ov)).T.astype(jnp.int32)
        for b in range(own_blocks):
            hit = wanted == lanes + b * tile
            left[f * ov:(f + 1) * ov, b * tile:(b + 1) * tile] = jnp.where(hit, 1.0, 0.0).astype(BF16)
    basis = basis_ref[...]
    left[faces:faces + coarse, :] = basis
    if left.shape[0] > faces + coarse:
        left[faces + coarse:, :] = jnp.zeros((left.shape[0] - faces - coarse, rows), BF16)
    for f in range(4):
        ext_send[f] = dot_rows(basis, left[f * ov:(f + 1) * ov, :]).astype(BF16)

    met()
    for f in range(4):
        @pl.when(sends[f])
        def _():
            ext_copy(f).start()

    def pair_copy(c):
        return remote(pair_send.at[c], pair_recv.at[c], pair_ss.at[c], pair_rs.at[c], pair)

    def y_copy(c):
        return remote(y_send.at[c], y_recv.at[c], y_ss.at[c], y_rs.at[c], y_near)

    def columns(i):
        return pl.ds(pl.multiple_of(i * half, half), half)

    def pass_half(c):
        pair_copy(c).wait_recv()
        y_send[c] = (keep[c, :, columns(1 - gy)] + pair_recv[c, :, columns(1 - gy)]).astype(BF16)
        y_copy(c).start()
        y_keep[c] = keep[c, :, columns(gy)] + pair_recv[c, :, columns(gy)]

    def select(c):
        load_resid(c).wait()
        if c == 0:
            for later in range(2, chunks):
                load_resid(later).start()
            load_tiles.start()
        if c == 1:
            load_inv.start()
        both = wide_dot(left[...], resid[c])
        face_send[c] = both[:faces].astype(BF16)
        for q in range(2):
            @pl.when(core == q)
            def _():
                keep[c] = both[faces:faces + coarse, q * part:(q + 1) * part]
                pair_send[c] = both[faces:faces + coarse, (1 - q) * part:(2 - q) * part]

        pair_copy(c).start()

    def fill():
        for f in range(4):
            @pl.when(jnp.logical_not(arrives[f]))
            def _():
                ext[own_blocks + f] = jnp.zeros((coarse, tile), BF16)
                face_recv[:, f * ov:(f + 1) * ov, :] = jnp.zeros((chunks, ov, width), BF16)
        for b in range(own_blocks):
            ext[b] = basis_ref[:, b * tile:(b + 1) * tile]

    wide = gal.shape[2]
    gal_swap = remote(gal.at[1 - core], gal_pair, swap_ss.at[0], swap_rs.at[0], pair)

    def assemble():
        load_tiles.wait()
        for f in range(4):
            @pl.when(arrives[f])
            def _():
                ext_copy(f).wait_recv()

        @pl.loop(0, row_blocks)
        def _(b):
            row = jnp.concatenate([tiles[b, j] for j in range(per_row)], axis=1)
            picked = jnp.concatenate([ext[col_ref[b, j]] for j in range(per_row)], axis=1)
            applied[pl.ds(pl.multiple_of(b * tile, tile), tile), :] = dot_rows(row, picked).astype(BF16)

        whole = wide_dot(basis_ref[...], applied[...])
        gal[0, :coarse, :] = whole[:, :wide]
        gal[0, coarse:, :] = jnp.zeros((gal.shape[1] - coarse, wide), F32)
        gal[1] = jnp.zeros(gal.shape[1:], F32)
        gal[1, :coarse, :coarse - wide] = whole[:, wide:]
        gal_swap.start()

    def multiply(c):
        if c == 3:
            load_inv.wait()
        total[c] = wide_dot(inv[:, :rows], resid[c])

    def z_copy(c):
        return remote(z_send.at[c], z_recv.at[chip], z_ss.at[c], z_rs.at[chip], (g, c * 2 + core))

    def z_from(i):
        frm = lax.rem(chip + i, chips)
        return remote(z_send.at[frm], z_recv.at[frm], z_ss.at[frm], z_rs.at[frm], (g, frm * 2 + core))

    def pass_quarter(c):
        y_copy(c).wait_recv()
        joined = y_keep[c] + y_recv[c].astype(F32)

        @pl.when(chip == c)
        def _():
            mine[...] = joined

        @pl.when(chip != c)
        def _():
            z_send[c] = joined.astype(BF16)
            z_copy(c).start()

    def rows_of(i):
        return pl.ds(pl.multiple_of(i * piece_rows, piece_rows), piece_rows)

    def holder(i):
        return (lax.rem(i, 2) * 2 + gx, (i // 2) * 2 + core)

    def gal_copy(i):
        to = lax.rem(me + i, pieces)
        return remote(gal_send.at[rows_of(to)], gal_recv.at[me], gal_ss.at[to], gal_rs.at[me], holder(to))

    def gal_from(i):
        frm = lax.rem(me + i, pieces)
        return remote(gal_send.at[rows_of(frm)], gal_recv.at[frm], gal_ss.at[frm], gal_rs.at[frm], holder(frm))

    def gal_spread():
        gal_swap.wait_recv()
        gal_both[...] = gal[core] + gal_pair[...]
        gal_send[...] = gal_both[...].astype(BF16)

        @pl.loop(1, pieces)
        def _(i):
            gal_copy(i).start()

    def relay_on(c):
        def do(f):
            slot = c - first
            remote(relay.at[slot], relay.at[slot], relay_ss.at[slot], relay_rs.at[slot], y_near).wait_recv()
            relay_out(c, f).start()

        when_relaying(do)

    gal_cross = remote(gal_sum, gal_other, swap_ss.at[1], swap_rs.at[1], x_near)

    def gal_gather():
        gal_sum[...] = gal_both[rows_of(me), :]

        @pl.loop(1, pieces)
        def _(i):
            gal_from(i).wait_recv()
            gal_sum[...] += gal_recv[lax.rem(me + i, pieces)].astype(F32)

        gal_cross.start()

    def cross_copy(i):
        to = lax.rem(g + i, n_grp)
        return remote(cross_send, cross_recv.at[g], cross_ss.at[to], cross_rs.at[g], (to, s))

    def cross_from(i):
        frm = lax.rem(g + i, n_grp)
        return remote(cross_send, cross_recv.at[frm], cross_ss.at[frm], cross_rs.at[frm], (frm, s))

    def cross():
        @pl.loop(1, chips)
        def _(i):
            z_from(i).wait_recv()
            mine[...] += z_recv[lax.rem(chip + i, chips)].astype(F32)

        cross_send[...] = mine[...].astype(BF16)

        @pl.loop(1, n_grp)
        def _(i):
            cross_copy(i).start()

    def glast_copy(i):
        to = lax.rem(me + i, pieces)
        return remote(gal_last, gal_full.at[rows_of(me)], glast_ss.at[to], glast_rs.at[me], holder(to))

    def glast_from(i):
        frm = lax.rem(me + i, pieces)
        return remote(gal_last, gal_full.at[rows_of(frm)], glast_ss.at[frm], glast_rs.at[frm], holder(frm))

    def await_faces(c, which):
        for f in which:
            @pl.when(arrives[f])
            def _():
                face_copy(c, f).wait_recv()

    def finish(c):
        await_faces(c, range(4))
        fix_ref[:, c * width:(c + 1) * width] = (total[c] + wide_dot(inv[:, rows:], face_recv[c])).astype(BF16)

    def add_sides(c):
        await_faces(c, (2, 3))
        total[c] += wide_dot(inv[:, rows + 2 * ov:], face_recv[c, 2 * ov:, :])

    def finish_near(c):
        await_faces(c, (0, 1))
        near_part = wide_dot(inv[:, rows:rows + 2 * ov], face_recv[c, :2 * ov, :])
        fix_ref[:, c * width:(c + 1) * width] = (total[c] + near_part).astype(BF16)

    def gal_return():
        gal_cross.wait_recv()
        gal_last[...] = (gal_sum[...] + gal_other[...]) * scaling

        @pl.loop(1, pieces)
        def _(i):
            glast_copy(i).start()

        gal_full[rows_of(me), :] = gal_last[...]

    gal_last_swap = remote(gal_full, gal_half, swap_ss.at[2], swap_rs.at[2], pair)

    def gal_share():
        @pl.loop(1, pieces)
        def _(i):
            glast_from(i).wait_recv()

        gal_last_swap.start()

    def gal_end():
        gal_last_swap.wait_recv()
        for q in range(2):
            @pl.when(core == q)
            def _():
                low, high = (gal_full, gal_half) if q == 0 else (gal_half, gal_full)
                gal_ref[:, :wide] = low[:coarse, :]
                gal_ref[:, wide:] = high[:coarse, :coarse - wide]

    def rhs_end():
        @pl.loop(1, n_grp)
        def _(i):
            cross_from(i).wait_recv()

        ours = cross_send[...].astype(F32) + cross_recv[beside].astype(F32)
        theirs = cross_recv[above].astype(F32) + cross_recv[n_grp - 1 - g].astype(F32)
        rhs_ref[:, columns(gy)] = ours * scaling
        rhs_ref[:, columns(1 - gy)] = theirs * scaling

    select(0)
    diagonal(0)
    select(1)
    near(1)
    fill()
    side(1)
    pass_half(0)
    select(2)
    diagonal(2)
    near(0)
    side(2)
    select(3)
    side(0)
    pass_half(1)
    side(3)
    met_further()
    assemble()
    pass_half(3)
    met_all()
    pass_quarter(0)
    near(2)
    multiply(3)
    gal_spread()
    pass_half(2)
    multiply(0)
    diagonal(3)
    relay_on(2)
    pass_quarter(3)
    multiply(2)
    pass_quarter(2)
    pass_quarter(1)
    diagonal(1)
    gal_gather()
    add_sides(3)
    relay_on(3)
    cross()
    gal_return()
    near(3)
    finish(0)
    multiply(1)
    finish(2)
    finish(1)
    rhs_end()
    gal_share()
    finish_near(3)
    gal_end()
    for f in range(4):
        @pl.when(sends[f])
        def _():
            ext_copy(f).wait_send()

            @pl.loop(0, chunks)
            def _(c):
                face_copy(c, f).wait_send()

    def sent_on(f):
        @pl.loop(first, chunks)
        def _(c):
            relay_out(c, f).wait_send()

    when_relaying(sent_on)

    @pl.loop(0, chunks)
    def _(c):
        pair_copy(c).wait_send()
        y_copy(c).wait_send()

        @pl.when(c != chip)
        def _():
            z_copy(c).wait_send()

    @pl.loop(1, pieces)
    def _(i):
        gal_copy(i).wait_send()
        glast_copy(i).wait_send()

    @pl.loop(1, n_grp)
    def _(i):
        cross_copy(i).wait_send()

    for copy in (gal_swap, gal_cross, gal_last_swap):
        copy.wait_send()


def store_kernel(fix_vmem, gal_vmem, rhs_vmem, fix_hbm, gal_hbm, rhs_hbm, sems):
    parts = sems.shape[0] - 2
    span = fix_vmem.shape[0] // parts
    pairs = [(gal_vmem, gal_hbm), (rhs_vmem, rhs_hbm)]
    pairs += [(fix_vmem.at[pl.ds(i * span, span)], fix_hbm.at[pl.ds(i * span, span)]) for i in range(parts)]
    copies = [pltpu.make_async_copy(src, dst, sems.at[i]) for i, (src, dst) in enumerate(pairs)]
    for copy in copies:
        copy.start()
    for copy in copies:
        copy.wait()


def fits_plane(mesh):
    return mesh.shape["grp"] == 4 and mesh.shape["sub"] == 8


def local_plane(n_grp, n_sub, residual, inverse_blocks, operator_tiles, column_blocks, coarse_basis, face_rows):
    resid = residual[0, 0]
    inv = inverse_blocks[0, 0]
    tiles = operator_tiles[0, 0]
    basis = jnp.swapaxes(coarse_basis[0, 0], 0, 1)
    faces = face_rows[0, 0]
    rows, k = resid.shape
    coarse = basis.shape[0]
    ov = faces.shape[1]
    tile = tiles.shape[-1]
    ext_blocks = inv.shape[1] // tile
    part = k // n_sub
    half = part // 2
    width = 2 * part
    chunks = chips = n_sub // 2
    relayed = chunks // 2
    pieces = 2 * chips
    piece_rows = -(-coarse // (16 * pieces)) * 16
    wide = -(-coarse // 256) * 128
    scaling = 1.0 / math.sqrt(rows * n_grp * n_sub)
    dma = pltpu.SemaphoreType.DMA
    hbm = pl.BlockSpec(memory_space=pl.ANY)
    vmem = pl.BlockSpec(memory_space=pltpu.VMEM)
    left_rows = -(-(4 * ov + coarse) // 16) * 16
    fix, gal, rhs = pl.pallas_call(
        functools.partial(plane_kernel, n_sub, scaling, relayed),
        out_shape=(
            pltpu.VMEM((rows, k), BF16),
            pltpu.VMEM((coarse, coarse), F32),
            pltpu.VMEM((coarse, part), F32),
        ),
        in_specs=[pl.BlockSpec(memory_space=pltpu.SMEM), vmem, vmem, hbm, hbm, hbm],
        out_specs=(vmem, vmem, vmem),
        scratch_shapes=[
            pltpu.VMEM((chunks, rows, width), BF16),
            pltpu.VMEM(inv.shape, BF16),
            pltpu.VMEM(tiles.shape, BF16),
            pltpu.VMEM((left_rows, rows), BF16),
            pltpu.VMEM((4, coarse, tile), BF16),
            pltpu.VMEM((ext_blocks, coarse, tile), BF16),
            pltpu.VMEM((chunks, 4 * ov, width), BF16),
            pltpu.VMEM((chunks, 4 * ov, width), BF16),
            pltpu.VMEM((relayed, ov, width), BF16),
            pltpu.VMEM((chunks, rows, width), F32),
            pltpu.VMEM((chips, coarse, part), F32),
            pltpu.VMEM((chips, coarse, part), F32),
            pltpu.VMEM((chips, coarse, part), F32),
            pltpu.VMEM((chips, coarse, half), F32),
            pltpu.VMEM((chips, coarse, half), BF16),
            pltpu.VMEM((chips, coarse, half), BF16),
            pltpu.VMEM((chips, coarse, half), BF16),
            pltpu.VMEM((chips, coarse, half), BF16),
            pltpu.VMEM((coarse, half), F32),
            pltpu.VMEM((coarse, half), BF16),
            pltpu.VMEM((n_grp, coarse, half), BF16),
            pltpu.VMEM((rows, coarse), BF16),
            pltpu.VMEM((2, pieces * piece_rows, wide), F32),
            pltpu.VMEM((pieces * piece_rows, wide), F32),
            pltpu.VMEM((pieces * piece_rows, wide), F32),
            pltpu.VMEM((pieces * piece_rows, wide), BF16),
            pltpu.VMEM((pieces, piece_rows, wide), BF16),
            pltpu.VMEM((piece_rows, wide), F32),
            pltpu.VMEM((piece_rows, wide), F32),
            pltpu.VMEM((piece_rows, wide), F32),
            pltpu.VMEM((pieces * piece_rows, wide), F32),
            pltpu.VMEM((pieces * piece_rows, wide), F32),
            dma((2,)),
            dma((chunks,)),
            dma((4,)),
            dma((4,)),
            dma((chunks, 4)),
            dma((chunks, 4)),
            dma((relayed,)),
            dma((relayed,)),
            dma((chips,)),
            dma((chips,)),
            dma((chips,)),
            dma((chips,)),
            dma((chips,)),
            dma((chips,)),
            pltpu.SemaphoreType.REGULAR((2,)),
            dma((3,)),
            dma((3,)),
            dma((n_grp,)),
            dma((n_grp,)),
            dma((pieces,)),
            dma((pieces,)),
            dma((pieces,)),
            dma((pieces,)),
        ],
        compiler_params=pltpu.CompilerParams(
            collective_id=0, has_side_effects=True, vmem_limit_bytes=55 * 1024 * 1024
        ),
    )(column_blocks[0, 0], faces, basis, resid, inv, tiles)
    fix, gal, rhs = pl.pallas_call(
        store_kernel,
        out_shape=tuple(jax.ShapeDtypeStruct(x.shape, x.dtype) for x in (fix, gal, rhs)),
        in_specs=[vmem, vmem, vmem],
        out_specs=(hbm, hbm, hbm),
        scratch_shapes=[dma((3,))],
        compiler_params=pltpu.CompilerParams(vmem_limit_bytes=16 * 1024 * 1024),
    )(*(pltpu.with_memory_space_constraint(x, pltpu.VMEM) for x in (fix, gal, rhs)))
    return fix[None, None], gal, rhs


def solution(mesh):
    body = local_plane if fits_plane(mesh) else local_any
    return jax.shard_map(
        functools.partial(body, mesh.shape["grp"], mesh.shape["sub"]),
        mesh=mesh,
        in_specs=(
            P("grp", "sub", None, None),
            P("grp", "sub", None, None),
            P("grp", "sub", None, None, None, None),
            P("grp", "sub", None, None),
            P("grp", "sub", None, None),
            P("grp", "sub", None, None),
        ),
        out_specs=(P("grp", "sub", None, None), P(), P(None, "sub")),
        check_vma=False,
    )
```

```python
import functools
import math

import jax
import jax.numpy as jnp
from jax import lax
from jax.experimental import pallas as pl
from jax.experimental.pallas import tpu as pltpu
from jax.sharding import PartitionSpec as P

MESH = pl.DeviceIdType.MESH
F32 = jnp.float32
BF16 = jnp.bfloat16


def wide_dot(a, b):
    return jnp.dot(a, b, preferred_element_type=F32)


def dot_rows(a, b):
    return lax.dot_general(a, b, (((1,), (1,)), ((), ())), preferred_element_type=F32)


def any_kernel(
    n_grp, n_sub, width, scaling,
    col_ref, face_ref, basis_ref, resid_hbm, inv_hbm, tiles_hbm,
    fix_ref, gal_ref, rhs_ref,
    resid, inv, tiles, pick, ext_send, ext, face_send, face_recv, relay, total,
    keep, pair_send, pair_recv, rhs_send, rhs_recv, sum_send, sum_recv, sum_last, sum_full,
    applied, gal, gal_pair, gal_both, gal_recv, gal_sum, gal_sum_recv, gal_last, gal_full,
    in_sem, resid_sem, ext_ss, ext_rs, face_ss, face_rs, relay_ss, relay_rs,
    pair_ss, pair_rs, gpair_ss, gpair_rs, rhs_ss, rhs_rs,
    sum_ss, sum_rs, last_ss, last_rs, gal_ss, gal_rs, gsum_ss, gsum_rs, glast_ss, glast_rs,
):
    g = lax.axis_index("grp")
    s = lax.axis_index("sub")
    chip, core = s // 2, lax.rem(s, 2)
    partner = s + 1 - 2 * core
    chips = n_sub // 2
    chunks, rows, _ = resid.shape
    coarse = basis_ref.shape[0]
    row_blocks, per_row, tile = tiles.shape[:3]
    own_blocks = rows // tile
    ov = face_ref.shape[1]
    part = chunks * width // n_sub
    per_chunk = width // part
    gal_rows = gal_recv.shape[1]
    sum_rows = sum_recv.shape[1]
    relayed = n_grp == 4

    def load_resid(c):
        cols = pl.ds(pl.multiple_of(c * width, width), width)
        return pltpu.make_async_copy(resid_hbm.at[:, cols], resid.at[c], resid_sem.at[c])

    load_tiles = pltpu.make_async_copy(tiles_hbm, tiles, in_sem.at[0])
    load_inv = pltpu.make_async_copy(inv_hbm, inv, in_sem.at[1])

    @pl.loop(0, chunks)
    def _(c):
        load_resid(c).start()

    load_tiles.start()
    load_inv.start()

    barrier = pltpu.get_barrier_semaphore()

    @pl.loop(1, n_sub)
    def _(i):
        pl.semaphore_signal(barrier, inc=1, device_id=(g, lax.rem(s + i, n_sub)), device_id_type=MESH)

    @pl.loop(1, n_grp)
    def _(i):
        pl.semaphore_signal(barrier, inc=1, device_id=(lax.rem(g + i, n_grp), s), device_id_type=MESH)

    targets = ((g + 1, s), (g - 1, s), (g, s + 1), (g, s - 1))
    sends = (g < n_grp - 1, g > 0, s < n_sub - 1, s > 0)
    arrives = (g > 0, g < n_grp - 1, s > 0, s < n_sub - 1)

    def remote(src, dst, send_sem, recv_sem, device):
        return pltpu.make_async_remote_copy(
            src_ref=src, dst_ref=dst, send_sem=send_sem, recv_sem=recv_sem,
            device_id=device, device_id_type=MESH,
        )

    def ext_copy(f):
        return remote(ext_send.at[f], ext.at[own_blocks + f], ext_ss.at[f], ext_rs.at[f], targets[f])

    def face_copy(c, f, far=False):
        span = pl.ds(f * ov, ov)
        if far:
            way = (n_grp - 1) * (lax.rem(c + f, 2))
            return remote(face_send.at[c, span], relay.at[c], face_ss.at[c, f], relay_rs.at[c], (way, s))
        return remote(face_send.at[c, span], face_recv.at[c, span], face_ss.at[c, f], face_rs.at[c, f], targets[f])

    def forward(c, f):
        span = pl.ds(f * ov, ov)
        return remote(relay.at[c], face_recv.at[c, span], relay_ss.at[c], face_rs.at[c, f], (2 - f, s))

    def far_face(f):
        return (g == 1 + f) if relayed and f < 2 else None

    def face_start(c, f):
        far = far_face(f)
        if far is None:
            @pl.when(sends[f])
            def _():
                face_copy(c, f).start()
        else:
            @pl.when(far)
            def _():
                face_copy(c, f, True).start()

            @pl.when(jnp.logical_and(sends[f], jnp.logical_not(far)))
            def _():
                face_copy(c, f).start()

    def when_relaying(c, do):
        if relayed:
            turn = lax.rem(c + jnp.where(g == 3, 1, 0), 2)
            for f in range(2):
                @pl.when(jnp.logical_and(jnp.logical_or(g == 0, g == 3), turn == f))
                def _():
                    do(forward(c, f))

    lanes = lax.broadcasted_iota(jnp.int32, (ov, tile), 1)
    for f in range(4):
        wanted = jnp.broadcast_to(face_ref[f:f + 1, :].astype(F32), (ov, ov)).T.astype(jnp.int32)
        for b in range(own_blocks):
            hit = wanted == lanes + b * tile
            pick[f * ov:(f + 1) * ov, b * tile:(b + 1) * tile] = jnp.where(hit, 1.0, 0.0).astype(BF16)
    basis = basis_ref[...]
    for f in range(4):
        ext_send[f] = dot_rows(basis, pick[f * ov:(f + 1) * ov, :]).astype(BF16)
    for b in range(own_blocks):
        ext[b] = basis_ref[:, b * tile:(b + 1) * tile]

    for f in range(4):
        @pl.when(jnp.logical_not(arrives[f]))
        def _():
            ext[own_blocks + f] = jnp.zeros((coarse, tile), BF16)
            face_recv[:, f * ov:(f + 1) * ov, :] = jnp.zeros((chunks, ov, width), BF16)

    pl.semaphore_wait(barrier, n_sub - 1 + n_grp - 1)
    for f in range(4):
        @pl.when(sends[f])
        def _():
            ext_copy(f).start()

    def pair_copy(i):
        return remote(pair_send.at[i], pair_recv.at[i], pair_ss.at[i], pair_rs.at[i], (g, partner))

    @pl.loop(0, chunks)
    def _(c):
        load_resid(c).wait()
        face_send[c] = wide_dot(pick[...], resid[c]).astype(BF16)
        for f in range(4):
            face_start(c, f)
        term = wide_dot(basis_ref[...], resid[c])
        for q in range(per_chunk):
            to = c * per_chunk + q
            piece = term[:, q * part:(q + 1) * part]

            @pl.when(lax.rem(to, 2) == core)
            def _():
                keep[to // 2] = piece

            @pl.when(lax.rem(to, 2) != core)
            def _():
                pair_send[to // 2] = piece
                pair_copy(to // 2).start()

    load_tiles.wait()
    for f in range(4):
        @pl.when(arrives[f])
        def _():
            ext_copy(f).wait_recv()

    @pl.loop(0, row_blocks)
    def _(b):
        row = jnp.concatenate([tiles[b, j] for j in range(per_row)], axis=1)
        picked = jnp.concatenate([ext[col_ref[b, j]] for j in range(per_row)], axis=1)
        applied[pl.ds(pl.multiple_of(b * tile, tile), tile), :] = dot_rows(row, picked).astype(BF16)

    gal[coarse:, :] = jnp.zeros((gal.shape[0] - coarse, coarse), F32)
    gal[:coarse, :] = wide_dot(basis_ref[...], applied[...])

    gal_swap = remote(gal, gal_pair, gpair_ss.at[0], gpair_rs.at[0], (g, partner))
    gal_swap.start()
    def rhs_copy(i):
        to = lax.rem(chip + i, chips)
        return remote(rhs_send.at[to], rhs_recv.at[chip], rhs_ss.at[to], rhs_rs.at[chip], (g, to * 2 + core))

    def rhs_from(i):
        frm = lax.rem(chip + i, chips)
        return remote(rhs_send.at[frm], rhs_recv.at[frm], rhs_ss.at[frm], rhs_rs.at[frm], (g, frm * 2 + core))

    @pl.loop(1, chips)
    def _(i):
        to = lax.rem(chip + i, chips)
        pair_copy(to).wait_recv()
        rhs_send[to] = (keep[to] + pair_recv[to]).astype(BF16)
        rhs_copy(i).start()

    pair_copy(chip).wait_recv()
    sum_send[:coarse, :] = keep[chip] + pair_recv[chip]
    if sum_send.shape[0] > coarse:
        sum_send[coarse:, :] = jnp.zeros((sum_send.shape[0] - coarse, part), F32)
    load_inv.wait()

    @pl.loop(0, chunks // 2)
    def _(c):
        total[c] = wide_dot(inv[:, :rows], resid[c])

    def gal_piece(i):
        return pl.ds(pl.multiple_of(i * gal_rows, 8), gal_rows)

    def gal_copy(i):
        to = lax.rem(chip + i, chips)
        piece = gal_both.at[gal_piece(to * 2 + core)]
        return remote(piece, gal_recv.at[chip], gal_ss.at[to], gal_rs.at[chip], (g, to * 2 + core))

    def gal_from(i):
        frm = lax.rem(chip + i, chips)
        piece = gal_both.at[gal_piece(frm * 2 + core)]
        return remote(piece, gal_recv.at[frm], gal_ss.at[frm], gal_rs.at[frm], (g, frm * 2 + core))

    gal_swap.wait_recv()
    gal_both[...] = gal[...] + gal_pair[...]

    @pl.loop(1, chips)
    def _(i):
        gal_copy(i).start()

    gal_sum[...] = gal_both[gal_piece(s), :]

    @pl.loop(chunks // 2, chunks)
    def _(c):
        total[c] = wide_dot(inv[:, :rows], resid[c])

    def finish(c):
        def pass_on(copy):
            remote(relay.at[c], relay.at[c], relay_ss.at[c], relay_rs.at[c], (1, s)).wait_recv()
            copy.start()

        when_relaying(c, pass_on)
        for f in range(4):
            @pl.when(arrives[f])
            def _():
                face_copy(c, f).wait_recv()
        cols = pl.ds(pl.multiple_of(c * width, width), width)
        fix_ref[:, cols] = (total[c] + wide_dot(inv[:, rows:], face_recv[c])).astype(BF16)

    late = chunks - chunks // 4

    @pl.loop(0, late)
    def _(c):
        finish(c)

    def gsum_copy(i):
        to = lax.rem(g + i, n_grp)
        return remote(gal_sum, gal_sum_recv.at[g], gsum_ss.at[to], gsum_rs.at[g], (to, s))

    def gsum_from(i):
        frm = lax.rem(g + i, n_grp)
        return remote(gal_sum, gal_sum_recv.at[frm], gsum_ss.at[frm], gsum_rs.at[frm], (frm, s))

    def sum_piece(i):
        return pl.ds(pl.multiple_of(i * sum_rows, 8), sum_rows)

    def sum_copy(i):
        to = lax.rem(g + i, n_grp)
        return remote(sum_send.at[sum_piece(to)], sum_recv.at[g], sum_ss.at[to], sum_rs.at[g], (to, s))

    def sum_from(i):
        frm = lax.rem(g + i, n_grp)
        return remote(sum_send.at[sum_piece(frm)], sum_recv.at[frm], sum_ss.at[frm], sum_rs.at[frm], (frm, s))

    def last_copy(i):
        to = lax.rem(g + i, n_grp)
        return remote(sum_last, sum_full.at[sum_piece(g)], last_ss.at[to], last_rs.at[g], (to, s))

    def last_from(i):
        frm = lax.rem(g + i, n_grp)
        return remote(sum_last, sum_full.at[sum_piece(frm)], last_ss.at[frm], last_rs.at[frm], (frm, s))

    def glast_copy(i):
        to = lax.rem(s + i, n_sub)
        return remote(gal_last, gal_full.at[gal_piece(s)], glast_ss.at[to], glast_rs.at[s], (g, to))

    def glast_from(i):
        frm = lax.rem(s + i, n_sub)
        return remote(gal_last, gal_full.at[gal_piece(frm)], glast_ss.at[frm], glast_rs.at[frm], (g, frm))

    @pl.loop(1, chips)
    def _(i):
        gal_from(i).wait_recv()
        gal_sum[...] += gal_recv[lax.rem(chip + i, chips)]

    @pl.loop(1, n_grp)
    def _(i):
        gsum_copy(i).start()

    @pl.loop(1, chips)
    def _(i):
        rhs_from(i).wait_recv()
        sum_send[:coarse, :] += rhs_recv[lax.rem(chip + i, chips)].astype(F32)

    @pl.loop(1, n_grp)
    def _(i):
        sum_copy(i).start()

    @pl.loop(late, chunks)
    def _(c):
        finish(c)

    gal_last[...] = gal_sum[...]

    @pl.loop(1, n_grp)
    def _(i):
        gsum_from(i).wait_recv()
        gal_last[...] += gal_sum_recv[lax.rem(g + i, n_grp)]

    gal_last[...] = gal_last[...] * scaling

    @pl.loop(1, n_sub)
    def _(i):
        glast_copy(i).start()

    sum_last[...] = sum_send[sum_piece(g), :]

    @pl.loop(1, n_grp)
    def _(i):
        sum_from(i).wait_recv()
        sum_last[...] += sum_recv[lax.rem(g + i, n_grp)]

    sum_last[...] = sum_last[...] * scaling

    @pl.loop(1, n_grp)
    def _(i):
        last_copy(i).start()

    gal_full[gal_piece(s), :] = gal_last[...]
    sum_full[sum_piece(g), :] = sum_last[...]

    @pl.loop(1, n_sub)
    def _(i):
        glast_from(i).wait_recv()

    gal_ref[...] = gal_full[:coarse, :]

    @pl.loop(1, n_grp)
    def _(i):
        last_from(i).wait_recv()

    rhs_ref[...] = sum_full[:coarse, :]

    for f in range(4):
        @pl.when(sends[f])
        def _():
            ext_copy(f).wait_send()

            @pl.loop(0, chunks)
            def _(c):
                face_copy(c, f).wait_send()

    @pl.loop(0, chunks)
    def _(c):
        when_relaying(c, lambda copy: copy.wait_send())

    gal_swap.wait_send()

    @pl.loop(0, chips)
    def _(i):
        pair_copy(i).wait_send()

    @pl.loop(1, chips)
    def _(i):
        rhs_copy(i).wait_send()
        gal_copy(i).wait_send()

    @pl.loop(1, n_sub)
    def _(i):
        glast_copy(i).wait_send()

    @pl.loop(1, n_grp)
    def _(i):
        gsum_copy(i).wait_send()
        sum_copy(i).wait_send()
        last_copy(i).wait_send()


def local_any(n_grp, n_sub, residual, inverse_blocks, operator_tiles, column_blocks, coarse_basis, face_rows):
    resid = residual[0, 0]
    inv = inverse_blocks[0, 0]
    tiles = operator_tiles[0, 0]
    basis = jnp.swapaxes(coarse_basis[0, 0], 0, 1)
    faces = face_rows[0, 0]
    rows, k = resid.shape
    coarse = basis.shape[0]
    ov = faces.shape[1]
    tile = tiles.shape[-1]
    ext_blocks = inv.shape[1] // tile
    part = k // n_sub
    width = max(512, part)
    chunks = k // width
    gal_rows = -(-coarse // (8 * n_sub)) * 8
    sum_rows = -(-coarse // (8 * n_grp)) * 8
    chips = n_sub // 2
    scaling = 1.0 / math.sqrt(rows * n_grp * n_sub)
    dma = pltpu.SemaphoreType.DMA
    hbm = pl.BlockSpec(memory_space=pl.ANY)
    vmem = pl.BlockSpec(memory_space=pltpu.VMEM)
    fix, gal, rhs = pl.pallas_call(
        functools.partial(any_kernel, n_grp, n_sub, width, scaling),
        out_shape=(
            pltpu.VMEM((rows, k), BF16),
            pltpu.VMEM((coarse, coarse), F32),
            pltpu.VMEM((coarse, part), F32),
        ),
        in_specs=[pl.BlockSpec(memory_space=pltpu.SMEM), vmem, vmem, hbm, hbm, hbm],
        out_specs=(vmem, vmem, vmem),
        scratch_shapes=[
            pltpu.VMEM((chunks, rows, width), BF16),
            pltpu.VMEM(inv.shape, BF16),
            pltpu.VMEM(tiles.shape, BF16),
            pltpu.VMEM((4 * ov, rows), BF16),
            pltpu.VMEM((4, coarse, tile), BF16),
            pltpu.VMEM((ext_blocks, coarse, tile), BF16),
            pltpu.VMEM((chunks, 4 * ov, width), BF16),
            pltpu.VMEM((chunks, 4 * ov, width), BF16),
            pltpu.VMEM((chunks, ov, width), BF16),
            pltpu.VMEM((chunks, rows, width), F32),
            pltpu.VMEM((chips, coarse, part), F32),
            pltpu.VMEM((chips, coarse, part), F32),
            pltpu.VMEM((chips, coarse, part), F32),
            pltpu.VMEM((chips, coarse, part), BF16),
            pltpu.VMEM((chips, coarse, part), BF16),
            pltpu.VMEM((n_grp * sum_rows, part), F32),
            pltpu.VMEM((n_grp, sum_rows, part), F32),
            pltpu.VMEM((sum_rows, part), F32),
            pltpu.VMEM((n_grp * sum_rows, part), F32),
            pltpu.VMEM((rows, coarse), BF16),
            pltpu.VMEM((n_sub * gal_rows, coarse), F32),
            pltpu.VMEM((n_sub * gal_rows, coarse), F32),
            pltpu.VMEM((n_sub * gal_rows, coarse), F32),
            pltpu.VMEM((chips, gal_rows, coarse), F32),
            pltpu.VMEM((gal_rows, coarse), F32),
            pltpu.VMEM((n_grp, gal_rows, coarse), F32),
            pltpu.VMEM((gal_rows, coarse), F32),
            pltpu.VMEM((n_sub * gal_rows, coarse), F32),
            dma((2,)),
            dma((chunks,)),
            dma((4,)),
            dma((4,)),
            dma((chunks, 4)),
            dma((chunks, 4)),
            dma((chunks,)),
            dma((chunks,)),
            dma((chips,)),
            dma((chips,)),
            dma((1,)),
            dma((1,)),
            dma((chips,)),
            dma((chips,)),
            dma((n_grp,)),
            dma((n_grp,)),
            dma((n_grp,)),
            dma((n_grp,)),
            dma((chips,)),
            dma((chips,)),
            dma((n_grp,)),
            dma((n_grp,)),
            dma((n_sub,)),
            dma((n_sub,)),
        ],
        compiler_params=pltpu.CompilerParams(
            collective_id=0, has_side_effects=True, vmem_limit_bytes=55 * 1024 * 1024
        ),
    )(column_blocks[0, 0], faces, basis, resid, inv, tiles)
    return fix[None, None], gal, rhs


def plane_kernel(
    n_sub, scaling, relayed, last,
    col_hbm, face_hbm, basis_hbm, resid_hbm, inv_hbm, tiles_hbm,
    done_ref, last_ref, face_recv, inv, gal_ref, rhs_ref,
    col_ref, face_ref, basis_ref, resid, tiles, left, ext_send, ext, face_send, relay, total,
    keep, pair_send, pair_recv, y_keep, y_send, y_recv, z_send, z_recv, mine, cross_send, cross_recv,
    applied, gal, gal_pair, gal_both, gal_send, gal_recv, gal_sum, gal_other, gal_last, gal_full, gal_half,
    in_sem, resid_sem, ext_ss, ext_rs, face_ss, face_rs, relay_ss, relay_rs,
    pair_ss, pair_rs, y_ss, y_rs, z_ss, z_rs, token_sem, swap_ss, swap_rs, cross_ss, cross_rs, gal_ss, gal_rs, glast_ss, glast_rs,
):
    g = lax.axis_index("grp")
    s = lax.axis_index("sub")
    n_grp = 4
    gx, gy = lax.rem(g, 2), g // 2
    chip, core = s // 2, lax.rem(s, 2)
    beside = g + 1 - 2 * gx
    above = lax.rem(g + 2, 4)
    x_near, y_near, pair = (beside, s), (above, s), (g, s + 1 - 2 * core)
    chips = n_sub // 2
    chunks, rows, width = resid.shape
    coarse = basis_ref.shape[0]
    row_blocks, per_row, tile = tiles.shape[:3]
    own_blocks = rows // tile
    ov = face_ref.shape[1]
    faces = 4 * ov
    part = width // 2
    half = part // 2
    pieces = 2 * chips
    piece_rows = gal_sum.shape[0]
    me = chip * 2 + gy

    def load_resid(c):
        cols = pl.ds(pl.multiple_of(c * width, width), width)
        return pltpu.make_async_copy(resid_hbm.at[:, cols], resid.at[c], resid_sem.at[c])

    load_tiles = pltpu.make_async_copy(tiles_hbm, tiles, in_sem.at[0])
    load_inv = pltpu.make_async_copy(inv_hbm, inv, in_sem.at[1])
    load_faces = pltpu.make_async_copy(face_hbm, face_ref, in_sem.at[2])
    load_basis = pltpu.make_async_copy(basis_hbm, basis_ref, in_sem.at[3])
    load_col = pltpu.make_async_copy(col_hbm, col_ref, in_sem.at[4])

    for load in (load_faces, load_basis, load_resid(0), load_col, load_resid(1)):
        load.start()

    barrier = pltpu.get_barrier_semaphore()

    def greet(device):
        pl.semaphore_signal(barrier, inc=1, device_id=device, device_id_type=MESH)

    across = s - 1 + 2 * core
    below, over = chip > 0, chip < chips - 1
    faces_across = jnp.logical_and(across >= 0, across < n_sub)
    middle = jnp.logical_and(g > 0, g < n_grp - 1)
    for device in (x_near, y_near, pair):
        greet(device)
    for exists, device in (
        (middle, (n_grp - 1 - g, s)), (faces_across, (g, across)), (below, (g, s - 2)), (over, (g, s + 2)),
    ):
        @pl.when(exists)
        def _():
            greet(device)

    def count(*conditions):
        return sum(jnp.where(condition, 1, 0) for condition in conditions)

    def tell(i, device):
        pl.semaphore_signal(token_sem.at[i], inc=1, device_id=device, device_id_type=MESH)

    def met():
        pl.semaphore_wait(barrier, 3 + count(middle, faces_across, below, over))
        tell(0, y_near)
        for exists, device in ((below, (g, s - 2)), (over, (g, s + 2))):
            @pl.when(exists)
            def _():
                tell(0, device)

    def met_further():
        pl.semaphore_wait(token_sem.at[0], 1 + count(below, over))
        tell(1, (g, lax.rem(s + n_sub // 2, n_sub)))

    def met_all():
        pl.semaphore_wait(token_sem.at[1], 1)

    targets = ((g + 1, s), (g - 1, s), (g, s + 1), (g, s - 1))
    sends = (g < n_grp - 1, g > 0, s < n_sub - 1, s > 0)
    arrives = (g > 0, g < n_grp - 1, s > 0, s < n_sub - 1)

    def remote(src, dst, send_sem, recv_sem, device):
        return pltpu.make_async_remote_copy(
            src_ref=src, dst_ref=dst, send_sem=send_sem, recv_sem=recv_sem,
            device_id=device, device_id_type=MESH,
        )

    def ext_copy(f):
        return remote(ext_send.at[f], ext.at[own_blocks + f], ext_ss.at[f], ext_rs.at[f], targets[f])

    def face_copy(c, f):
        span = pl.ds(f * ov, ov)
        return remote(face_send.at[c, span], face_recv.at[c, span], face_ss.at[c, f], face_rs.at[c, f], targets[f])

    first = chunks - relayed

    def relay_in(c, f):
        slot = c - first
        return remote(face_send.at[c, pl.ds(f * ov, ov)], relay.at[slot], face_ss.at[c, f], relay_rs.at[slot], y_near)

    def relay_out(c, f):
        slot, span = c - first, pl.ds(f * ov, ov)
        return remote(relay.at[slot], face_recv.at[c, span], relay_ss.at[slot], face_rs.at[c, f], x_near)

    def when_relaying(do):
        for f, at in ((0, n_grp - 1), (1, 0)):
            @pl.when(g == at)
            def _():
                do(f)

    def near(c):
        for f in range(2):
            @pl.when(jnp.logical_and(sends[f], g != 1 + f))
            def _():
                face_copy(c, f).start()

    def diagonal(c):
        for f in range(2):
            @pl.when(g == 1 + f)
            def _():
                (face_copy if c < first else relay_in)(c, f).start()

    def side(c):
        for f in range(2, 4):
            @pl.when(sends[f])
            def _():
                face_copy(c, f).start()

    load_faces.wait()
    lanes = lax.broadcasted_iota(jnp.int32, (ov, tile), 1)
    for f in range(4):
        wanted = jnp.broadcast_to(face_ref[f:f + 1, :].astype(F32), (ov, ov)).T.astype(jnp.int32)
        for b in range(own_blocks):
            hit = wanted == lanes + b * tile
            left[f * ov:(f + 1) * ov, b * tile:(b + 1) * tile] = jnp.where(hit, 1.0, 0.0).astype(BF16)
    load_basis.wait()
    basis = basis_ref[...]
    left[faces:faces + coarse, :] = basis
    if left.shape[0] > faces + coarse:
        left[faces + coarse:, :] = jnp.zeros((left.shape[0] - faces - coarse, rows), BF16)
    for f in range(4):
        ext_send[f] = dot_rows(basis, left[f * ov:(f + 1) * ov, :]).astype(BF16)

    met()
    for f in range(4):
        @pl.when(sends[f])
        def _():
            ext_copy(f).start()

    def pair_copy(c):
        return remote(pair_send.at[c], pair_recv.at[c], pair_ss.at[c], pair_rs.at[c], pair)

    def y_copy(c):
        return remote(y_send.at[c], y_recv.at[c], y_ss.at[c], y_rs.at[c], y_near)

    def columns(i):
        return pl.ds(pl.multiple_of(i * half, half), half)

    def pass_half(c):
        pair_copy(c).wait_recv()
        y_send[c] = (keep[c, :, columns(1 - gy)] + pair_recv[c, :, columns(1 - gy)]).astype(BF16)
        y_copy(c).start()
        y_keep[c] = keep[c, :, columns(gy)] + pair_recv[c, :, columns(gy)]

    def select(c):
        load_resid(c).wait()
        if c == 0:
            for later in range(2, chunks):
                load_resid(later).start()
            load_tiles.start()
        if c == 1:
            load_inv.start()
        both = wide_dot(left[...], resid[c])
        face_send[c] = both[:faces].astype(BF16)
        for q in range(2):
            @pl.when(core == q)
            def _():
                keep[c] = both[faces:faces + coarse, q * part:(q + 1) * part]
                pair_send[c] = both[faces:faces + coarse, (1 - q) * part:(2 - q) * part]

        pair_copy(c).start()

    def fill():
        for f in range(4):
            @pl.when(jnp.logical_not(arrives[f]))
            def _():
                ext[own_blocks + f] = jnp.zeros((coarse, tile), BF16)
                face_recv[:, f * ov:(f + 1) * ov, :] = jnp.zeros((chunks, ov, width), BF16)
        for b in range(own_blocks):
            ext[b] = basis_ref[:, b * tile:(b + 1) * tile]

    wide = gal.shape[2]
    gal_swap = remote(gal.at[1 - core], gal_pair, swap_ss.at[0], swap_rs.at[0], pair)

    def assemble():
        load_tiles.wait()
        load_col.wait()
        for f in range(4):
            @pl.when(arrives[f])
            def _():
                ext_copy(f).wait_recv()

        for b in range(row_blocks):
            row = jnp.concatenate([tiles[b, j] for j in range(per_row)], axis=1)
            picked = jnp.concatenate([ext[col_ref[b, j]] for j in range(per_row)], axis=1)
            applied[:, b * tile:(b + 1) * tile] = dot_rows(picked, row).astype(BF16)

        whole = dot_rows(basis_ref[...], applied[...])
        gal[0, :coarse, :] = whole[:, :wide]
        gal[0, coarse:, :] = jnp.zeros((gal.shape[1] - coarse, wide), F32)
        gal[1] = jnp.zeros(gal.shape[1:], F32)
        gal[1, :coarse, :coarse - wide] = whole[:, wide:]
        gal_swap.start()

    def slot_of(c):
        return c - 1 if c > last else c

    def multiply(c):
        if c == 1:
            load_inv.wait()
        (last_ref if c == last else total.at[slot_of(c)])[...] = wide_dot(inv[:, :rows], resid[c])

    def z_copy(c):
        return remote(z_send.at[c], z_recv.at[chip], z_ss.at[c], z_rs.at[chip], (g, c * 2 + core))

    def z_from(i):
        frm = lax.rem(chip + i, chips)
        return remote(z_send.at[frm], z_recv.at[frm], z_ss.at[frm], z_rs.at[frm], (g, frm * 2 + core))

    def pass_quarter(c):
        y_copy(c).wait_recv()
        joined = y_keep[c] + y_recv[c].astype(F32)

        @pl.when(chip == c)
        def _():
            mine[...] = joined

        @pl.when(chip != c)
        def _():
            z_send[c] = joined.astype(BF16)
            z_copy(c).start()

    def rows_of(i):
        return pl.ds(pl.multiple_of(i * piece_rows, piece_rows), piece_rows)

    def holder(i):
        return (lax.rem(i, 2) * 2 + gx, (i // 2) * 2 + core)

    def gal_copy(i):
        to = lax.rem(me + i, pieces)
        return remote(gal_send.at[rows_of(to)], gal_recv.at[me], gal_ss.at[to], gal_rs.at[me], holder(to))

    def gal_from(i):
        frm = lax.rem(me + i, pieces)
        return remote(gal_send.at[rows_of(frm)], gal_recv.at[frm], gal_ss.at[frm], gal_rs.at[frm], holder(frm))

    def gal_spread():
        gal_swap.wait_recv()
        gal_both[...] = gal[core] + gal_pair[...]
        gal_send[...] = gal_both[...].astype(BF16)

        @pl.loop(1, pieces)
        def _(i):
            gal_copy(i).start()

    def relay_on(c):
        def do(f):
            slot = c - first
            remote(relay.at[slot], relay.at[slot], relay_ss.at[slot], relay_rs.at[slot], y_near).wait_recv()
            relay_out(c, f).start()

        when_relaying(do)

    gal_cross = remote(gal_sum, gal_other, swap_ss.at[1], swap_rs.at[1], x_near)

    def gal_gather():
        gal_sum[...] = gal_both[rows_of(me), :]

        @pl.loop(1, pieces)
        def _(i):
            gal_from(i).wait_recv()
            gal_sum[...] += gal_recv[lax.rem(me + i, pieces)].astype(F32)

        gal_cross.start()

    def cross_copy(i):
        to = lax.rem(g + i, n_grp)
        return remote(cross_send, cross_recv.at[g], cross_ss.at[to], cross_rs.at[g], (to, s))

    def cross_from(i):
        frm = lax.rem(g + i, n_grp)
        return remote(cross_send, cross_recv.at[frm], cross_ss.at[frm], cross_rs.at[frm], (frm, s))

    def cross():
        @pl.loop(1, chips)
        def _(i):
            z_from(i).wait_recv()
            mine[...] += z_recv[lax.rem(chip + i, chips)].astype(F32)

        cross_send[...] = mine[...].astype(BF16)

        @pl.loop(1, n_grp)
        def _(i):
            cross_copy(i).start()

    def glast_copy(i):
        to = lax.rem(me + i, pieces)
        return remote(gal_last, gal_full.at[rows_of(me)], glast_ss.at[to], glast_rs.at[me], holder(to))

    def glast_from(i):
        frm = lax.rem(me + i, pieces)
        return remote(gal_last, gal_full.at[rows_of(frm)], glast_ss.at[frm], glast_rs.at[frm], holder(frm))

    def await_faces(c, which):
        for f in which:
            @pl.when(arrives[f])
            def _():
                face_copy(c, f).wait_recv()

    def finish(c):
        await_faces(c, range(4))
        if c != last:
            margin = wide_dot(inv[:, rows:], face_recv[c])
            done_ref[slot_of(c)] = (total[slot_of(c)] + margin).astype(BF16)

    def gal_return():
        gal_cross.wait_recv()
        gal_last[...] = (gal_sum[...] + gal_other[...]) * scaling

        @pl.loop(1, pieces)
        def _(i):
            glast_copy(i).start()

        gal_full[rows_of(me), :] = gal_last[...]

    gal_last_swap = remote(gal_full, gal_half, swap_ss.at[2], swap_rs.at[2], pair)

    def gal_share():
        @pl.loop(1, pieces)
        def _(i):
            glast_from(i).wait_recv()

        gal_last_swap.start()

    def gal_end():
        gal_last_swap.wait_recv()
        for q in range(2):
            @pl.when(core == q)
            def _():
                low, high = (gal_full, gal_half) if q == 0 else (gal_half, gal_full)
                gal_ref[:, :wide] = low[:coarse, :]
                gal_ref[:, wide:] = high[:coarse, :coarse - wide]

    def rhs_end():
        @pl.loop(1, n_grp)
        def _(i):
            cross_from(i).wait_recv()

        ours = cross_send[...].astype(F32) + cross_recv[beside].astype(F32)
        theirs = cross_recv[above].astype(F32) + cross_recv[n_grp - 1 - g].astype(F32)
        rhs_ref[:, columns(gy)] = ours * scaling
        rhs_ref[:, columns(1 - gy)] = theirs * scaling

    select(0)
    near(0)
    fill()
    select(1)
    side(0)
    met_further()
    pass_half(0)
    select(2)
    diagonal(2)
    side(2)
    near(1)
    assemble()
    near(2)
    diagonal(0)
    side(1)
    met_all()
    gal_spread()
    pass_half(2)
    pass_half(1)
    select(3)
    multiply(1)
    pass_half(3)
    relay_on(2)
    pass_quarter(0)
    diagonal(3)
    multiply(3)
    side(3)
    multiply(2)
    gal_gather()
    pass_quarter(3)
    pass_quarter(1)
    near(3)
    pass_quarter(2)
    relay_on(3)
    diagonal(1)
    gal_return()
    multiply(0)
    cross()
    finish(0)
    finish(3)
    gal_share()
    finish(2)
    finish(1)
    gal_end()
    rhs_end()
    for f in range(4):
        @pl.when(sends[f])
        def _():
            ext_copy(f).wait_send()

            @pl.loop(0, chunks)
            def _(c):
                face_copy(c, f).wait_send()

    def sent_on(f):
        @pl.loop(first, chunks)
        def _(c):
            relay_out(c, f).wait_send()

    when_relaying(sent_on)

    @pl.loop(0, chunks)
    def _(c):
        pair_copy(c).wait_send()
        y_copy(c).wait_send()

        @pl.when(c != chip)
        def _():
            z_copy(c).wait_send()

    @pl.loop(1, pieces)
    def _(i):
        gal_copy(i).wait_send()
        glast_copy(i).wait_send()

    @pl.loop(1, n_grp)
    def _(i):
        cross_copy(i).wait_send()

    for copy in (gal_swap, gal_cross, gal_last_swap):
        copy.wait_send()


def store_kernel(last, done, total, faces, inv, gal, rhs, fix_hbm, gal_hbm, rhs_hbm, ends, sems):
    others, rows, width = done.shape
    chunks = others + 1
    halves, _, half = ends.shape

    def columns(start, size):
        return fix_hbm.at[:, pl.ds(start, size)]

    copies = [
        pltpu.make_async_copy(done.at[i], columns((i + (i >= last)) * width, width), sems.at[i]) for i in range(others)
    ]
    copies.append(pltpu.make_async_copy(gal, gal_hbm, sems.at[others]))
    copies.append(pltpu.make_async_copy(rhs, rhs_hbm, sems.at[others + 1]))
    for copy in copies:
        copy.start()
    for h in range(halves):
        span = slice(h * half, (h + 1) * half)
        margin = wide_dot(inv[:, rows:], faces[last, :, span])
        ends[h] = (total[:, span] + margin).astype(BF16)
        copy = pltpu.make_async_copy(ends.at[h], columns(last * width + h * half, half), sems.at[chunks + 1 + h])
        copy.start()
        copies.append(copy)
    for copy in copies:
        copy.wait()


def fits_plane(mesh):
    return mesh.shape["grp"] == 4 and mesh.shape["sub"] == 8


def local_plane(n_grp, n_sub, residual, inverse_blocks, operator_tiles, column_blocks, coarse_basis, face_rows):
    resid = residual[0, 0]
    inv = inverse_blocks[0, 0]
    tiles = operator_tiles[0, 0]
    basis = jnp.swapaxes(coarse_basis[0, 0], 0, 1)
    faces = face_rows[0, 0]
    rows, k = resid.shape
    coarse = basis.shape[0]
    ov = faces.shape[1]
    tile = tiles.shape[-1]
    ext_blocks = inv.shape[1] // tile
    part = k // n_sub
    half = part // 2
    width = 2 * part
    chunks = chips = n_sub // 2
    relayed = chunks // 2
    pieces = 2 * chips
    piece_rows = -(-coarse // (16 * pieces)) * 16
    wide = -(-coarse // 256) * 128
    scaling = 1.0 / math.sqrt(rows * n_grp * n_sub)
    dma = pltpu.SemaphoreType.DMA
    hbm = pl.BlockSpec(memory_space=pl.ANY)
    vmem = pl.BlockSpec(memory_space=pltpu.VMEM)
    left_rows = -(-(4 * ov + coarse) // 16) * 16
    last = 1
    kept = pl.pallas_call(
        functools.partial(plane_kernel, n_sub, scaling, relayed, last),
        out_shape=(
            pltpu.VMEM((chunks - 1, rows, width), BF16),
            pltpu.VMEM((rows, width), F32),
            pltpu.VMEM((chunks, 4 * ov, width), BF16),
            pltpu.VMEM(inv.shape, BF16),
            pltpu.VMEM((coarse, coarse), F32),
            pltpu.VMEM((coarse, part), F32),
        ),
        in_specs=[hbm] * 6,
        out_specs=(vmem,) * 6,
        scratch_shapes=[
            pltpu.SMEM(column_blocks.shape[2:], jnp.int32),
            pltpu.VMEM(faces.shape, jnp.int32),
            pltpu.VMEM(basis.shape, BF16),
            pltpu.VMEM((chunks, rows, width), BF16),
            pltpu.VMEM(tiles.shape, BF16),
            pltpu.VMEM((left_rows, rows), BF16),
            pltpu.VMEM((4, coarse, tile), BF16),
            pltpu.VMEM((ext_blocks, coarse, tile), BF16),
            pltpu.VMEM((chunks, 4 * ov, width), BF16),
            pltpu.VMEM((relayed, ov, width), BF16),
            pltpu.VMEM((chunks - 1, rows, width), F32),
            pltpu.VMEM((chips, coarse, part), F32),
            pltpu.VMEM((chips, coarse, part), F32),
            pltpu.VMEM((chips, coarse, part), F32),
            pltpu.VMEM((chips, coarse, half), F32),
            pltpu.VMEM((chips, coarse, half), BF16),
            pltpu.VMEM((chips, coarse, half), BF16),
            pltpu.VMEM((chips, coarse, half), BF16),
            pltpu.VMEM((chips, coarse, half), BF16),
            pltpu.VMEM((coarse, half), F32),
            pltpu.VMEM((coarse, half), BF16),
            pltpu.VMEM((n_grp, coarse, half), BF16),
            pltpu.VMEM((coarse, rows), BF16),
            pltpu.VMEM((2, pieces * piece_rows, wide), F32),
            pltpu.VMEM((pieces * piece_rows, wide), F32),
            pltpu.VMEM((pieces * piece_rows, wide), F32),
            pltpu.VMEM((pieces * piece_rows, wide), BF16),
            pltpu.VMEM((pieces, piece_rows, wide), BF16),
            pltpu.VMEM((piece_rows, wide), F32),
            pltpu.VMEM((piece_rows, wide), F32),
            pltpu.VMEM((piece_rows, wide), F32),
            pltpu.VMEM((pieces * piece_rows, wide), F32),
            pltpu.VMEM((pieces * piece_rows, wide), F32),
            dma((5,)),
            dma((chunks,)),
            dma((4,)),
            dma((4,)),
            dma((chunks, 4)),
            dma((chunks, 4)),
            dma((relayed,)),
            dma((relayed,)),
            dma((chips,)),
            dma((chips,)),
            dma((chips,)),
            dma((chips,)),
            dma((chips,)),
            dma((chips,)),
            pltpu.SemaphoreType.REGULAR((2,)),
            dma((3,)),
            dma((3,)),
            dma((n_grp,)),
            dma((n_grp,)),
            dma((pieces,)),
            dma((pieces,)),
            dma((pieces,)),
            dma((pieces,)),
        ],
        compiler_params=pltpu.CompilerParams(
            collective_id=0, has_side_effects=True, vmem_limit_bytes=50 * 1024 * 1024
        ),
    )(column_blocks[0, 0], faces, basis, resid, inv, tiles)
    fix, gal, rhs = pl.pallas_call(
        functools.partial(store_kernel, last),
        out_shape=(
            jax.ShapeDtypeStruct((rows, k), BF16),
            jax.ShapeDtypeStruct((coarse, coarse), F32),
            jax.ShapeDtypeStruct((coarse, part), F32),
        ),
        in_specs=[vmem] * 6,
        out_specs=(hbm, hbm, hbm),
        scratch_shapes=[pltpu.VMEM((2, rows, width // 2), BF16), dma((chunks + 3,))],
        compiler_params=pltpu.CompilerParams(vmem_limit_bytes=16 * 1024 * 1024),
    )(*(pltpu.with_memory_space_constraint(x, pltpu.VMEM) for x in kept))
    return fix[None, None], gal, rhs


def solution(mesh):
    body = local_plane if fits_plane(mesh) else local_any
    return jax.shard_map(
        functools.partial(body, mesh.shape["grp"], mesh.shape["sub"]),
        mesh=mesh,
        in_specs=(
            P("grp", "sub", None, None),
            P("grp", "sub", None, None),
            P("grp", "sub", None, None, None, None),
            P("grp", "sub", None, None),
            P("grp", "sub", None, None),
            P("grp", "sub", None, None),
        ),
        out_specs=(P("grp", "sub", None, None), P(), P(None, "sub")),
        check_vma=False,
    )
```

```python
import functools
import math

import jax
import jax.numpy as jnp
from jax import lax
from jax.experimental import pallas as pl
from jax.experimental.pallas import tpu as pltpu
from jax.sharding import PartitionSpec as P

MESH = pl.DeviceIdType.MESH
F32 = jnp.float32
BF16 = jnp.bfloat16


def wide_dot(a, b):
    return jnp.dot(a, b, preferred_element_type=F32)


def dot_rows(a, b):
    return lax.dot_general(a, b, (((1,), (1,)), ((), ())), preferred_element_type=F32)


def any_kernel(
    n_grp, n_sub, width, scaling,
    col_ref, face_ref, basis_ref, resid_hbm, inv_hbm, tiles_hbm,
    fix_ref, gal_ref, rhs_ref,
    resid, inv, tiles, pick, ext_send, ext, face_send, face_recv, relay, total,
    keep, pair_send, pair_recv, rhs_send, rhs_recv, sum_send, sum_recv, sum_last, sum_full,
    applied, gal, gal_pair, gal_both, gal_recv, gal_sum, gal_sum_recv, gal_last, gal_full,
    in_sem, resid_sem, ext_ss, ext_rs, face_ss, face_rs, relay_ss, relay_rs,
    pair_ss, pair_rs, gpair_ss, gpair_rs, rhs_ss, rhs_rs,
    sum_ss, sum_rs, last_ss, last_rs, gal_ss, gal_rs, gsum_ss, gsum_rs, glast_ss, glast_rs,
):
    g = lax.axis_index("grp")
    s = lax.axis_index("sub")
    chip, core = s // 2, lax.rem(s, 2)
    partner = s + 1 - 2 * core
    chips = n_sub // 2
    chunks, rows, _ = resid.shape
    coarse = basis_ref.shape[0]
    row_blocks, per_row, tile = tiles.shape[:3]
    own_blocks = rows // tile
    ov = face_ref.shape[1]
    part = chunks * width // n_sub
    per_chunk = width // part
    gal_rows = gal_recv.shape[1]
    sum_rows = sum_recv.shape[1]
    relayed = n_grp == 4

    def load_resid(c):
        cols = pl.ds(pl.multiple_of(c * width, width), width)
        return pltpu.make_async_copy(resid_hbm.at[:, cols], resid.at[c], resid_sem.at[c])

    load_tiles = pltpu.make_async_copy(tiles_hbm, tiles, in_sem.at[0])
    load_inv = pltpu.make_async_copy(inv_hbm, inv, in_sem.at[1])

    @pl.loop(0, chunks)
    def _(c):
        load_resid(c).start()

    load_tiles.start()
    load_inv.start()

    barrier = pltpu.get_barrier_semaphore()

    @pl.loop(1, n_sub)
    def _(i):
        pl.semaphore_signal(barrier, inc=1, device_id=(g, lax.rem(s + i, n_sub)), device_id_type=MESH)

    @pl.loop(1, n_grp)
    def _(i):
        pl.semaphore_signal(barrier, inc=1, device_id=(lax.rem(g + i, n_grp), s), device_id_type=MESH)

    targets = ((g + 1, s), (g - 1, s), (g, s + 1), (g, s - 1))
    sends = (g < n_grp - 1, g > 0, s < n_sub - 1, s > 0)
    arrives = (g > 0, g < n_grp - 1, s > 0, s < n_sub - 1)

    def remote(src, dst, send_sem, recv_sem, device):
        return pltpu.make_async_remote_copy(
            src_ref=src, dst_ref=dst, send_sem=send_sem, recv_sem=recv_sem,
            device_id=device, device_id_type=MESH,
        )

    def ext_copy(f):
        return remote(ext_send.at[f], ext.at[own_blocks + f], ext_ss.at[f], ext_rs.at[f], targets[f])

    def face_copy(c, f, far=False):
        span = pl.ds(f * ov, ov)
        if far:
            way = (n_grp - 1) * (lax.rem(c + f, 2))
            return remote(face_send.at[c, span], relay.at[c], face_ss.at[c, f], relay_rs.at[c], (way, s))
        return remote(face_send.at[c, span], face_recv.at[c, span], face_ss.at[c, f], face_rs.at[c, f], targets[f])

    def forward(c, f):
        span = pl.ds(f * ov, ov)
        return remote(relay.at[c], face_recv.at[c, span], relay_ss.at[c], face_rs.at[c, f], (2 - f, s))

    def far_face(f):
        return (g == 1 + f) if relayed and f < 2 else None

    def face_start(c, f):
        far = far_face(f)
        if far is None:
            @pl.when(sends[f])
            def _():
                face_copy(c, f).start()
        else:
            @pl.when(far)
            def _():
                face_copy(c, f, True).start()

            @pl.when(jnp.logical_and(sends[f], jnp.logical_not(far)))
            def _():
                face_copy(c, f).start()

    def when_relaying(c, do):
        if relayed:
            turn = lax.rem(c + jnp.where(g == 3, 1, 0), 2)
            for f in range(2):
                @pl.when(jnp.logical_and(jnp.logical_or(g == 0, g == 3), turn == f))
                def _():
                    do(forward(c, f))

    lanes = lax.broadcasted_iota(jnp.int32, (ov, tile), 1)
    for f in range(4):
        wanted = jnp.broadcast_to(face_ref[f:f + 1, :].astype(F32), (ov, ov)).T.astype(jnp.int32)
        for b in range(own_blocks):
            hit = wanted == lanes + b * tile
            pick[f * ov:(f + 1) * ov, b * tile:(b + 1) * tile] = jnp.where(hit, 1.0, 0.0).astype(BF16)
    basis = basis_ref[...]
    for f in range(4):
        ext_send[f] = dot_rows(basis, pick[f * ov:(f + 1) * ov, :]).astype(BF16)
    for b in range(own_blocks):
        ext[b] = basis_ref[:, b * tile:(b + 1) * tile]

    for f in range(4):
        @pl.when(jnp.logical_not(arrives[f]))
        def _():
            ext[own_blocks + f] = jnp.zeros((coarse, tile), BF16)
            face_recv[:, f * ov:(f + 1) * ov, :] = jnp.zeros((chunks, ov, width), BF16)

    pl.semaphore_wait(barrier, n_sub - 1 + n_grp - 1)
    for f in range(4):
        @pl.when(sends[f])
        def _():
            ext_copy(f).start()

    def pair_copy(i):
        return remote(pair_send.at[i], pair_recv.at[i], pair_ss.at[i], pair_rs.at[i], (g, partner))

    @pl.loop(0, chunks)
    def _(c):
        load_resid(c).wait()
        face_send[c] = wide_dot(pick[...], resid[c]).astype(BF16)
        for f in range(4):
            face_start(c, f)
        term = wide_dot(basis_ref[...], resid[c])
        for q in range(per_chunk):
            to = c * per_chunk + q
            piece = term[:, q * part:(q + 1) * part]

            @pl.when(lax.rem(to, 2) == core)
            def _():
                keep[to // 2] = piece

            @pl.when(lax.rem(to, 2) != core)
            def _():
                pair_send[to // 2] = piece
                pair_copy(to // 2).start()

    load_tiles.wait()
    for f in range(4):
        @pl.when(arrives[f])
        def _():
            ext_copy(f).wait_recv()

    @pl.loop(0, row_blocks)
    def _(b):
        row = jnp.concatenate([tiles[b, j] for j in range(per_row)], axis=1)
        picked = jnp.concatenate([ext[col_ref[b, j]] for j in range(per_row)], axis=1)
        applied[pl.ds(pl.multiple_of(b * tile, tile), tile), :] = dot_rows(row, picked).astype(BF16)

    gal[coarse:, :] = jnp.zeros((gal.shape[0] - coarse, coarse), F32)
    gal[:coarse, :] = wide_dot(basis_ref[...], applied[...])

    gal_swap = remote(gal, gal_pair, gpair_ss.at[0], gpair_rs.at[0], (g, partner))
    gal_swap.start()
    def rhs_copy(i):
        to = lax.rem(chip + i, chips)
        return remote(rhs_send.at[to], rhs_recv.at[chip], rhs_ss.at[to], rhs_rs.at[chip], (g, to * 2 + core))

    def rhs_from(i):
        frm = lax.rem(chip + i, chips)
        return remote(rhs_send.at[frm], rhs_recv.at[frm], rhs_ss.at[frm], rhs_rs.at[frm], (g, frm * 2 + core))

    @pl.loop(1, chips)
    def _(i):
        to = lax.rem(chip + i, chips)
        pair_copy(to).wait_recv()
        rhs_send[to] = (keep[to] + pair_recv[to]).astype(BF16)
        rhs_copy(i).start()

    pair_copy(chip).wait_recv()
    sum_send[:coarse, :] = keep[chip] + pair_recv[chip]
    if sum_send.shape[0] > coarse:
        sum_send[coarse:, :] = jnp.zeros((sum_send.shape[0] - coarse, part), F32)
    load_inv.wait()

    @pl.loop(0, chunks // 2)
    def _(c):
        total[c] = wide_dot(inv[:, :rows], resid[c])

    def gal_piece(i):
        return pl.ds(pl.multiple_of(i * gal_rows, 8), gal_rows)

    def gal_copy(i):
        to = lax.rem(chip + i, chips)
        piece = gal_both.at[gal_piece(to * 2 + core)]
        return remote(piece, gal_recv.at[chip], gal_ss.at[to], gal_rs.at[chip], (g, to * 2 + core))

    def gal_from(i):
        frm = lax.rem(chip + i, chips)
        piece = gal_both.at[gal_piece(frm * 2 + core)]
        return remote(piece, gal_recv.at[frm], gal_ss.at[frm], gal_rs.at[frm], (g, frm * 2 + core))

    gal_swap.wait_recv()
    gal_both[...] = gal[...] + gal_pair[...]

    @pl.loop(1, chips)
    def _(i):
        gal_copy(i).start()

    gal_sum[...] = gal_both[gal_piece(s), :]

    @pl.loop(chunks // 2, chunks)
    def _(c):
        total[c] = wide_dot(inv[:, :rows], resid[c])

    def finish(c):
        def pass_on(copy):
            remote(relay.at[c], relay.at[c], relay_ss.at[c], relay_rs.at[c], (1, s)).wait_recv()
            copy.start()

        when_relaying(c, pass_on)
        for f in range(4):
            @pl.when(arrives[f])
            def _():
                face_copy(c, f).wait_recv()
        cols = pl.ds(pl.multiple_of(c * width, width), width)
        fix_ref[:, cols] = (total[c] + wide_dot(inv[:, rows:], face_recv[c])).astype(BF16)

    late = chunks - chunks // 4

    @pl.loop(0, late)
    def _(c):
        finish(c)

    def gsum_copy(i):
        to = lax.rem(g + i, n_grp)
        return remote(gal_sum, gal_sum_recv.at[g], gsum_ss.at[to], gsum_rs.at[g], (to, s))

    def gsum_from(i):
        frm = lax.rem(g + i, n_grp)
        return remote(gal_sum, gal_sum_recv.at[frm], gsum_ss.at[frm], gsum_rs.at[frm], (frm, s))

    def sum_piece(i):
        return pl.ds(pl.multiple_of(i * sum_rows, 8), sum_rows)

    def sum_copy(i):
        to = lax.rem(g + i, n_grp)
        return remote(sum_send.at[sum_piece(to)], sum_recv.at[g], sum_ss.at[to], sum_rs.at[g], (to, s))

    def sum_from(i):
        frm = lax.rem(g + i, n_grp)
        return remote(sum_send.at[sum_piece(frm)], sum_recv.at[frm], sum_ss.at[frm], sum_rs.at[frm], (frm, s))

    def last_copy(i):
        to = lax.rem(g + i, n_grp)
        return remote(sum_last, sum_full.at[sum_piece(g)], last_ss.at[to], last_rs.at[g], (to, s))

    def last_from(i):
        frm = lax.rem(g + i, n_grp)
        return remote(sum_last, sum_full.at[sum_piece(frm)], last_ss.at[frm], last_rs.at[frm], (frm, s))

    def glast_copy(i):
        to = lax.rem(s + i, n_sub)
        return remote(gal_last, gal_full.at[gal_piece(s)], glast_ss.at[to], glast_rs.at[s], (g, to))

    def glast_from(i):
        frm = lax.rem(s + i, n_sub)
        return remote(gal_last, gal_full.at[gal_piece(frm)], glast_ss.at[frm], glast_rs.at[frm], (g, frm))

    @pl.loop(1, chips)
    def _(i):
        gal_from(i).wait_recv()
        gal_sum[...] += gal_recv[lax.rem(chip + i, chips)]

    @pl.loop(1, n_grp)
    def _(i):
        gsum_copy(i).start()

    @pl.loop(1, chips)
    def _(i):
        rhs_from(i).wait_recv()
        sum_send[:coarse, :] += rhs_recv[lax.rem(chip + i, chips)].astype(F32)

    @pl.loop(1, n_grp)
    def _(i):
        sum_copy(i).start()

    @pl.loop(late, chunks)
    def _(c):
        finish(c)

    gal_last[...] = gal_sum[...]

    @pl.loop(1, n_grp)
    def _(i):
        gsum_from(i).wait_recv()
        gal_last[...] += gal_sum_recv[lax.rem(g + i, n_grp)]

    gal_last[...] = gal_last[...] * scaling

    @pl.loop(1, n_sub)
    def _(i):
        glast_copy(i).start()

    sum_last[...] = sum_send[sum_piece(g), :]

    @pl.loop(1, n_grp)
    def _(i):
        sum_from(i).wait_recv()
        sum_last[...] += sum_recv[lax.rem(g + i, n_grp)]

    sum_last[...] = sum_last[...] * scaling

    @pl.loop(1, n_grp)
    def _(i):
        last_copy(i).start()

    gal_full[gal_piece(s), :] = gal_last[...]
    sum_full[sum_piece(g), :] = sum_last[...]

    @pl.loop(1, n_sub)
    def _(i):
        glast_from(i).wait_recv()

    gal_ref[...] = gal_full[:coarse, :]

    @pl.loop(1, n_grp)
    def _(i):
        last_from(i).wait_recv()

    rhs_ref[...] = sum_full[:coarse, :]

    for f in range(4):
        @pl.when(sends[f])
        def _():
            ext_copy(f).wait_send()

            @pl.loop(0, chunks)
            def _(c):
                face_copy(c, f).wait_send()

    @pl.loop(0, chunks)
    def _(c):
        when_relaying(c, lambda copy: copy.wait_send())

    gal_swap.wait_send()

    @pl.loop(0, chips)
    def _(i):
        pair_copy(i).wait_send()

    @pl.loop(1, chips)
    def _(i):
        rhs_copy(i).wait_send()
        gal_copy(i).wait_send()

    @pl.loop(1, n_sub)
    def _(i):
        glast_copy(i).wait_send()

    @pl.loop(1, n_grp)
    def _(i):
        gsum_copy(i).wait_send()
        sum_copy(i).wait_send()
        last_copy(i).wait_send()


def local_any(n_grp, n_sub, residual, inverse_blocks, operator_tiles, column_blocks, coarse_basis, face_rows):
    resid = residual[0, 0]
    inv = inverse_blocks[0, 0]
    tiles = operator_tiles[0, 0]
    basis = jnp.swapaxes(coarse_basis[0, 0], 0, 1)
    faces = face_rows[0, 0]
    rows, k = resid.shape
    coarse = basis.shape[0]
    ov = faces.shape[1]
    tile = tiles.shape[-1]
    ext_blocks = inv.shape[1] // tile
    part = k // n_sub
    width = max(512, part)
    chunks = k // width
    gal_rows = -(-coarse // (8 * n_sub)) * 8
    sum_rows = -(-coarse // (8 * n_grp)) * 8
    chips = n_sub // 2
    scaling = 1.0 / math.sqrt(rows * n_grp * n_sub)
    dma = pltpu.SemaphoreType.DMA
    hbm = pl.BlockSpec(memory_space=pl.ANY)
    vmem = pl.BlockSpec(memory_space=pltpu.VMEM)
    fix, gal, rhs = pl.pallas_call(
        functools.partial(any_kernel, n_grp, n_sub, width, scaling),
        out_shape=(
            pltpu.VMEM((rows, k), BF16),
            pltpu.VMEM((coarse, coarse), F32),
            pltpu.VMEM((coarse, part), F32),
        ),
        in_specs=[pl.BlockSpec(memory_space=pltpu.SMEM), vmem, vmem, hbm, hbm, hbm],
        out_specs=(vmem, vmem, vmem),
        scratch_shapes=[
            pltpu.VMEM((chunks, rows, width), BF16),
            pltpu.VMEM(inv.shape, BF16),
            pltpu.VMEM(tiles.shape, BF16),
            pltpu.VMEM((4 * ov, rows), BF16),
            pltpu.VMEM((4, coarse, tile), BF16),
            pltpu.VMEM((ext_blocks, coarse, tile), BF16),
            pltpu.VMEM((chunks, 4 * ov, width), BF16),
            pltpu.VMEM((chunks, 4 * ov, width), BF16),
            pltpu.VMEM((chunks, ov, width), BF16),
            pltpu.VMEM((chunks, rows, width), F32),
            pltpu.VMEM((chips, coarse, part), F32),
            pltpu.VMEM((chips, coarse, part), F32),
            pltpu.VMEM((chips, coarse, part), F32),
            pltpu.VMEM((chips, coarse, part), BF16),
            pltpu.VMEM((chips, coarse, part), BF16),
            pltpu.VMEM((n_grp * sum_rows, part), F32),
            pltpu.VMEM((n_grp, sum_rows, part), F32),
            pltpu.VMEM((sum_rows, part), F32),
            pltpu.VMEM((n_grp * sum_rows, part), F32),
            pltpu.VMEM((rows, coarse), BF16),
            pltpu.VMEM((n_sub * gal_rows, coarse), F32),
            pltpu.VMEM((n_sub * gal_rows, coarse), F32),
            pltpu.VMEM((n_sub * gal_rows, coarse), F32),
            pltpu.VMEM((chips, gal_rows, coarse), F32),
            pltpu.VMEM((gal_rows, coarse), F32),
            pltpu.VMEM((n_grp, gal_rows, coarse), F32),
            pltpu.VMEM((gal_rows, coarse), F32),
            pltpu.VMEM((n_sub * gal_rows, coarse), F32),
            dma((2,)),
            dma((chunks,)),
            dma((4,)),
            dma((4,)),
            dma((chunks, 4)),
            dma((chunks, 4)),
            dma((chunks,)),
            dma((chunks,)),
            dma((chips,)),
            dma((chips,)),
            dma((1,)),
            dma((1,)),
            dma((chips,)),
            dma((chips,)),
            dma((n_grp,)),
            dma((n_grp,)),
            dma((n_grp,)),
            dma((n_grp,)),
            dma((chips,)),
            dma((chips,)),
            dma((n_grp,)),
            dma((n_grp,)),
            dma((n_sub,)),
            dma((n_sub,)),
        ],
        compiler_params=pltpu.CompilerParams(
            collective_id=0, has_side_effects=True, vmem_limit_bytes=55 * 1024 * 1024
        ),
    )(column_blocks[0, 0], faces, basis, resid, inv, tiles)
    return fix[None, None], gal, rhs


def plane_kernel(
    n_sub, scaling, relayed, last,
    col_hbm, face_hbm, basis_hbm, resid_hbm, inv_hbm, tiles_hbm,
    done_ref, last_ref, face_recv, inv, gal_ref, rhs_ref,
    col_ref, face_ref, basis_ref, resid, tiles, left, ext_send, ext, face_send, relay, total,
    keep, pair_send, pair_recv, y_keep, y_send, y_recv, z_send, z_recv, mine, cross_send, cross_recv,
    applied, gal, gal_pair, gal_both, gal_send, gal_recv, gal_sum, gal_other, gal_last, gal_full, gal_half,
    in_sem, resid_sem, ext_ss, ext_rs, face_ss, face_rs, relay_ss, relay_rs,
    pair_ss, pair_rs, y_ss, y_rs, z_ss, z_rs, token_sem, swap_ss, swap_rs, cross_ss, cross_rs, gal_ss, gal_rs, glast_ss, glast_rs,
):
    g = lax.axis_index("grp")
    s = lax.axis_index("sub")
    n_grp = 4
    gx, gy = lax.rem(g, 2), g // 2
    chip, core = s // 2, lax.rem(s, 2)
    beside = g + 1 - 2 * gx
    above = lax.rem(g + 2, 4)
    x_near, y_near, pair = (beside, s), (above, s), (g, s + 1 - 2 * core)
    chips = n_sub // 2
    chunks, rows, width = resid.shape
    coarse = basis_ref.shape[0]
    row_blocks, per_row, tile = tiles.shape[:3]
    own_blocks = rows // tile
    ov = face_ref.shape[1]
    faces = 4 * ov
    part = width // 2
    half = part // 2
    pieces = 2 * chips
    piece_rows = gal_sum.shape[0]
    me = chip * 2 + gy

    def load_resid(c):
        cols = pl.ds(pl.multiple_of(c * width, width), width)
        return pltpu.make_async_copy(resid_hbm.at[:, cols], resid.at[c], resid_sem.at[c])

    load_tiles = pltpu.make_async_copy(tiles_hbm, tiles, in_sem.at[0])
    load_inv = pltpu.make_async_copy(inv_hbm, inv, in_sem.at[1])
    load_faces = pltpu.make_async_copy(face_hbm, face_ref, in_sem.at[2])
    load_basis = pltpu.make_async_copy(basis_hbm, basis_ref, in_sem.at[3])
    load_col = pltpu.make_async_copy(col_hbm, col_ref, in_sem.at[4])

    for load in (load_faces, load_basis, load_resid(0), load_col, load_resid(1)):
        load.start()

    barrier = pltpu.get_barrier_semaphore()

    def greet(device):
        pl.semaphore_signal(barrier, inc=1, device_id=device, device_id_type=MESH)

    across = s - 1 + 2 * core
    below, over = chip > 0, chip < chips - 1
    faces_across = jnp.logical_and(across >= 0, across < n_sub)
    middle = jnp.logical_and(g > 0, g < n_grp - 1)
    for device in (x_near, y_near, pair):
        greet(device)
    for exists, device in (
        (middle, (n_grp - 1 - g, s)), (faces_across, (g, across)), (below, (g, s - 2)), (over, (g, s + 2)),
    ):
        @pl.when(exists)
        def _():
            greet(device)

    def count(*conditions):
        return sum(jnp.where(condition, 1, 0) for condition in conditions)

    def tell(i, device):
        pl.semaphore_signal(token_sem.at[i], inc=1, device_id=device, device_id_type=MESH)

    def met():
        pl.semaphore_wait(barrier, 3 + count(middle, faces_across, below, over))
        tell(0, y_near)
        for exists, device in ((below, (g, s - 2)), (over, (g, s + 2))):
            @pl.when(exists)
            def _():
                tell(0, device)

    def met_further():
        pl.semaphore_wait(token_sem.at[0], 1 + count(below, over))
        tell(1, (g, lax.rem(s + n_sub // 2, n_sub)))

    def met_all():
        pl.semaphore_wait(token_sem.at[1], 1)

    targets = ((g + 1, s), (g - 1, s), (g, s + 1), (g, s - 1))
    sends = (g < n_grp - 1, g > 0, s < n_sub - 1, s > 0)
    arrives = (g > 0, g < n_grp - 1, s > 0, s < n_sub - 1)

    def remote(src, dst, send_sem, recv_sem, device):
        return pltpu.make_async_remote_copy(
            src_ref=src, dst_ref=dst, send_sem=send_sem, recv_sem=recv_sem,
            device_id=device, device_id_type=MESH,
        )

    def ext_copy(f):
        return remote(ext_send.at[f], ext.at[own_blocks + f], ext_ss.at[f], ext_rs.at[f], targets[f])

    def face_copy(c, f):
        span = pl.ds(f * ov, ov)
        return remote(face_send.at[c, span], face_recv.at[c, span], face_ss.at[c, f], face_rs.at[c, f], targets[f])

    first = chunks - relayed

    def relay_in(c, f):
        slot = c - first
        return remote(face_send.at[c, pl.ds(f * ov, ov)], relay.at[slot], face_ss.at[c, f], relay_rs.at[slot], y_near)

    def relay_out(c, f):
        slot, span = c - first, pl.ds(f * ov, ov)
        return remote(relay.at[slot], face_recv.at[c, span], relay_ss.at[slot], face_rs.at[c, f], x_near)

    def when_relaying(do):
        for f, at in ((0, n_grp - 1), (1, 0)):
            @pl.when(g == at)
            def _():
                do(f)

    def near(c):
        for f in range(2):
            @pl.when(jnp.logical_and(sends[f], g != 1 + f))
            def _():
                face_copy(c, f).start()

    def diagonal(c):
        for f in range(2):
            @pl.when(g == 1 + f)
            def _():
                (face_copy if c < first else relay_in)(c, f).start()

    def side(c):
        for f in range(2, 4):
            @pl.when(sends[f])
            def _():
                face_copy(c, f).start()

    load_faces.wait()
    lanes = lax.broadcasted_iota(jnp.int32, (ov, tile), 1)
    for f in range(4):
        wanted = jnp.broadcast_to(face_ref[f:f + 1, :].astype(F32), (ov, ov)).T.astype(jnp.int32)
        for b in range(own_blocks):
            hit = wanted == lanes + b * tile
            left[f * ov:(f + 1) * ov, b * tile:(b + 1) * tile] = jnp.where(hit, 1.0, 0.0).astype(BF16)
    load_basis.wait()
    basis = basis_ref[...]
    left[faces:faces + coarse, :] = basis
    if left.shape[0] > faces + coarse:
        left[faces + coarse:, :] = jnp.zeros((left.shape[0] - faces - coarse, rows), BF16)
    for f in range(4):
        ext_send[f] = dot_rows(basis, left[f * ov:(f + 1) * ov, :]).astype(BF16)

    met()
    for f in range(4):
        @pl.when(sends[f])
        def _():
            ext_copy(f).start()

    def pair_copy(c):
        return remote(pair_send.at[c], pair_recv.at[c], pair_ss.at[c], pair_rs.at[c], pair)

    def y_copy(c):
        return remote(y_send.at[c], y_recv.at[c], y_ss.at[c], y_rs.at[c], y_near)

    def columns(i):
        return pl.ds(pl.multiple_of(i * half, half), half)

    def pass_half(c):
        pair_copy(c).wait_recv()
        y_send[c] = (keep[c, :, columns(1 - gy)] + pair_recv[c, :, columns(1 - gy)]).astype(BF16)
        y_copy(c).start()
        y_keep[c] = keep[c, :, columns(gy)] + pair_recv[c, :, columns(gy)]

    def select(c):
        load_resid(c).wait()
        if c == 0:
            for later in range(2, chunks):
                load_resid(later).start()
            load_tiles.start()
        if c == 1:
            load_inv.start()
        both = wide_dot(left[...], resid[c])
        face_send[c] = both[:faces].astype(BF16)
        for q in range(2):
            @pl.when(core == q)
            def _():
                keep[c] = both[faces:faces + coarse, q * part:(q + 1) * part]
                pair_send[c] = both[faces:faces + coarse, (1 - q) * part:(2 - q) * part]

        pair_copy(c).start()

    def fill():
        for f in range(4):
            @pl.when(jnp.logical_not(arrives[f]))
            def _():
                ext[own_blocks + f] = jnp.zeros((coarse, tile), BF16)
                face_recv[:, f * ov:(f + 1) * ov, :] = jnp.zeros((chunks, ov, width), BF16)
        for b in range(own_blocks):
            ext[b] = basis_ref[:, b * tile:(b + 1) * tile]

    wide = gal.shape[2]
    gal_swap = remote(gal.at[1 - core], gal_pair, swap_ss.at[0], swap_rs.at[0], pair)

    def assemble():
        load_tiles.wait()
        load_col.wait()
        for f in range(4):
            @pl.when(arrives[f])
            def _():
                ext_copy(f).wait_recv()

        for b in range(row_blocks):
            row = jnp.concatenate([tiles[b, j] for j in range(per_row)], axis=1)
            picked = jnp.concatenate([ext[col_ref[b, j]] for j in range(per_row)], axis=1)
            applied[:, b * tile:(b + 1) * tile] = dot_rows(picked, row).astype(BF16)

        whole = dot_rows(basis_ref[...], applied[...])
        gal[0, :coarse, :] = whole[:, :wide]
        gal[0, coarse:, :] = jnp.zeros((gal.shape[1] - coarse, wide), F32)
        gal[1] = jnp.zeros(gal.shape[1:], F32)
        gal[1, :coarse, :coarse - wide] = whole[:, wide:]
        gal_swap.start()

    def slot_of(c):
        return c - 1 if c > last else c

    def multiply(c):
        if c == 3:
            load_inv.wait()
        (last_ref if c == last else total.at[slot_of(c)])[...] = wide_dot(inv[:, :rows], resid[c])

    def z_copy(c):
        return remote(z_send.at[c], z_recv.at[chip], z_ss.at[c], z_rs.at[chip], (g, c * 2 + core))

    def z_from(i):
        frm = lax.rem(chip + i, chips)
        return remote(z_send.at[frm], z_recv.at[frm], z_ss.at[frm], z_rs.at[frm], (g, frm * 2 + core))

    def pass_quarter(c):
        y_copy(c).wait_recv()
        joined = y_keep[c] + y_recv[c].astype(F32)

        @pl.when(chip == c)
        def _():
            mine[...] = joined

        @pl.when(chip != c)
        def _():
            z_send[c] = joined.astype(BF16)
            z_copy(c).start()

    def rows_of(i):
        return pl.ds(pl.multiple_of(i * piece_rows, piece_rows), piece_rows)

    def holder(i):
        return (lax.rem(i, 2) * 2 + gx, (i // 2) * 2 + core)

    def gal_copy(i):
        to = lax.rem(me + i, pieces)
        return remote(gal_send.at[rows_of(to)], gal_recv.at[me], gal_ss.at[to], gal_rs.at[me], holder(to))

    def gal_from(i):
        frm = lax.rem(me + i, pieces)
        return remote(gal_send.at[rows_of(frm)], gal_recv.at[frm], gal_ss.at[frm], gal_rs.at[frm], holder(frm))

    def gal_spread():
        gal_swap.wait_recv()
        gal_both[...] = gal[core] + gal_pair[...]
        gal_send[...] = gal_both[...].astype(BF16)

        @pl.loop(1, pieces)
        def _(i):
            gal_copy(i).start()

    def relay_on(c):
        def do(f):
            slot = c - first
            remote(relay.at[slot], relay.at[slot], relay_ss.at[slot], relay_rs.at[slot], y_near).wait_recv()
            relay_out(c, f).start()

        when_relaying(do)

    gal_cross = remote(gal_sum, gal_other, swap_ss.at[1], swap_rs.at[1], x_near)

    def gal_gather():
        gal_sum[...] = gal_both[rows_of(me), :]

        @pl.loop(1, pieces)
        def _(i):
            gal_from(i).wait_recv()
            gal_sum[...] += gal_recv[lax.rem(me + i, pieces)].astype(F32)

        gal_cross.start()

    def cross_copy(i):
        to = lax.rem(g + i, n_grp)
        return remote(cross_send, cross_recv.at[g], cross_ss.at[to], cross_rs.at[g], (to, s))

    def cross_from(i):
        frm = lax.rem(g + i, n_grp)
        return remote(cross_send, cross_recv.at[frm], cross_ss.at[frm], cross_rs.at[frm], (frm, s))

    def cross():
        @pl.loop(1, chips)
        def _(i):
            z_from(i).wait_recv()
            mine[...] += z_recv[lax.rem(chip + i, chips)].astype(F32)

        cross_send[...] = mine[...].astype(BF16)

        @pl.loop(1, n_grp)
        def _(i):
            cross_copy(i).start()

    def glast_copy(i):
        to = lax.rem(me + i, pieces)
        return remote(gal_last, gal_full.at[rows_of(me)], glast_ss.at[to], glast_rs.at[me], holder(to))

    def glast_from(i):
        frm = lax.rem(me + i, pieces)
        return remote(gal_last, gal_full.at[rows_of(frm)], glast_ss.at[frm], glast_rs.at[frm], holder(frm))

    def await_faces(c, which):
        for f in which:
            @pl.when(arrives[f])
            def _():
                face_copy(c, f).wait_recv()

    def finish(c):
        await_faces(c, range(4))
        if c != last:
            margin = wide_dot(inv[:, rows:], face_recv[c])
            done_ref[slot_of(c)] = (total[slot_of(c)] + margin).astype(BF16)

    def gal_return():
        gal_cross.wait_recv()
        gal_last[...] = (gal_sum[...] + gal_other[...]) * scaling

        @pl.loop(1, pieces)
        def _(i):
            glast_copy(i).start()

        gal_full[rows_of(me), :] = gal_last[...]

    gal_last_swap = remote(gal_full, gal_half, swap_ss.at[2], swap_rs.at[2], pair)

    def gal_share():
        @pl.loop(1, pieces)
        def _(i):
            glast_from(i).wait_recv()

        gal_last_swap.start()

    def gal_end():
        gal_last_swap.wait_recv()
        for q in range(2):
            @pl.when(core == q)
            def _():
                low, high = (gal_full, gal_half) if q == 0 else (gal_half, gal_full)
                gal_ref[:, :wide] = low[:coarse, :]
                gal_ref[:, wide:] = high[:coarse, :coarse - wide]

    def rhs_end():
        @pl.loop(1, n_grp)
        def _(i):
            cross_from(i).wait_recv()

        ours = cross_send[...].astype(F32) + cross_recv[beside].astype(F32)
        theirs = cross_recv[above].astype(F32) + cross_recv[n_grp - 1 - g].astype(F32)
        rhs_ref[:, columns(gy)] = ours * scaling
        rhs_ref[:, columns(1 - gy)] = theirs * scaling

    def settle():
        for f in range(4):
            @pl.when(sends[f])
            def _():
                ext_copy(f).wait_send()

        for f in range(2, 4):
            @pl.when(sends[f])
            def _():
                for c in range(chunks):
                    face_copy(c, f).wait_send()

        for c in range(chunks):
            pair_copy(c).wait_send()
            y_copy(c).wait_send()

            @pl.when(c != chip)
            def _():
                z_copy(c).wait_send()

        for i in range(1, pieces):
            gal_copy(i).wait_send()
        gal_swap.wait_send()

    select(0)
    near(0)
    fill()
    select(1)
    side(1)
    met_further()
    pass_half(0)
    select(2)
    diagonal(2)
    near(2)
    side(2)
    assemble()
    select(3)
    pass_half(2)
    near(3)
    met_all()
    gal_spread()
    side(0)
    diagonal(1)
    pass_half(1)
    pass_half(3)
    multiply(3)
    relay_on(2)
    multiply(1)
    diagonal(3)
    side(3)
    pass_quarter(0)
    gal_gather()
    pass_quarter(2)
    pass_quarter(1)
    diagonal(0)
    near(1)
    pass_quarter(3)
    multiply(2)
    finish(2)
    relay_on(3)
    gal_return()
    multiply(0)
    cross()
    finish(0)
    settle()
    gal_share()
    finish(3)
    finish(1)
    gal_end()
    rhs_end()
    for f in range(2):
        @pl.when(sends[f])
        def _():
            @pl.loop(0, chunks)
            def _(c):
                face_copy(c, f).wait_send()

    def sent_on(f):
        @pl.loop(first, chunks)
        def _(c):
            relay_out(c, f).wait_send()

    when_relaying(sent_on)

    @pl.loop(1, pieces)
    def _(i):
        glast_copy(i).wait_send()

    @pl.loop(1, n_grp)
    def _(i):
        cross_copy(i).wait_send()

    for copy in (gal_cross, gal_last_swap):
        copy.wait_send()


def store_kernel(last, done, total, faces, inv, gal, rhs, fix_hbm, gal_hbm, rhs_hbm, ends, sems):
    others, rows, width = done.shape
    chunks = others + 1
    halves, _, half = ends.shape

    def columns(start, size):
        return fix_hbm.at[:, pl.ds(start, size)]

    copies = [
        pltpu.make_async_copy(done.at[i], columns((i + (i >= last)) * width, width), sems.at[i]) for i in range(others)
    ]
    copies.append(pltpu.make_async_copy(gal, gal_hbm, sems.at[others]))
    copies.append(pltpu.make_async_copy(rhs, rhs_hbm, sems.at[others + 1]))
    for copy in copies:
        copy.start()
    for h in range(halves):
        span = slice(h * half, (h + 1) * half)
        margin = wide_dot(inv[:, rows:], faces[last, :, span])
        ends[h] = (total[:, span] + margin).astype(BF16)
        copy = pltpu.make_async_copy(ends.at[h], columns(last * width + h * half, half), sems.at[chunks + 1 + h])
        copy.start()
        copies.append(copy)
    for copy in copies:
        copy.wait()


def fits_plane(mesh):
    return mesh.shape["grp"] == 4 and mesh.shape["sub"] == 8


def local_plane(n_grp, n_sub, residual, inverse_blocks, operator_tiles, column_blocks, coarse_basis, face_rows):
    resid = residual[0, 0]
    inv = inverse_blocks[0, 0]
    tiles = operator_tiles[0, 0]
    basis = jnp.swapaxes(coarse_basis[0, 0], 0, 1)
    faces = face_rows[0, 0]
    rows, k = resid.shape
    coarse = basis.shape[0]
    ov = faces.shape[1]
    tile = tiles.shape[-1]
    ext_blocks = inv.shape[1] // tile
    part = k // n_sub
    half = part // 2
    width = 2 * part
    chunks = chips = n_sub // 2
    relayed = chunks // 2
    pieces = 2 * chips
    piece_rows = -(-coarse // (16 * pieces)) * 16
    wide = -(-coarse // 256) * 128
    scaling = 1.0 / math.sqrt(rows * n_grp * n_sub)
    dma = pltpu.SemaphoreType.DMA
    hbm = pl.BlockSpec(memory_space=pl.ANY)
    vmem = pl.BlockSpec(memory_space=pltpu.VMEM)
    left_rows = -(-(4 * ov + coarse) // 16) * 16
    last = 1
    kept = pl.pallas_call(
        functools.partial(plane_kernel, n_sub, scaling, relayed, last),
        out_shape=(
            pltpu.VMEM((chunks - 1, rows, width), BF16),
            pltpu.VMEM((rows, width), F32),
            pltpu.VMEM((chunks, 4 * ov, width), BF16),
            pltpu.VMEM(inv.shape, BF16),
            pltpu.VMEM((coarse, coarse), F32),
            pltpu.VMEM((coarse, part), F32),
        ),
        in_specs=[hbm] * 6,
        out_specs=(vmem,) * 6,
        scratch_shapes=[
            pltpu.SMEM(column_blocks.shape[2:], jnp.int32),
            pltpu.VMEM(faces.shape, jnp.int32),
            pltpu.VMEM(basis.shape, BF16),
            pltpu.VMEM((chunks, rows, width), BF16),
            pltpu.VMEM(tiles.shape, BF16),
            pltpu.VMEM((left_rows, rows), BF16),
            pltpu.VMEM((4, coarse, tile), BF16),
            pltpu.VMEM((ext_blocks, coarse, tile), BF16),
            pltpu.VMEM((chunks, 4 * ov, width), BF16),
            pltpu.VMEM((relayed, ov, width), BF16),
            pltpu.VMEM((chunks - 1, rows, width), F32),
            pltpu.VMEM((chips, coarse, part), F32),
            pltpu.VMEM((chips, coarse, part), F32),
            pltpu.VMEM((chips, coarse, part), F32),
            pltpu.VMEM((chips, coarse, half), F32),
            pltpu.VMEM((chips, coarse, half), BF16),
            pltpu.VMEM((chips, coarse, half), BF16),
            pltpu.VMEM((chips, coarse, half), BF16),
            pltpu.VMEM((chips, coarse, half), BF16),
            pltpu.VMEM((coarse, half), F32),
            pltpu.VMEM((coarse, half), BF16),
            pltpu.VMEM((n_grp, coarse, half), BF16),
            pltpu.VMEM((coarse, rows), BF16),
            pltpu.VMEM((2, pieces * piece_rows, wide), F32),
            pltpu.VMEM((pieces * piece_rows, wide), F32),
            pltpu.VMEM((pieces * piece_rows, wide), F32),
            pltpu.VMEM((pieces * piece_rows, wide), BF16),
            pltpu.VMEM((pieces, piece_rows, wide), BF16),
            pltpu.VMEM((piece_rows, wide), F32),
            pltpu.VMEM((piece_rows, wide), F32),
            pltpu.VMEM((piece_rows, wide), F32),
            pltpu.VMEM((pieces * piece_rows, wide), F32),
            pltpu.VMEM((pieces * piece_rows, wide), F32),
            dma((5,)),
            dma((chunks,)),
            dma((4,)),
            dma((4,)),
            dma((chunks, 4)),
            dma((chunks, 4)),
            dma((relayed,)),
            dma((relayed,)),
            dma((chips,)),
            dma((chips,)),
            dma((chips,)),
            dma((chips,)),
            dma((chips,)),
            dma((chips,)),
            pltpu.SemaphoreType.REGULAR((2,)),
            dma((3,)),
            dma((3,)),
            dma((n_grp,)),
            dma((n_grp,)),
            dma((pieces,)),
            dma((pieces,)),
            dma((pieces,)),
            dma((pieces,)),
        ],
        compiler_params=pltpu.CompilerParams(
            collective_id=0, has_side_effects=True, vmem_limit_bytes=50 * 1024 * 1024
        ),
    )(column_blocks[0, 0], faces, basis, resid, inv, tiles)
    fix, gal, rhs = pl.pallas_call(
        functools.partial(store_kernel, last),
        out_shape=(
            jax.ShapeDtypeStruct((rows, k), BF16),
            jax.ShapeDtypeStruct((coarse, coarse), F32),
            jax.ShapeDtypeStruct((coarse, part), F32),
        ),
        in_specs=[vmem] * 6,
        out_specs=(hbm, hbm, hbm),
        scratch_shapes=[pltpu.VMEM((2, rows, width // 2), BF16), dma((chunks + 3,))],
        compiler_params=pltpu.CompilerParams(vmem_limit_bytes=16 * 1024 * 1024),
    )(*(pltpu.with_memory_space_constraint(x, pltpu.VMEM) for x in kept))
    return fix[None, None], gal, rhs


def solution(mesh):
    body = local_plane if fits_plane(mesh) else local_any
    return jax.shard_map(
        functools.partial(body, mesh.shape["grp"], mesh.shape["sub"]),
        mesh=mesh,
        in_specs=(
            P("grp", "sub", None, None),
            P("grp", "sub", None, None),
            P("grp", "sub", None, None, None, None),
            P("grp", "sub", None, None),
            P("grp", "sub", None, None),
            P("grp", "sub", None, None),
        ),
        out_specs=(P("grp", "sub", None, None), P(), P(None, "sub")),
        check_vma=False,
    )
```

```python
import functools
import math

import jax
import jax.numpy as jnp
from jax import lax
from jax.experimental import pallas as pl
from jax.experimental.pallas import tpu as pltpu
from jax.sharding import PartitionSpec as P

MESH = pl.DeviceIdType.MESH
F32 = jnp.float32
BF16 = jnp.bfloat16


def wide_dot(a, b):
    return jnp.dot(a, b, preferred_element_type=F32)


def dot_rows(a, b):
    return lax.dot_general(a, b, (((1,), (1,)), ((), ())), preferred_element_type=F32)


def any_kernel(
    n_grp, n_sub, width, scaling,
    col_ref, face_ref, basis_ref, resid_hbm, inv_hbm, tiles_hbm,
    fix_ref, gal_ref, rhs_ref,
    resid, inv, tiles, pick, ext_send, ext, face_send, face_recv, relay, total,
    keep, pair_send, pair_recv, rhs_send, rhs_recv, sum_send, sum_recv, sum_last, sum_full,
    applied, gal, gal_pair, gal_both, gal_recv, gal_sum, gal_sum_recv, gal_last, gal_full,
    in_sem, resid_sem, ext_ss, ext_rs, face_ss, face_rs, relay_ss, relay_rs,
    pair_ss, pair_rs, gpair_ss, gpair_rs, rhs_ss, rhs_rs,
    sum_ss, sum_rs, last_ss, last_rs, gal_ss, gal_rs, gsum_ss, gsum_rs, glast_ss, glast_rs,
):
    g = lax.axis_index("grp")
    s = lax.axis_index("sub")
    chip, core = s // 2, lax.rem(s, 2)
    partner = s + 1 - 2 * core
    chips = n_sub // 2
    chunks, rows, _ = resid.shape
    coarse = basis_ref.shape[0]
    row_blocks, per_row, tile = tiles.shape[:3]
    own_blocks = rows // tile
    ov = face_ref.shape[1]
    part = chunks * width // n_sub
    per_chunk = width // part
    gal_rows = gal_recv.shape[1]
    sum_rows = sum_recv.shape[1]
    relayed = n_grp == 4

    def load_resid(c):
        cols = pl.ds(pl.multiple_of(c * width, width), width)
        return pltpu.make_async_copy(resid_hbm.at[:, cols], resid.at[c], resid_sem.at[c])

    load_tiles = pltpu.make_async_copy(tiles_hbm, tiles, in_sem.at[0])
    load_inv = pltpu.make_async_copy(inv_hbm, inv, in_sem.at[1])

    @pl.loop(0, chunks)
    def _(c):
        load_resid(c).start()

    load_tiles.start()
    load_inv.start()

    barrier = pltpu.get_barrier_semaphore()

    @pl.loop(1, n_sub)
    def _(i):
        pl.semaphore_signal(barrier, inc=1, device_id=(g, lax.rem(s + i, n_sub)), device_id_type=MESH)

    @pl.loop(1, n_grp)
    def _(i):
        pl.semaphore_signal(barrier, inc=1, device_id=(lax.rem(g + i, n_grp), s), device_id_type=MESH)

    targets = ((g + 1, s), (g - 1, s), (g, s + 1), (g, s - 1))
    sends = (g < n_grp - 1, g > 0, s < n_sub - 1, s > 0)
    arrives = (g > 0, g < n_grp - 1, s > 0, s < n_sub - 1)

    def remote(src, dst, send_sem, recv_sem, device):
        return pltpu.make_async_remote_copy(
            src_ref=src, dst_ref=dst, send_sem=send_sem, recv_sem=recv_sem,
            device_id=device, device_id_type=MESH,
        )

    def ext_copy(f):
        return remote(ext_send.at[f], ext.at[own_blocks + f], ext_ss.at[f], ext_rs.at[f], targets[f])

    def face_copy(c, f, far=False):
        span = pl.ds(f * ov, ov)
        if far:
            way = (n_grp - 1) * (lax.rem(c + f, 2))
            return remote(face_send.at[c, span], relay.at[c], face_ss.at[c, f], relay_rs.at[c], (way, s))
        return remote(face_send.at[c, span], face_recv.at[c, span], face_ss.at[c, f], face_rs.at[c, f], targets[f])

    def forward(c, f):
        span = pl.ds(f * ov, ov)
        return remote(relay.at[c], face_recv.at[c, span], relay_ss.at[c], face_rs.at[c, f], (2 - f, s))

    def far_face(f):
        return (g == 1 + f) if relayed and f < 2 else None

    def face_start(c, f):
        far = far_face(f)
        if far is None:
            @pl.when(sends[f])
            def _():
                face_copy(c, f).start()
        else:
            @pl.when(far)
            def _():
                face_copy(c, f, True).start()

            @pl.when(jnp.logical_and(sends[f], jnp.logical_not(far)))
            def _():
                face_copy(c, f).start()

    def when_relaying(c, do):
        if relayed:
            turn = lax.rem(c + jnp.where(g == 3, 1, 0), 2)
            for f in range(2):
                @pl.when(jnp.logical_and(jnp.logical_or(g == 0, g == 3), turn == f))
                def _():
                    do(forward(c, f))

    lanes = lax.broadcasted_iota(jnp.int32, (ov, tile), 1)
    for f in range(4):
        wanted = jnp.broadcast_to(face_ref[f:f + 1, :].astype(F32), (ov, ov)).T.astype(jnp.int32)
        for b in range(own_blocks):
            hit = wanted == lanes + b * tile
            pick[f * ov:(f + 1) * ov, b * tile:(b + 1) * tile] = jnp.where(hit, 1.0, 0.0).astype(BF16)
    basis = basis_ref[...]
    for f in range(4):
        ext_send[f] = dot_rows(basis, pick[f * ov:(f + 1) * ov, :]).astype(BF16)
    for b in range(own_blocks):
        ext[b] = basis_ref[:, b * tile:(b + 1) * tile]

    for f in range(4):
        @pl.when(jnp.logical_not(arrives[f]))
        def _():
            ext[own_blocks + f] = jnp.zeros((coarse, tile), BF16)
            face_recv[:, f * ov:(f + 1) * ov, :] = jnp.zeros((chunks, ov, width), BF16)

    pl.semaphore_wait(barrier, n_sub - 1 + n_grp - 1)
    for f in range(4):
        @pl.when(sends[f])
        def _():
            ext_copy(f).start()

    def pair_copy(i):
        return remote(pair_send.at[i], pair_recv.at[i], pair_ss.at[i], pair_rs.at[i], (g, partner))

    @pl.loop(0, chunks)
    def _(c):
        load_resid(c).wait()
        face_send[c] = wide_dot(pick[...], resid[c]).astype(BF16)
        for f in range(4):
            face_start(c, f)
        term = wide_dot(basis_ref[...], resid[c])
        for q in range(per_chunk):
            to = c * per_chunk + q
            piece = term[:, q * part:(q + 1) * part]

            @pl.when(lax.rem(to, 2) == core)
            def _():
                keep[to // 2] = piece

            @pl.when(lax.rem(to, 2) != core)
            def _():
                pair_send[to // 2] = piece
                pair_copy(to // 2).start()

    load_tiles.wait()
    for f in range(4):
        @pl.when(arrives[f])
        def _():
            ext_copy(f).wait_recv()

    @pl.loop(0, row_blocks)
    def _(b):
        row = jnp.concatenate([tiles[b, j] for j in range(per_row)], axis=1)
        picked = jnp.concatenate([ext[col_ref[b, j]] for j in range(per_row)], axis=1)
        applied[pl.ds(pl.multiple_of(b * tile, tile), tile), :] = dot_rows(row, picked).astype(BF16)

    gal[coarse:, :] = jnp.zeros((gal.shape[0] - coarse, coarse), F32)
    gal[:coarse, :] = wide_dot(basis_ref[...], applied[...])

    gal_swap = remote(gal, gal_pair, gpair_ss.at[0], gpair_rs.at[0], (g, partner))
    gal_swap.start()
    def rhs_copy(i):
        to = lax.rem(chip + i, chips)
        return remote(rhs_send.at[to], rhs_recv.at[chip], rhs_ss.at[to], rhs_rs.at[chip], (g, to * 2 + core))

    def rhs_from(i):
        frm = lax.rem(chip + i, chips)
        return remote(rhs_send.at[frm], rhs_recv.at[frm], rhs_ss.at[frm], rhs_rs.at[frm], (g, frm * 2 + core))

    @pl.loop(1, chips)
    def _(i):
        to = lax.rem(chip + i, chips)
        pair_copy(to).wait_recv()
        rhs_send[to] = (keep[to] + pair_recv[to]).astype(BF16)
        rhs_copy(i).start()

    pair_copy(chip).wait_recv()
    sum_send[:coarse, :] = keep[chip] + pair_recv[chip]
    if sum_send.shape[0] > coarse:
        sum_send[coarse:, :] = jnp.zeros((sum_send.shape[0] - coarse, part), F32)
    load_inv.wait()

    @pl.loop(0, chunks // 2)
    def _(c):
        total[c] = wide_dot(inv[:, :rows], resid[c])

    def gal_piece(i):
        return pl.ds(pl.multiple_of(i * gal_rows, 8), gal_rows)

    def gal_copy(i):
        to = lax.rem(chip + i, chips)
        piece = gal_both.at[gal_piece(to * 2 + core)]
        return remote(piece, gal_recv.at[chip], gal_ss.at[to], gal_rs.at[chip], (g, to * 2 + core))

    def gal_from(i):
        frm = lax.rem(chip + i, chips)
        piece = gal_both.at[gal_piece(frm * 2 + core)]
        return remote(piece, gal_recv.at[frm], gal_ss.at[frm], gal_rs.at[frm], (g, frm * 2 + core))

    gal_swap.wait_recv()
    gal_both[...] = gal[...] + gal_pair[...]

    @pl.loop(1, chips)
    def _(i):
        gal_copy(i).start()

    gal_sum[...] = gal_both[gal_piece(s), :]

    @pl.loop(chunks // 2, chunks)
    def _(c):
        total[c] = wide_dot(inv[:, :rows], resid[c])

    def finish(c):
        def pass_on(copy):
            remote(relay.at[c], relay.at[c], relay_ss.at[c], relay_rs.at[c], (1, s)).wait_recv()
            copy.start()

        when_relaying(c, pass_on)
        for f in range(4):
            @pl.when(arrives[f])
            def _():
                face_copy(c, f).wait_recv()
        cols = pl.ds(pl.multiple_of(c * width, width), width)
        fix_ref[:, cols] = (total[c] + wide_dot(inv[:, rows:], face_recv[c])).astype(BF16)

    late = chunks - chunks // 4

    @pl.loop(0, late)
    def _(c):
        finish(c)

    def gsum_copy(i):
        to = lax.rem(g + i, n_grp)
        return remote(gal_sum, gal_sum_recv.at[g], gsum_ss.at[to], gsum_rs.at[g], (to, s))

    def gsum_from(i):
        frm = lax.rem(g + i, n_grp)
        return remote(gal_sum, gal_sum_recv.at[frm], gsum_ss.at[frm], gsum_rs.at[frm], (frm, s))

    def sum_piece(i):
        return pl.ds(pl.multiple_of(i * sum_rows, 8), sum_rows)

    def sum_copy(i):
        to = lax.rem(g + i, n_grp)
        return remote(sum_send.at[sum_piece(to)], sum_recv.at[g], sum_ss.at[to], sum_rs.at[g], (to, s))

    def sum_from(i):
        frm = lax.rem(g + i, n_grp)
        return remote(sum_send.at[sum_piece(frm)], sum_recv.at[frm], sum_ss.at[frm], sum_rs.at[frm], (frm, s))

    def last_copy(i):
        to = lax.rem(g + i, n_grp)
        return remote(sum_last, sum_full.at[sum_piece(g)], last_ss.at[to], last_rs.at[g], (to, s))

    def last_from(i):
        frm = lax.rem(g + i, n_grp)
        return remote(sum_last, sum_full.at[sum_piece(frm)], last_ss.at[frm], last_rs.at[frm], (frm, s))

    def glast_copy(i):
        to = lax.rem(s + i, n_sub)
        return remote(gal_last, gal_full.at[gal_piece(s)], glast_ss.at[to], glast_rs.at[s], (g, to))

    def glast_from(i):
        frm = lax.rem(s + i, n_sub)
        return remote(gal_last, gal_full.at[gal_piece(frm)], glast_ss.at[frm], glast_rs.at[frm], (g, frm))

    @pl.loop(1, chips)
    def _(i):
        gal_from(i).wait_recv()
        gal_sum[...] += gal_recv[lax.rem(chip + i, chips)]

    @pl.loop(1, n_grp)
    def _(i):
        gsum_copy(i).start()

    @pl.loop(1, chips)
    def _(i):
        rhs_from(i).wait_recv()
        sum_send[:coarse, :] += rhs_recv[lax.rem(chip + i, chips)].astype(F32)

    @pl.loop(1, n_grp)
    def _(i):
        sum_copy(i).start()

    @pl.loop(late, chunks)
    def _(c):
        finish(c)

    gal_last[...] = gal_sum[...]

    @pl.loop(1, n_grp)
    def _(i):
        gsum_from(i).wait_recv()
        gal_last[...] += gal_sum_recv[lax.rem(g + i, n_grp)]

    gal_last[...] = gal_last[...] * scaling

    @pl.loop(1, n_sub)
    def _(i):
        glast_copy(i).start()

    sum_last[...] = sum_send[sum_piece(g), :]

    @pl.loop(1, n_grp)
    def _(i):
        sum_from(i).wait_recv()
        sum_last[...] += sum_recv[lax.rem(g + i, n_grp)]

    sum_last[...] = sum_last[...] * scaling

    @pl.loop(1, n_grp)
    def _(i):
        last_copy(i).start()

    gal_full[gal_piece(s), :] = gal_last[...]
    sum_full[sum_piece(g), :] = sum_last[...]

    @pl.loop(1, n_sub)
    def _(i):
        glast_from(i).wait_recv()

    gal_ref[...] = gal_full[:coarse, :]

    @pl.loop(1, n_grp)
    def _(i):
        last_from(i).wait_recv()

    rhs_ref[...] = sum_full[:coarse, :]

    for f in range(4):
        @pl.when(sends[f])
        def _():
            ext_copy(f).wait_send()

            @pl.loop(0, chunks)
            def _(c):
                face_copy(c, f).wait_send()

    @pl.loop(0, chunks)
    def _(c):
        when_relaying(c, lambda copy: copy.wait_send())

    gal_swap.wait_send()

    @pl.loop(0, chips)
    def _(i):
        pair_copy(i).wait_send()

    @pl.loop(1, chips)
    def _(i):
        rhs_copy(i).wait_send()
        gal_copy(i).wait_send()

    @pl.loop(1, n_sub)
    def _(i):
        glast_copy(i).wait_send()

    @pl.loop(1, n_grp)
    def _(i):
        gsum_copy(i).wait_send()
        sum_copy(i).wait_send()
        last_copy(i).wait_send()


def local_any(n_grp, n_sub, residual, inverse_blocks, operator_tiles, column_blocks, coarse_basis, face_rows):
    resid = residual[0, 0]
    inv = inverse_blocks[0, 0]
    tiles = operator_tiles[0, 0]
    basis = jnp.swapaxes(coarse_basis[0, 0], 0, 1)
    faces = face_rows[0, 0]
    rows, k = resid.shape
    coarse = basis.shape[0]
    ov = faces.shape[1]
    tile = tiles.shape[-1]
    ext_blocks = inv.shape[1] // tile
    part = k // n_sub
    width = max(512, part)
    chunks = k // width
    gal_rows = -(-coarse // (8 * n_sub)) * 8
    sum_rows = -(-coarse // (8 * n_grp)) * 8
    chips = n_sub // 2
    scaling = 1.0 / math.sqrt(rows * n_grp * n_sub)
    dma = pltpu.SemaphoreType.DMA
    hbm = pl.BlockSpec(memory_space=pl.ANY)
    vmem = pl.BlockSpec(memory_space=pltpu.VMEM)
    fix, gal, rhs = pl.pallas_call(
        functools.partial(any_kernel, n_grp, n_sub, width, scaling),
        out_shape=(
            pltpu.VMEM((rows, k), BF16),
            pltpu.VMEM((coarse, coarse), F32),
            pltpu.VMEM((coarse, part), F32),
        ),
        in_specs=[pl.BlockSpec(memory_space=pltpu.SMEM), vmem, vmem, hbm, hbm, hbm],
        out_specs=(vmem, vmem, vmem),
        scratch_shapes=[
            pltpu.VMEM((chunks, rows, width), BF16),
            pltpu.VMEM(inv.shape, BF16),
            pltpu.VMEM(tiles.shape, BF16),
            pltpu.VMEM((4 * ov, rows), BF16),
            pltpu.VMEM((4, coarse, tile), BF16),
            pltpu.VMEM((ext_blocks, coarse, tile), BF16),
            pltpu.VMEM((chunks, 4 * ov, width), BF16),
            pltpu.VMEM((chunks, 4 * ov, width), BF16),
            pltpu.VMEM((chunks, ov, width), BF16),
            pltpu.VMEM((chunks, rows, width), F32),
            pltpu.VMEM((chips, coarse, part), F32),
            pltpu.VMEM((chips, coarse, part), F32),
            pltpu.VMEM((chips, coarse, part), F32),
            pltpu.VMEM((chips, coarse, part), BF16),
            pltpu.VMEM((chips, coarse, part), BF16),
            pltpu.VMEM((n_grp * sum_rows, part), F32),
            pltpu.VMEM((n_grp, sum_rows, part), F32),
            pltpu.VMEM((sum_rows, part), F32),
            pltpu.VMEM((n_grp * sum_rows, part), F32),
            pltpu.VMEM((rows, coarse), BF16),
            pltpu.VMEM((n_sub * gal_rows, coarse), F32),
            pltpu.VMEM((n_sub * gal_rows, coarse), F32),
            pltpu.VMEM((n_sub * gal_rows, coarse), F32),
            pltpu.VMEM((chips, gal_rows, coarse), F32),
            pltpu.VMEM((gal_rows, coarse), F32),
            pltpu.VMEM((n_grp, gal_rows, coarse), F32),
            pltpu.VMEM((gal_rows, coarse), F32),
            pltpu.VMEM((n_sub * gal_rows, coarse), F32),
            dma((2,)),
            dma((chunks,)),
            dma((4,)),
            dma((4,)),
            dma((chunks, 4)),
            dma((chunks, 4)),
            dma((chunks,)),
            dma((chunks,)),
            dma((chips,)),
            dma((chips,)),
            dma((1,)),
            dma((1,)),
            dma((chips,)),
            dma((chips,)),
            dma((n_grp,)),
            dma((n_grp,)),
            dma((n_grp,)),
            dma((n_grp,)),
            dma((chips,)),
            dma((chips,)),
            dma((n_grp,)),
            dma((n_grp,)),
            dma((n_sub,)),
            dma((n_sub,)),
        ],
        compiler_params=pltpu.CompilerParams(
            collective_id=0, has_side_effects=True, vmem_limit_bytes=55 * 1024 * 1024
        ),
    )(column_blocks[0, 0], faces, basis, resid, inv, tiles)
    return fix[None, None], gal, rhs


def plane_kernel(
    n_sub, scaling, relayed, last,
    col_hbm, face_hbm, basis_hbm, resid_hbm, inv_hbm, tiles_hbm,
    done_ref, last_ref, face_recv, inv, gal_ref, rhs_ref,
    col_ref, face_ref, basis_ref, resid, tiles, left, ext_send, ext, face_send, relay, total,
    keep, pair_send, pair_recv, y_keep, y_send, y_recv, z_send, z_recv, mine, cross_send, cross_recv,
    applied, gal, gal_pair, gal_both, gal_send, gal_recv, gal_sum, gal_other, gal_last, gal_full, gal_half,
    in_sem, resid_sem, ext_ss, ext_rs, face_ss, face_rs, relay_ss, relay_rs,
    pair_ss, pair_rs, y_ss, y_rs, z_ss, z_rs, token_sem, swap_ss, swap_rs, cross_ss, cross_rs, gal_ss, gal_rs, glast_ss, glast_rs,
):
    g = lax.axis_index("grp")
    s = lax.axis_index("sub")
    n_grp = 4
    gx, gy = lax.rem(g, 2), g // 2
    chip, core = s // 2, lax.rem(s, 2)
    beside = g + 1 - 2 * gx
    above = lax.rem(g + 2, 4)
    x_near, y_near, pair = (beside, s), (above, s), (g, s + 1 - 2 * core)
    chips = n_sub // 2
    chunks, rows, width = resid.shape
    coarse = basis_ref.shape[0]
    row_blocks, per_row, tile = tiles.shape[:3]
    own_blocks = rows // tile
    ov = face_ref.shape[1]
    faces = 4 * ov
    part = width // 2
    half = part // 2
    pieces = 2 * chips
    piece_rows = gal_sum.shape[0]
    me = chip * 2 + gy

    def load_resid(c):
        cols = pl.ds(pl.multiple_of(c * width, width), width)
        return pltpu.make_async_copy(resid_hbm.at[:, cols], resid.at[c], resid_sem.at[c])

    load_tiles = pltpu.make_async_copy(tiles_hbm, tiles, in_sem.at[0])
    load_inv = pltpu.make_async_copy(inv_hbm, inv, in_sem.at[1])
    load_faces = pltpu.make_async_copy(face_hbm, face_ref, in_sem.at[2])
    load_basis = pltpu.make_async_copy(basis_hbm, basis_ref, in_sem.at[3])
    load_col = pltpu.make_async_copy(col_hbm, col_ref, in_sem.at[4])

    load_faces.start()
    load_basis.start()
    barrier = pltpu.get_barrier_semaphore()

    def greet(device):
        pl.semaphore_signal(barrier, inc=1, device_id=device, device_id_type=MESH)

    across = s - 1 + 2 * core
    below, over = chip > 0, chip < chips - 1
    faces_across = jnp.logical_and(across >= 0, across < n_sub)
    middle = jnp.logical_and(g > 0, g < n_grp - 1)
    for device in (x_near, y_near, pair):
        greet(device)
    for exists, device in (
        (middle, (n_grp - 1 - g, s)), (faces_across, (g, across)), (below, (g, s - 2)), (over, (g, s + 2)),
    ):
        @pl.when(exists)
        def _():
            greet(device)

    for load in (load_resid(0), load_col, load_resid(1)):
        load.start()

    def count(*conditions):
        return sum(jnp.where(condition, 1, 0) for condition in conditions)

    def tell(i, device):
        pl.semaphore_signal(token_sem.at[i], inc=1, device_id=device, device_id_type=MESH)

    def met():
        pl.semaphore_wait(barrier, 3 + count(middle, faces_across, below, over))
        tell(0, y_near)
        for exists, device in ((below, (g, s - 2)), (over, (g, s + 2))):
            @pl.when(exists)
            def _():
                tell(0, device)

    def met_further():
        pl.semaphore_wait(token_sem.at[0], 1 + count(below, over))
        tell(1, (g, lax.rem(s + n_sub // 2, n_sub)))

    def met_all():
        pl.semaphore_wait(token_sem.at[1], 1)

    targets = ((g + 1, s), (g - 1, s), (g, s + 1), (g, s - 1))
    sends = (g < n_grp - 1, g > 0, s < n_sub - 1, s > 0)
    arrives = (g > 0, g < n_grp - 1, s > 0, s < n_sub - 1)

    def remote(src, dst, send_sem, recv_sem, device):
        return pltpu.make_async_remote_copy(
            src_ref=src, dst_ref=dst, send_sem=send_sem, recv_sem=recv_sem,
            device_id=device, device_id_type=MESH,
        )

    def ext_copy(f):
        return remote(ext_send.at[f], ext.at[own_blocks + f], ext_ss.at[f], ext_rs.at[f], targets[f])

    def face_copy(c, f):
        span = pl.ds(f * ov, ov)
        return remote(face_send.at[c, span], face_recv.at[c, span], face_ss.at[c, f], face_rs.at[c, f], targets[f])

    first = chunks - relayed

    def relay_in(c, f):
        slot = c - first
        return remote(face_send.at[c, pl.ds(f * ov, ov)], relay.at[slot], face_ss.at[c, f], relay_rs.at[slot], y_near)

    def relay_out(c, f):
        slot, span = c - first, pl.ds(f * ov, ov)
        return remote(relay.at[slot], face_recv.at[c, span], relay_ss.at[slot], face_rs.at[c, f], x_near)

    def when_relaying(do):
        for f, at in ((0, n_grp - 1), (1, 0)):
            @pl.when(g == at)
            def _():
                do(f)

    def near(c):
        for f in range(2):
            @pl.when(jnp.logical_and(sends[f], g != 1 + f))
            def _():
                face_copy(c, f).start()

    def diagonal(c):
        for f in range(2):
            @pl.when(g == 1 + f)
            def _():
                (face_copy if c < first else relay_in)(c, f).start()

    def side(c):
        for f in range(2, 4):
            @pl.when(sends[f])
            def _():
                face_copy(c, f).start()

    load_faces.wait()
    lanes = lax.broadcasted_iota(jnp.int32, (ov, tile), 1)
    for f in range(4):
        wanted = jnp.broadcast_to(face_ref[f:f + 1, :].astype(F32), (ov, ov)).T.astype(jnp.int32)
        for b in range(own_blocks):
            hit = wanted == lanes + b * tile
            left[f * ov:(f + 1) * ov, b * tile:(b + 1) * tile] = jnp.where(hit, 1.0, 0.0).astype(BF16)
    load_basis.wait()
    basis = basis_ref[...]
    for f in range(4):
        ext_send[f] = dot_rows(basis, left[f * ov:(f + 1) * ov, :]).astype(BF16)

    met()
    for f in range(4):
        @pl.when(sends[f])
        def _():
            ext_copy(f).start()

    left[faces:faces + coarse, :] = basis
    if left.shape[0] > faces + coarse:
        left[faces + coarse:, :] = jnp.zeros((left.shape[0] - faces - coarse, rows), BF16)

    def pair_copy(c):
        return remote(pair_send.at[c], pair_recv.at[c], pair_ss.at[c], pair_rs.at[c], pair)

    def y_copy(c):
        return remote(y_send.at[c], y_recv.at[c], y_ss.at[c], y_rs.at[c], y_near)

    def columns(i):
        return pl.ds(pl.multiple_of(i * half, half), half)

    def pass_half(c):
        pair_copy(c).wait_recv()
        y_send[c] = (keep[c, :, columns(1 - gy)] + pair_recv[c, :, columns(1 - gy)]).astype(BF16)
        y_copy(c).start()
        y_keep[c] = keep[c, :, columns(gy)] + pair_recv[c, :, columns(gy)]

    def select(c):
        load_resid(c).wait()
        if c == 0:
            for later in range(2, chunks):
                load_resid(later).start()
            load_tiles.start()
        if c == 1:
            load_inv.start()
        both = wide_dot(left[...], resid[c])
        face_send[c] = both[:faces].astype(BF16)
        for q in range(2):
            @pl.when(core == q)
            def _():
                keep[c] = both[faces:faces + coarse, q * part:(q + 1) * part]
                pair_send[c] = both[faces:faces + coarse, (1 - q) * part:(2 - q) * part]

        pair_copy(c).start()

    def fill():
        for f in range(4):
            @pl.when(jnp.logical_not(arrives[f]))
            def _():
                ext[own_blocks + f] = jnp.zeros((coarse, tile), BF16)
                face_recv[:, f * ov:(f + 1) * ov, :] = jnp.zeros((chunks, ov, width), BF16)
        for b in range(own_blocks):
            ext[b] = basis_ref[:, b * tile:(b + 1) * tile]

    wide = gal.shape[2]
    gal_swap = remote(gal.at[1 - core], gal_pair, swap_ss.at[0], swap_rs.at[0], pair)

    def assemble():
        load_tiles.wait()
        load_col.wait()
        for f in range(4):
            @pl.when(arrives[f])
            def _():
                ext_copy(f).wait_recv()

        for b in range(row_blocks):
            row = jnp.concatenate([tiles[b, j] for j in range(per_row)], axis=1)
            picked = jnp.concatenate([ext[col_ref[b, j]] for j in range(per_row)], axis=1)
            applied[:, b * tile:(b + 1) * tile] = dot_rows(picked, row).astype(BF16)

        whole = dot_rows(basis_ref[...], applied[...])
        gal[0, :coarse, :] = whole[:, :wide]
        gal[0, coarse:, :] = jnp.zeros((gal.shape[1] - coarse, wide), F32)
        gal[1] = jnp.zeros(gal.shape[1:], F32)
        gal[1, :coarse, :coarse - wide] = whole[:, wide:]
        gal_swap.start()

    def slot_of(c):
        return c - 1 if c > last else c

    def multiply(c):
        if c == 3:
            load_inv.wait()
        (last_ref if c == last else total.at[slot_of(c)])[...] = wide_dot(inv[:, :rows], resid[c])

    def z_copy(c):
        return remote(z_send.at[c], z_recv.at[chip], z_ss.at[c], z_rs.at[chip], (g, c * 2 + core))

    def z_from(i):
        frm = lax.rem(chip + i, chips)
        return remote(z_send.at[frm], z_recv.at[frm], z_ss.at[frm], z_rs.at[frm], (g, frm * 2 + core))

    def pass_quarter(c):
        y_copy(c).wait_recv()
        joined = y_keep[c] + y_recv[c].astype(F32)

        @pl.when(chip == c)
        def _():
            mine[...] = joined

        @pl.when(chip != c)
        def _():
            z_send[c] = joined.astype(BF16)
            z_copy(c).start()

    def rows_of(i):
        return pl.ds(pl.multiple_of(i * piece_rows, piece_rows), piece_rows)

    def holder(i):
        return (lax.rem(i, 2) * 2 + gx, (i // 2) * 2 + core)

    def gal_copy(i):
        to = lax.rem(me + i, pieces)
        return remote(gal_send.at[rows_of(to)], gal_recv.at[me], gal_ss.at[to], gal_rs.at[me], holder(to))

    def gal_from(i):
        frm = lax.rem(me + i, pieces)
        return remote(gal_send.at[rows_of(frm)], gal_recv.at[frm], gal_ss.at[frm], gal_rs.at[frm], holder(frm))

    def gal_spread():
        gal_swap.wait_recv()
        gal_both[...] = gal[core] + gal_pair[...]
        gal_send[...] = gal_both[...].astype(BF16)

        @pl.loop(1, pieces)
        def _(i):
            gal_copy(i).start()

    def relay_on(c):
        def do(f):
            slot = c - first
            remote(relay.at[slot], relay.at[slot], relay_ss.at[slot], relay_rs.at[slot], y_near).wait_recv()
            relay_out(c, f).start()

        when_relaying(do)

    gal_cross = remote(gal_sum, gal_other, swap_ss.at[1], swap_rs.at[1], x_near)

    def gal_gather():
        gal_sum[...] = gal_both[rows_of(me), :]

        @pl.loop(1, pieces)
        def _(i):
            gal_from(i).wait_recv()
            gal_sum[...] += gal_recv[lax.rem(me + i, pieces)].astype(F32)

        gal_cross.start()

    def cross_copy(i):
        to = lax.rem(g + i, n_grp)
        return remote(cross_send, cross_recv.at[g], cross_ss.at[to], cross_rs.at[g], (to, s))

    def cross_from(i):
        frm = lax.rem(g + i, n_grp)
        return remote(cross_send, cross_recv.at[frm], cross_ss.at[frm], cross_rs.at[frm], (frm, s))

    def cross():
        @pl.loop(1, chips)
        def _(i):
            z_from(i).wait_recv()
            mine[...] += z_recv[lax.rem(chip + i, chips)].astype(F32)

        cross_send[...] = mine[...].astype(BF16)

        @pl.loop(1, n_grp)
        def _(i):
            cross_copy(i).start()

    def glast_copy(i):
        to = lax.rem(me + i, pieces)
        return remote(gal_last, gal_full.at[rows_of(me)], glast_ss.at[to], glast_rs.at[me], holder(to))

    def glast_from(i):
        frm = lax.rem(me + i, pieces)
        return remote(gal_last, gal_full.at[rows_of(frm)], glast_ss.at[frm], glast_rs.at[frm], holder(frm))

    def await_faces(c, which):
        for f in which:
            @pl.when(arrives[f])
            def _():
                face_copy(c, f).wait_recv()

    def finish(c):
        await_faces(c, range(4))
        if c != last:
            margin = wide_dot(inv[:, rows:], face_recv[c])
            done_ref[slot_of(c)] = (total[slot_of(c)] + margin).astype(BF16)

    def gal_return():
        gal_cross.wait_recv()
        gal_last[...] = (gal_sum[...] + gal_other[...]) * scaling

        @pl.loop(1, pieces)
        def _(i):
            glast_copy(i).start()

        gal_full[rows_of(me), :] = gal_last[...]

    gal_last_swap = remote(gal_full, gal_half, swap_ss.at[2], swap_rs.at[2], pair)

    def gal_share():
        @pl.loop(1, pieces)
        def _(i):
            glast_from(i).wait_recv()

        gal_last_swap.start()

    def gal_end():
        gal_last_swap.wait_recv()
        for q in range(2):
            @pl.when(core == q)
            def _():
                low, high = (gal_full, gal_half) if q == 0 else (gal_half, gal_full)
                gal_ref[:, :wide] = low[:coarse, :]
                gal_ref[:, wide:] = high[:coarse, :coarse - wide]

    def rhs_end():
        @pl.loop(1, n_grp)
        def _(i):
            cross_from(i).wait_recv()

        ours = cross_send[...].astype(F32) + cross_recv[beside].astype(F32)
        theirs = cross_recv[above].astype(F32) + cross_recv[n_grp - 1 - g].astype(F32)
        rhs_ref[:, columns(gy)] = ours * scaling
        rhs_ref[:, columns(1 - gy)] = theirs * scaling

    def settle():
        for f in range(4):
            @pl.when(sends[f])
            def _():
                ext_copy(f).wait_send()

        for f in range(2, 4):
            @pl.when(sends[f])
            def _():
                for c in range(chunks):
                    face_copy(c, f).wait_send()

        for c in range(chunks):
            pair_copy(c).wait_send()
            y_copy(c).wait_send()

            @pl.when(c != chip)
            def _():
                z_copy(c).wait_send()

        for i in range(1, pieces):
            gal_copy(i).wait_send()
        gal_swap.wait_send()

    select(0)
    near(0)
    fill()
    select(1)
    side(1)
    met_further()
    pass_half(0)
    select(2)
    diagonal(2)
    near(2)
    side(2)
    assemble()
    select(3)
    pass_half(2)
    near(3)
    met_all()
    gal_spread()
    side(0)
    diagonal(1)
    pass_half(1)
    pass_half(3)
    multiply(3)
    relay_on(2)
    multiply(1)
    diagonal(3)
    side(3)
    pass_quarter(0)
    pass_quarter(2)
    gal_gather()
    pass_quarter(1)
    diagonal(0)
    near(1)
    pass_quarter(3)
    multiply(2)
    relay_on(3)
    gal_return()
    finish(2)
    multiply(0)
    cross()
    finish(0)
    finish(3)
    settle()
    gal_share()
    finish(1)
    gal_end()
    rhs_end()
    for f in range(2):
        @pl.when(sends[f])
        def _():
            @pl.loop(0, chunks)
            def _(c):
                face_copy(c, f).wait_send()

    def sent_on(f):
        @pl.loop(first, chunks)
        def _(c):
            relay_out(c, f).wait_send()

    when_relaying(sent_on)

    @pl.loop(1, pieces)
    def _(i):
        glast_copy(i).wait_send()

    @pl.loop(1, n_grp)
    def _(i):
        cross_copy(i).wait_send()

    for copy in (gal_cross, gal_last_swap):
        copy.wait_send()


def store_kernel(last, done, total, faces, inv, gal, rhs, fix_hbm, gal_hbm, rhs_hbm, ends, sems):
    others, rows, width = done.shape
    chunks = others + 1
    halves, _, half = ends.shape

    def columns(start, size):
        return fix_hbm.at[:, pl.ds(start, size)]

    copies = [
        pltpu.make_async_copy(done.at[i], columns((i + (i >= last)) * width, width), sems.at[i]) for i in range(others)
    ]
    copies.append(pltpu.make_async_copy(gal, gal_hbm, sems.at[others]))
    copies.append(pltpu.make_async_copy(rhs, rhs_hbm, sems.at[others + 1]))
    for copy in copies:
        copy.start()
    for h in range(halves):
        span = slice(h * half, (h + 1) * half)
        margin = wide_dot(inv[:, rows:], faces[last, :, span])
        ends[h] = (total[:, span] + margin).astype(BF16)
        copy = pltpu.make_async_copy(ends.at[h], columns(last * width + h * half, half), sems.at[chunks + 1 + h])
        copy.start()
        copies.append(copy)
    for copy in copies:
        copy.wait()


def fits_plane(mesh):
    return mesh.shape["grp"] == 4 and mesh.shape["sub"] == 8


def local_plane(n_grp, n_sub, residual, inverse_blocks, operator_tiles, column_blocks, coarse_basis, face_rows):
    resid = residual[0, 0]
    inv = inverse_blocks[0, 0]
    tiles = operator_tiles[0, 0]
    basis = jnp.swapaxes(coarse_basis[0, 0], 0, 1)
    faces = face_rows[0, 0]
    rows, k = resid.shape
    coarse = basis.shape[0]
    ov = faces.shape[1]
    tile = tiles.shape[-1]
    ext_blocks = inv.shape[1] // tile
    part = k // n_sub
    half = part // 2
    width = 2 * part
    chunks = chips = n_sub // 2
    relayed = chunks // 2
    pieces = 2 * chips
    piece_rows = -(-coarse // (16 * pieces)) * 16
    wide = -(-coarse // 256) * 128
    scaling = 1.0 / math.sqrt(rows * n_grp * n_sub)
    dma = pltpu.SemaphoreType.DMA
    hbm = pl.BlockSpec(memory_space=pl.ANY)
    vmem = pl.BlockSpec(memory_space=pltpu.VMEM)
    left_rows = -(-(4 * ov + coarse) // 16) * 16
    last = 1
    kept = pl.pallas_call(
        functools.partial(plane_kernel, n_sub, scaling, relayed, last),
        out_shape=(
            pltpu.VMEM((chunks - 1, rows, width), BF16),
            pltpu.VMEM((rows, width), F32),
            pltpu.VMEM((chunks, 4 * ov, width), BF16),
            pltpu.VMEM(inv.shape, BF16),
            pltpu.VMEM((coarse, coarse), F32),
            pltpu.VMEM((coarse, part), F32),
        ),
        in_specs=[hbm] * 6,
        out_specs=(vmem,) * 6,
        scratch_shapes=[
            pltpu.SMEM(column_blocks.shape[2:], jnp.int32),
            pltpu.VMEM(faces.shape, jnp.int32),
            pltpu.VMEM(basis.shape, BF16),
            pltpu.VMEM((chunks, rows, width), BF16),
            pltpu.VMEM(tiles.shape, BF16),
            pltpu.VMEM((left_rows, rows), BF16),
            pltpu.VMEM((4, coarse, tile), BF16),
            pltpu.VMEM((ext_blocks, coarse, tile), BF16),
            pltpu.VMEM((chunks, 4 * ov, width), BF16),
            pltpu.VMEM((relayed, ov, width), BF16),
            pltpu.VMEM((chunks - 1, rows, width), F32),
            pltpu.VMEM((chips, coarse, part), F32),
            pltpu.VMEM((chips, coarse, part), F32),
            pltpu.VMEM((chips, coarse, part), F32),
            pltpu.VMEM((chips, coarse, half), F32),
            pltpu.VMEM((chips, coarse, half), BF16),
            pltpu.VMEM((chips, coarse, half), BF16),
            pltpu.VMEM((chips, coarse, half), BF16),
            pltpu.VMEM((chips, coarse, half), BF16),
            pltpu.VMEM((coarse, half), F32),
            pltpu.VMEM((coarse, half), BF16),
            pltpu.VMEM((n_grp, coarse, half), BF16),
            pltpu.VMEM((coarse, rows), BF16),
            pltpu.VMEM((2, pieces * piece_rows, wide), F32),
            pltpu.VMEM((pieces * piece_rows, wide), F32),
            pltpu.VMEM((pieces * piece_rows, wide), F32),
            pltpu.VMEM((pieces * piece_rows, wide), BF16),
            pltpu.VMEM((pieces, piece_rows, wide), BF16),
            pltpu.VMEM((piece_rows, wide), F32),
            pltpu.VMEM((piece_rows, wide), F32),
            pltpu.VMEM((piece_rows, wide), F32),
            pltpu.VMEM((pieces * piece_rows, wide), F32),
            pltpu.VMEM((pieces * piece_rows, wide), F32),
            dma((5,)),
            dma((chunks,)),
            dma((4,)),
            dma((4,)),
            dma((chunks, 4)),
            dma((chunks, 4)),
            dma((relayed,)),
            dma((relayed,)),
            dma((chips,)),
            dma((chips,)),
            dma((chips,)),
            dma((chips,)),
            dma((chips,)),
            dma((chips,)),
            pltpu.SemaphoreType.REGULAR((2,)),
            dma((3,)),
            dma((3,)),
            dma((n_grp,)),
            dma((n_grp,)),
            dma((pieces,)),
            dma((pieces,)),
            dma((pieces,)),
            dma((pieces,)),
        ],
        compiler_params=pltpu.CompilerParams(
            collective_id=0, has_side_effects=True, vmem_limit_bytes=50 * 1024 * 1024
        ),
    )(column_blocks[0, 0], faces, basis, resid, inv, tiles)
    fix, gal, rhs = pl.pallas_call(
        functools.partial(store_kernel, last),
        out_shape=(
            jax.ShapeDtypeStruct((rows, k), BF16),
            jax.ShapeDtypeStruct((coarse, coarse), F32),
            jax.ShapeDtypeStruct((coarse, part), F32),
        ),
        in_specs=[vmem] * 6,
        out_specs=(hbm, hbm, hbm),
        scratch_shapes=[pltpu.VMEM((2, rows, width // 2), BF16), dma((chunks + 3,))],
        compiler_params=pltpu.CompilerParams(vmem_limit_bytes=16 * 1024 * 1024),
    )(*(pltpu.with_memory_space_constraint(x, pltpu.VMEM) for x in kept))
    return fix[None, None], gal, rhs


def solution(mesh):
    body = local_plane if fits_plane(mesh) else local_any
    return jax.shard_map(
        functools.partial(body, mesh.shape["grp"], mesh.shape["sub"]),
        mesh=mesh,
        in_specs=(
            P("grp", "sub", None, None),
            P("grp", "sub", None, None),
            P("grp", "sub", None, None, None, None),
            P("grp", "sub", None, None),
            P("grp", "sub", None, None),
            P("grp", "sub", None, None),
        ),
        out_specs=(P("grp", "sub", None, None), P(), P(None, "sub")),
        check_vma=False,
    )
```
